32 devices in a mesh: lat: 4 (over z), lon: 4 (over y, x), rad: 2 (over core).
Axes of the slice: x: 2, y: 2, z: 4, core: 2. Of those that a mesh axis runs over, the one named last changes fastest.
Arguments:
- velocity: float32 [3, 32, 32, 1024], P(None, 'rad', 'lat', 'lon'), may hold values from -6 to 6
- forcing: float32 [3, 32, 32, 1024], P(None, 'rad', 'lat', 'lon'), may hold values from -6 to 6
- viscosity: float32 [32, 32, 1024], P('rad', 'lat', 'lon'), may hold values from 0.1 to 10
- plate_ids: int32 [4, 128], P('lat', 'lon'), may hold values from 0 to 11, as said below
Outputs:
- new_velocity: float32 [3, 32, 32, 1024], P(None, 'rad', 'lat', 'lon')
- coarse_residual: float32 [3, 16, 16, 512], P(None, None, 'lat', 'lon')
- plate_velocity: float32 [3, 32, 1024], P(None, 'lat', 'lon')
The draws below stay inside these ranges and needn't reach their ends.
Inputs may be any that keep to these rules, and one draw needn't show every extreme that they name: `plate_ids`: every plate number from 0 to 11 names at least one face block.
All inputs are finite; a program needn't handle non-finite values.
Results may differ from the reference program's by a relative error of at most 0.0003.
Values sent between devices are 32-bit elements; how exact they have to be, the bound alone decides.
A program may use at most 64 MiB of HBM per device.

```python
import math
import jax
import jax.numpy as jnp
from jax import lax

SWEEPS = 3
PLATES = 12
FACE = 8
NR = 32
NA = 32
NO = 1024


def draw_plate_ids(key, part):
    block_rows = NA // FACE
    block_cols = NO // FACE
    plates = jax.random.randint(key, (block_rows * block_cols,), 0, PLATES, dtype=jnp.int32)
    places = jax.random.permutation(jax.random.fold_in(key, 17), block_rows * block_cols)[:PLATES]
    plates = plates.at[places].set(jnp.arange(PLATES, dtype=jnp.int32))
    return plates.reshape(block_rows, block_cols)


def levels(stream_key, extent, shards, least, high):
    factor_of, own = 1.0, jax.random.fold_in(stream_key, 6)
    for dim, shards_of in shards:
        heights = jnp.exp(jax.random.uniform(jax.random.fold_in(own, dim), (shards_of,), jnp.float32, least / len(shards), high / len(shards)))
        factor_of = factor_of * jnp.repeat(heights, extent[dim] // shards_of).reshape([-1 if axis == dim else 1 for axis in range(len(extent))])
    return factor_of


def bell_draw(key, shape, scale, reach, pieces=(), held_as=jnp.bfloat16):
    gain = levels(key, shape, pieces, -0.22, 0.18) if pieces else 1.0
    values = jax.random.normal(key, shape, jnp.float32) * scale * gain
    return jnp.minimum(jnp.maximum(values, -reach), reach).astype(held_as)


def setup_inputs(seed: int = 0) -> dict:
    arg_keys = jax.random.split(jax.random.key(seed), 5)
    velocity = bell_draw(arg_keys[0], (3, NR, NA, NO), 1.0, 6.0, ((1, 2), (2, 4), (3, 4)), jnp.float32)
    forcing = bell_draw(arg_keys[1], (3, NR, NA, NO), 1.0, 6.0, ((1, 2), (2, 4), (3, 4)), jnp.float32)
    viscosity = jnp.clip(jnp.exp(math.log(10.0) - 4.6051702 * jax.random.uniform(arg_keys[2], (NR, NA, NO), jnp.float32) ** levels(arg_keys[2], (NR, NA, NO), ((0, 2), (1, 4), (2, 4)), -0.2, 0.2)), 0.1, 10.0)
    plate_ids = draw_plate_ids(jax.random.fold_in(arg_keys[4], 71), 0)
    return dict(velocity=velocity, forcing=forcing, viscosity=viscosity, plate_ids=plate_ids)


relaxation = 0.8
neighbours = ((0, 1, 1), (2, 1, 1), (1, 0, 1), (1, 2, 1), (1, 1, 0), (1, 1, 2))

def harmonic(own_visc, other_visc):
    total = own_visc + other_visc
    positive = total > 0
    safe_total = jnp.where(positive, total, 1.0)
    return jnp.where(positive, 2.0 * own_visc * other_visc / safe_total, 0.0)

def operate(padded_vel, padded_visc):
    center_vel = padded_vel[:, 1:-1, 1:-1, 1:-1]
    own_visc = padded_visc[1:-1, 1:-1, 1:-1]
    count_rad, count_lat, count_lon = own_visc.shape
    action = 0.5 * own_visc * center_vel
    diagonal = 0.5 * own_visc
    for step_rad, step_lat, step_lon in neighbours:
        other_visc = padded_visc[step_rad:step_rad + count_rad, step_lat:step_lat + count_lat, step_lon:step_lon + count_lon]
        other_vel = padded_vel[:, step_rad:step_rad + count_rad, step_lat:step_lat + count_lat, step_lon:step_lon + count_lon]
        link_weight = harmonic(own_visc, other_visc)
        diagonal = diagonal + link_weight
        action = action + link_weight * (center_vel - other_vel)
    return (action, diagonal, center_vel, own_visc)

def relax_step(padded_vel, forcing_in, padded_visc):
    action, diagonal, center_vel, own_visc = operate(padded_vel, padded_visc)
    inside = own_visc > 0
    safe_diag = jnp.where(inside, diagonal, 1.0)
    updated = center_vel + relaxation * (forcing_in - action) / safe_diag
    return jnp.where(inside, updated, center_vel)

def restrict(residual_field):
    shape_all = residual_field.shape
    blocks = residual_field.reshape(shape_all[0], shape_all[1] // 2, 2, shape_all[2] // 2, 2, shape_all[3] // 2, 2)
    return lax.optimization_barrier(jnp.mean(blocks, axis=(2, 4, 6)))

def surface(velocity, viscosity, lat_cells, lon_cells, lat_total, lon_total):
    latitude = jnp.pi * ((lat_cells + 0.5) / lat_total - 0.5)
    longitude = 2.0 * jnp.pi * (lon_cells + 0.5) / lon_total
    lon_ones = jnp.ones_like(longitude)[None, :]
    cos_lat = jnp.cos(latitude)[:, None] * lon_ones
    radius_x = cos_lat * jnp.cos(longitude)[None, :]
    radius_y = cos_lat * jnp.sin(longitude)[None, :]
    radius_z = jnp.sin(latitude)[:, None] * lon_ones
    traction = viscosity[-1][None] * (velocity[:, -1] - velocity[:, -2])
    torque = jnp.stack([(radius_y * traction[2] - radius_z * traction[1]) * cos_lat, (radius_z * traction[0] - radius_x * traction[2]) * cos_lat, (radius_x * traction[1] - radius_y * traction[0]) * cos_lat, cos_lat])
    return (torque, (radius_x, radius_y, radius_z))

def plate_table(plate_ids):
    cell_plates = jnp.repeat(jnp.repeat(plate_ids, FACE, axis=0), FACE, axis=1)
    numbers = jnp.arange(PLATES, dtype=jnp.int32)[:, None, None]
    onehot = (cell_plates[None] == numbers).astype(jnp.float32)
    return onehot.reshape(PLATES, -1)

def rotate(rotation, onehot, radius):
    per_cell = jnp.dot(rotation, onehot, precision=lax.Precision.HIGHEST).reshape((3,) + radius[0].shape)
    radius_x, radius_y, radius_z = radius
    return jnp.stack([per_cell[1] * radius_z - per_cell[2] * radius_y, per_cell[2] * radius_x - per_cell[0] * radius_z, per_cell[0] * radius_y - per_cell[1] * radius_x])

def pad_cells(block):
    block = jnp.concatenate([block[..., -1:], block, block[..., :1]], axis=-1)
    widths = [(0, 0)] * (block.ndim - 3) + [(1, 1), (1, 1), (0, 0)]
    return jnp.pad(block, widths)

def reference(velocity, forcing, viscosity, plate_ids):
    padded_visc = pad_cells(viscosity)
    current = velocity
    for sweep_index in range(SWEEPS):
        current = relax_step(pad_cells(current), forcing, padded_visc)
    action = operate(pad_cells(current), padded_visc)[0]
    coarse_residual = restrict(forcing - action)
    torque, radius = surface(current, viscosity, jnp.arange(NA, dtype=jnp.float32), jnp.arange(NO, dtype=jnp.float32), NA, NO)
    onehot = plate_table(plate_ids)
    sums = jnp.dot(torque.reshape(4, -1), onehot.T, precision=lax.Precision.HIGHEST)
    rotation = sums[:3] / jnp.sqrt(sums[3])[None]
    return (current, coarse_residual, rotate(rotation, onehot, radius))
```

```python
import functools
import math

import jax
import jax.numpy as jnp
from jax import lax
from jax.experimental import pallas as pl
from jax.experimental.pallas import tpu as pltpu
from jax.sharding import PartitionSpec as P

SWEEPS = 3
PLATES = 12
FACE = 8
RELAX = 0.8
COMPS = 3
LANES = 128
SLOT = 32
MESH = pl.DeviceIdType.MESH
HIGHEST = lax.Precision.HIGHEST
UNROLL = 4
DIRECT = 64
FIELDS = 2 * (COMPS + 1)


def harmonic(own, other):
    return 2.0 * own * other / (own + other)


def harmonic0(own, other):
    return 2.0 * own * other / jnp.maximum(own + other, 1e-30)


class Link:
    def __init__(self, make):
        self.make = make

    def start(self):
        self.make().start()

    def wait_send(self):
        self.make().wait_send()

    def wait_recv(self):
        self.make().wait_recv()


def kernel(
    sizes, vel, forc, visc, ids_in,
    last, coarse, plate,
    early, ids, ids_near, f, eta, w_lat, w_lon, w_rad, gain, diag, part, num,
    row_out, row_in, row_sum, row_w, row_g, row_q, row_p,
    col_out, col_in, col_sum, col_w, col_g, col_d, col_p,
    plane_num, plane_d, plane_g, plane_l, plane_q,
    corner_out, corner_in, corner_t, edge_in, side_in,
    pairs, sums, lat_sums, stage_out, tally, tally_thin,
    load_sem, lon_send, lat_send, rad_send, edge_send, lon_recv, lat_recv, rad_recv, edge_recv,
    ids_send, ids_recv, wave, s1_send, s1_recv, s2_send, s2_recv, g_send, g_recv,
):
    n_lat, n_lon, n_rad = sizes
    n_r, n_a, n_o = visc.shape
    me_lat, me_lon, me_rad = (lax.axis_index(a) for a in ("lat", "lon", "rad"))
    lat_has = (me_lat > 0, me_lat < n_lat - 1)
    rad_has = (me_rad > 0, me_rad < n_rad - 1)
    lat_to = (me_lat - 1, me_lat + 1)
    rad_to = (me_rad - 1, me_rad + 1)
    lon_to = (lax.rem(me_lon + n_lon - 1, n_lon), lax.rem(me_lon + 1, n_lon))
    is_top = me_rad == n_rad - 1
    direct = n_lat * n_lon * n_rad <= DIRECT
    v = [early.at[t] for t in range(SWEEPS)] + [last]
    blocks_r = n_r // UNROLL
    end = blocks_r - 1
    both = (0, 1)

    def guarded(cond, call):
        if cond is None:
            call()
        else:
            pl.when(cond)(call)

    def all_of(*conds):
        conds = [c for c in conds if c is not None]
        return functools.reduce(jnp.logical_and, conds)

    barrier = pltpu.get_barrier_semaphore()

    def greet(device):
        pl.semaphore_signal(barrier, inc=1, device_id=device, device_id_type=MESH)

    expected = n_lon * n_rad - 1
    for step in range(1, n_lon * n_rad):
        greet({
            "lon": lax.rem(me_lon + step // n_rad, n_lon),
            "rad": lax.rem(me_rad + step % n_rad, n_rad),
        })
    for s in both:
        if direct:
            pl.when(lat_has[s])(functools.partial(greet, {"lat": lat_to[s]}))
            expected = expected + jnp.where(lat_has[s], 1, 0)
        for q in both:
            pl.when(lat_has[s])(functools.partial(greet, {"lat": lat_to[s], "lon": lon_to[q]}))
            expected = expected + jnp.where(lat_has[s], 1, 0)
        for p in both:
            has = all_of(lat_has[s], rad_has[p])
            pl.when(has)(functools.partial(greet, {"lat": lat_to[s], "rad": rad_to[p]}))
            expected = expected + jnp.where(has, 1, 0)
    if not direct:
        for step in range(1, n_lat):
            greet({"lat": lax.rem(me_lat + step, n_lat)})
        expected = expected + (n_lat - 1)

    def load_chunk(b):
        here_r = pl.ds(b * UNROLL, UNROLL)
        inner = pl.ds(1 + b * UNROLL, UNROLL)
        return [
            pltpu.make_async_copy(visc.at[here_r], eta.at[inner], load_sem.at[b]),
            pltpu.make_async_copy(vel.at[:, here_r], v[0].at[:, inner], load_sem.at[b]),
            pltpu.make_async_copy(forc.at[:, here_r], f.at[:, here_r], load_sem.at[b]),
        ]

    for b in reversed(range(blocks_r)):
        for load in load_chunk(b):
            load.start()
    load_ids = pltpu.make_async_copy(ids_in, ids, load_sem.at[blocks_r])
    load_ids.start()

    def rows_of(ref):
        return ref.size // n_o

    def await_rows(sem, rows, sending=False):
        some = tally.at[pl.ds(0, rows)]
        copy = pltpu.make_async_remote_copy(
            some, some, sem, sem, device_id={"lon": lon_to[1]}, device_id_type=MESH,
        )
        copy.wait_send() if sending else copy.wait_recv()

    def await_thin(sem, rows, sending=False):
        some = tally_thin.at[pl.ds(0, rows)]
        copy = pltpu.make_async_remote_copy(
            some, some, sem, sem, device_id={"lon": lon_to[1]}, device_id_type=MESH,
        )
        copy.wait_send() if sending else copy.wait_recv()

    def loaded(b):
        some = tally.at[pl.ds(0, (2 * COMPS + 1) * UNROLL * n_a)]
        pltpu.make_async_copy(some, some, load_sem.at[b]).wait()

    lane_wide = lax.broadcasted_iota(jnp.int32, (n_a, n_o), 1)
    lane = lax.broadcasted_iota(jnp.int32, (n_a, LANES), 1)
    row = lax.broadcasted_iota(jnp.int32, (n_a, n_o), 0)
    row_thin = lax.broadcasted_iota(jnp.int32, (n_a, LANES), 0)
    even = lane % 2 == 0
    field_of = (lane + 1) % LANES // 2 % FIELDS
    layer_of = (lane + 1) % LANES // (2 * FIELDS)
    reps = n_o // LANES
    row_edge = (0, n_a - 1)
    lane_edge = (0, n_o - 1)
    thin_edge = (0, LANES - 1)

    plane_rows = n_a
    tile_rows = n_a * LANES // n_o

    def phase(call):
        pl.when(me_lat >= 0)(call)

    for p, slot, face in ((0, 0, 0), (1, n_r + 1, n_r)):
        @pl.when(jnp.logical_not(rad_has[p]))
        def _():
            zero_plane = jnp.zeros((n_a, n_o), jnp.float32)
            w_rad[face] = zero_plane
            for t in range(SWEEPS + 1):
                for c in range(COMPS):
                    v[t][c, slot] = zero_plane
            for h in both:
                for s in both:
                    edge_in[h, s, p] = zero_plane
                    side_in[h, p, s] = jnp.zeros((n_a, LANES), jnp.float32)
    for s in both:
        @pl.when(jnp.logical_not(lat_has[s]))
        def _():
            blank_rows = jnp.where(row == FIELDS - 1, 1.0, 0.0)
            for h in both:
                for r in range(n_r):
                    row_in[h, s, r] = blank_rows
                for b in range(blocks_r):
                    for q in both:
                        corner_in[h, b, s, q] = jnp.zeros((1, LANES), jnp.float32)
                for p in both:
                    edge_in[h, s, p] = jnp.zeros((n_a, n_o), jnp.float32)
            ids_near[s] = jnp.zeros(ids.shape, jnp.int32)

    def messages(h, b):
        t = 2 * h
        table = []

        def add(src, dst, sends, takes, device, cond):
            table.append((Link(functools.partial(
                pltpu.make_async_remote_copy, src, dst, sends, takes,
                device_id=device, device_id_type=MESH,
            )), cond))

        for p, layer, slot in ((0, 1, n_r + 1), (1, n_r, 0)):
            if p not in near_planes(b):
                continue
            sems = (rad_send.at[p], rad_recv.at[h, 1 - p])
            device = {"rad": rad_to[p]}
            add(v[t].at[:, layer], v[t].at[:, slot], *sems, device, rad_has[p])
            add(num.at[h, :, layer - 1], plane_num.at[h, 1 - p], *sems, device, rad_has[p])
            if h == 0:
                add(eta.at[layer], eta.at[slot], *sems, device, rad_has[p])
                add(part.at[layer - 1], plane_d.at[1 - p], *sems, device, rad_has[p])
            for q in both:
                add(
                    col_out.at[h, b], side_in.at[h, 1 - p, 1 - q], *sems,
                    {"lon": lon_to[q], "rad": rad_to[p]}, rad_has[p],
                )
            for s in both:
                add(
                    row_out.at[h, s, layer - 1], edge_in.at[h, 1 - s, 1 - p],
                    edge_send.at[s, p], edge_recv.at[h, 1 - s, 1 - p],
                    {"lat": lat_to[s], "rad": rad_to[p]}, all_of(rad_has[p], lat_has[s]),
                )
        for q in both:
            add(
                col_out.at[h, b], col_in.at[h, b, 1 - q], lon_send.at[0], lon_recv.at[h, b],
                {"lon": lon_to[q]}, None,
            )
        for s in both:
            for q in both:
                add(
                    corner_out.at[h, b, s], corner_in.at[h, b, 1 - s, 1 - q],
                    lat_send.at[s], lat_recv.at[h, b, 1 - s],
                    {"lat": lat_to[s], "lon": lon_to[q]}, lat_has[s],
                )
        layers = pl.ds(b * UNROLL, UNROLL)
        for s in both:
            add(
                row_out.at[h, s, layers], row_in.at[h, 1 - s, layers],
                lat_send.at[s], lat_recv.at[h, b, 1 - s], {"lat": lat_to[s]}, lat_has[s],
            )
        return table

    corner_rows = 2 * LANES // n_o
    lat_rows = UNROLL * FIELDS + corner_rows

    def rad_rows(h):
        return (2 * COMPS + (2 if h == 0 else 0)) * n_a + 2 * tile_rows

    def start(h, b):
        for copy, cond in messages(h, b):
            guarded(cond, copy.start)

    def near_planes(b):
        return [p for p, at in ((0, 0), (1, end)) if b == at]

    def arrive(h, b):
        for p in near_planes(b):
            guarded(rad_has[p], functools.partial(await_rows, rad_recv.at[h, p], rad_rows(h)))
            for s in both:
                guarded(
                    all_of(rad_has[p], lat_has[s]),
                    functools.partial(await_rows, edge_recv.at[h, s, p], FIELDS),
                )
        await_rows(lon_recv.at[h, b], 2 * tile_rows)
        for s in both:
            guarded(lat_has[s], functools.partial(await_rows, lat_recv.at[h, b, s], lat_rows))

    def sent(h):
        for p in both:
            guarded(rad_has[p], functools.partial(await_rows, rad_send.at[p], rad_rows(h), True))
            for s in both:
                guarded(
                    all_of(rad_has[p], lat_has[s]),
                    functools.partial(await_rows, edge_send.at[s, p], FIELDS, True),
                )
        await_rows(lon_send.at[0], blocks_r * 2 * tile_rows, True)
        for s in both:
            guarded(lat_has[s], functools.partial(await_rows, lat_send.at[s], blocks_r * lat_rows, True))

    def turn(x, shift, axis):
        shift = shift % x.shape[axis]
        return pltpu.roll(x, shift, axis) if shift else x

    def interior(t, r, c):
        tile = v[t][c, r + 1]
        return tile, (
            (w_lat[0, r] * turn(tile, 1, 0) + w_lat[1, r] * turn(tile, -1, 0))
            + (w_lon[0, r] * turn(tile, 1, 1) + w_lon[1, r] * turn(tile, -1, 1))
        )

    def radial(t, r, c, seams):
        total = None
        for face, slot in ((r, r), (r + 1, r + 2)):
            if (slot in (0, n_r + 1)) == seams or (seams is None):
                term = w_rad[face] * v[t][c, slot]
                total = term if total is None else total + term
        return total

    def lane_at(g, j):
        return 2 * (j * FIELDS + g)

    def ends_of(x, k):
        x = turn(x, -k, 1)
        west = jnp.where(lane == 0, x, 0.0)
        east = jnp.where(lane == LANES - 1, x, 0.0)
        if reps == 1:
            return west + east
        gap = [jnp.zeros((n_a, LANES), jnp.float32)] * (reps - 2)
        return jnp.concatenate([west] + gap + [east], 1)

    def edge_rows(low, high):
        return jnp.where(row == 0, low, jnp.where(row == n_a - 1, high, 0.0))

    def seams(t, b, j, c):
        r = b * UNROLL + j
        low, high = (row_sum[t, s, r, 1 + c : 2 + c] for s in both)
        return edge_rows(low, high) + ends_of(col_sum[t, b], lane_at(1 + c, j))

    def pack(h, r, k, tile, packed):
        row_out[h, 0, r, k : k + 1, :] = tile[:1]
        row_out[h, 1, r, k : k + 1, :] = tile[n_a - 1 :]
        at = lane_at(k, r % UNROLL)
        two = jnp.where(lane < LANES // 2, tile[:, :LANES], tile[:, n_o - LANES :])
        hit = jnp.logical_and(field_of == k, layer_of == r % UNROLL)
        return jnp.where(hit, turn(two, at, 1), packed)

    def prepare(h, b):
        t = 2 * h
        packed = jnp.zeros((n_a, LANES), jnp.float32)
        for j in range(UNROLL):
            r = b * UNROLL + j
            if h == 0:
                own = eta[r + 1]
                below = jnp.where(row == 0, 0.0, harmonic(own, turn(own, 1, 0)))
                above = jnp.where(row == n_a - 1, 0.0, turn(below, -1, 0))
                west = jnp.where(lane_wide == 0, 0.0, harmonic(own, turn(own, 1, 1)))
                east = jnp.where(lane_wide == n_o - 1, 0.0, turn(west, -1, 1))
                w_lat[0, r] = below
                w_lat[1, r] = above
                w_lon[0, r] = west
                w_lon[1, r] = east
                d = 0.5 * own + (below + above) + (west + east)
                if r > 0:
                    down = harmonic(own, eta[r])
                    w_rad[r] = down
                    d = d + down
                if r < n_r - 1:
                    d = d + harmonic(own, eta[r + 2])
                part[r] = d
                packed = pack(h, r, 0, own, packed)
                packed = pack(h, r, FIELDS - 1, d, packed)
        for j in range(UNROLL):
            r = b * UNROLL + j
            for c in range(COMPS):
                tile, near = interior(t, r, c)
                if h == 0:
                    total = f[c, r] + near
                    if r > 0:
                        total = total + w_rad[r] * v[t][c, r]
                    if r < n_r - 1:
                        up = w_rad[r + 1] if j < UNROLL - 1 else harmonic(eta[r + 1], eta[r + 2])
                        total = total + up * v[t][c, r + 2]
                else:
                    total = f[c, r] + (near + radial(t, r, c, False))
                num[h, c, r] = total
                packed = pack(h, r, 1 + c, tile, packed)
                packed = pack(h, r, 1 + COMPS + c, total, packed)
        col_out[h, b] = packed
        for s in both:
            corner_out[h, b, s] = packed[row_edge[s] : row_edge[s] + 1]

    def repeat_from(x, field, shifts):
        fields = field_of if x.shape[0] == n_a else field_of[:1]
        only = jnp.where(fields == field, x, 0.0)
        return functools.reduce(jnp.add, [turn(only, 2 * k, 1) for k in shifts])

    def repeat_first(x):
        return repeat_from(x, 0, range(COMPS + 1))

    def repeat_last(x):
        return repeat_from(x, FIELDS - 1, [1 + c - (FIELDS - 1) for c in range(COMPS)])

    def joined(from_west, from_east):
        at = even if from_west.shape[0] == n_a else even[:1]
        return jnp.where(at, turn(from_west, 1, 1), turn(from_east, -1, 1))

    def update_rows(h, b):
        t = 2 * h
        stacked = jnp.zeros((8, LANES), jnp.float32)
        spot = lax.broadcasted_iota(jnp.int32, (8, LANES), 0)
        for s in both:
            stacked = jnp.where(spot == 2 * s, turn(corner_in[h, b, s, 0], 1, 1), stacked)
            stacked = jnp.where(spot == 2 * s + 1, corner_in[h, b, s, 1], stacked)
        corner_t[h, b] = stacked.T
        for s in both:
            for j in range(UNROLL):
                r = b * UNROLL + j
                own, far = row_out[h, s, r], row_in[h, s, r]
                column = corner_t[h, b, pl.ds(lane_at(0, j), FIELDS, stride=2), :]
                west = jnp.where(lane == 0, column[:, 2 * s : 2 * s + 1], 0.0)
                east = jnp.where(lane == LANES - 1, column[:, 2 * s + 1 : 2 * s + 2], 0.0)
                if reps == 1:
                    corner = west + east
                else:
                    gap = [jnp.zeros((n_a, LANES), jnp.float32)] * (reps - 2)
                    corner = jnp.concatenate([west] + gap + [east], 1)
                near = [p for p, layer in ((0, 0), (1, n_r - 1)) if r == layer]
                if h == 0:
                    far_eta = far[:1]
                    w = harmonic(far_eta, own[:1])
                    wq = harmonic0(far_eta, corner[:1])
                    d = far[FIELDS - 1 :] + (w + wq)
                    for p in near:
                        wp = harmonic0(far_eta, edge_in[h, s, p, :1])
                        row_p[s, p] = wp
                        d = d + wp
                    row_w[s, r] = w
                    row_q[s, r] = wq
                    row_g[s, r] = RELAX / d
                w = row_w[s, r]
                total = turn(far, -COMPS, 0) + w * own + row_q[s, r] * corner
                for p in near:
                    total = total + row_p[s, p] * edge_in[h, s, p]
                row_sum[t, s, r] = w * far
                row_sum[t + 1, s, r] = w * ((1.0 - RELAX) * far + row_g[s, r] * total)

    def side_of(h, p):
        return joined(side_in[h, p, 0], side_in[h, p, 1])

    def update_cols(h, b):
        t = 2 * h
        far = joined(col_in[h, b, 0], col_in[h, b, 1])
        own = col_out[h, b]
        corners = [joined(corner_in[h, b, s, 0], corner_in[h, b, s, 1]) for s in both]
        move = 2 * FIELDS * (UNROLL - 1)
        sides = {p: turn(side_of(h, p), -move if p == 0 else move, 1) for p in near_planes(b)}
        if h == 0:
            far_eta = repeat_first(far)
            w = harmonic0(far_eta, repeat_first(own))
            d = repeat_last(far) + w
            for s in both:
                wd = jnp.where(
                    row_thin == row_edge[s], harmonic0(far_eta, repeat_first(corners[s])), 0.0,
                )
                col_d[b, s] = wd
                d = d + wd
            for p in near_planes(b):
                wp = jnp.where(
                    layer_of == (0, UNROLL - 1)[p], harmonic0(far_eta, repeat_first(sides[p])), 0.0,
                )
                col_p[p] = wp
                d = d + wp
            col_w[b] = w
            col_g[b] = RELAX / jnp.where(d > 0.0, d, 1.0)
        w = col_w[b]
        total = turn(far, -2 * COMPS, 1) + w * own
        for s in both:
            total = total + col_d[b, s] * corners[s]
        for p in near_planes(b):
            total = total + col_p[p] * sides[p]
        col_sum[t, b] = w * far
        col_sum[t + 1, b] = w * ((1.0 - RELAX) * far + col_g[b] * total)

    def update_plane(h, p):
        t = 2 * h
        slot, layer, face, j = ((0, 1, 0, UNROLL - 1), (n_r + 1, n_r, n_r, 0))[p]
        side = side_of(h, p)
        if h == 0:
            own = eta[slot]
            w = harmonic(own, eta[layer])
            w_rad[face] = w
            wq = harmonic0(own, ends_of(side, lane_at(0, j)))
            plane_q[p] = wq
            d = plane_d[p] + (w + wq)
            wl = edge_rows(*(harmonic0(own, edge_in[h, s, p, :1]) for s in both))
            plane_l[p] = wl
            plane_g[p] = RELAX / (d + wl)
        for c in range(COMPS):
            total = plane_num[h, p, c] + w_rad[face] * v[t][c, layer]
            total = total + plane_l[p] * edge_rows(*(edge_in[h, s, p, 1 + c : 2 + c] for s in both))
            total = total + plane_q[p] * ends_of(side, lane_at(1 + c, j))
            v[t + 1][c, slot] = (1.0 - RELAX) * v[t][c, slot] + plane_g[p] * total

    def receive(h, b):
        arrive(h, b)
        update_cols(h, b)
        update_rows(h, b)
        for p in near_planes(b):
            pl.when(rad_has[p])(functools.partial(update_plane, h, p))

    def settle(b):
        for j in range(UNROLL):
            r = b * UNROLL + j
            low, high = (row_w[s, r] for s in both)
            d = part[r] + (edge_rows(low, high) + ends_of(col_w[b], lane_at(0, j)))
            if r == 0:
                d = d + w_rad[0]
            if r == n_r - 1:
                d = d + w_rad[n_r]
            diag[r] = d
            gain[r] = RELAX / d

    def advance_face(h, b):
        t = 2 * h
        if h == 0:
            settle(b)
        for c in range(COMPS):
            for j in range(UNROLL):
                r = b * UNROLL + j
                total = num[h, c, r] + seams(t, b, j, c)
                if r in (0, n_r - 1):
                    total = total + radial(t, r, c, True)
                v[t + 1][c, r + 1] = (1.0 - RELAX) * v[t][c, r + 1] + gain[r] * total

    def first_step(h, b):
        receive(h, b)
        phase(functools.partial(advance_face, h, b))

    def whole_flux(t, b, c, j):
        r = b * UNROLL + j
        tile, near = interior(t, r, c)
        total = (f[c, r] + near) + (radial(t, r, c, None) + seams(t, b, j, c))
        return r, tile, total

    def second_step(t, b):
        for c in range(COMPS):
            for j in range(UNROLL):
                r, tile, total = whole_flux(t, b, c, j)
                v[t + 1][c, r + 1] = (1.0 - RELAX) * tile + gain[r] * total

    def residual(b):
        t = SWEEPS
        for c in range(COMPS):
            for i in range(UNROLL // 2):
                two = jnp.zeros((n_a, n_o), jnp.float32)
                for j in (2 * i, 2 * i + 1):
                    r, tile, total = whole_flux(t, b, c, j)
                    two = two + (total - diag[r] * tile)
                at = pl.ds((c * (n_r // 2) + b * (UNROLL // 2) + i) * n_a, n_a)
                for k in range(reps):
                    pairs[k, at] = two[:, k * LANES : (k + 1) * LANES]

    loaded(end)
    for b in reversed(range(blocks_r)):
        if b > 0:
            loaded(b - 1)
        phase(functools.partial(prepare, 0, b))
        if b == end:
            pl.semaphore_wait(barrier, expected)
        start(0, b)
    load_ids.wait()

    near_devices = [({"lat": lat_to[s]}, lat_has[s], lat_has[1 - s]) for s in both] + [
        ({"lon": lon_to[q]}, None, None) for q in both
    ]

    def ids_copy(i):
        return Link(functools.partial(
            pltpu.make_async_remote_copy, ids, ids_near.at[i ^ 1], ids_send.at[i], ids_recv.at[i],
            device_id=near_devices[i][0], device_id_type=MESH,
        ))

    for i, (_, send, _) in enumerate(near_devices):
        guarded(send, ids_copy(i).start)

    def wave_signal(k):
        for s in both:
            def tell():
                pl.semaphore_signal(wave.at[k, s], inc=1, device_id={"lat": lat_to[s]}, device_id_type=MESH)
            pl.when(lat_has[s])(tell)

    def wave_wait(k):
        for s in both:
            def hear():
                pl.semaphore_wait(wave.at[k, s], 1)
            pl.when(lat_has[1 - s])(hear)

    waves = n_lat - 1 if direct else 0
    if waves:
        wave_signal(0)

    lat_cell = (me_lat * n_a + row).astype(jnp.float32)
    lon_cell = (me_lon * n_o + lane_wide).astype(jnp.float32)
    phi = math.pi * ((lat_cell + 0.5) / (n_lat * n_a) - 0.5)
    lam = (2.0 * math.pi) * (lon_cell[:1] + 0.5) / (n_lon * n_o)
    cos_lat = jnp.cos(phi)
    cos_lon, sin_lon = jnp.cos(lam), jnp.sin(lam)
    rx = cos_lat * cos_lon
    ry = cos_lat * sin_lon
    rz = jnp.sin(phi)
    blocks = ids.shape[1]
    bands = n_a // FACE
    spread_rows = lax.broadcasted_iota(jnp.int32, (blocks, n_o), 0)
    spread_cols = lax.broadcasted_iota(jnp.int32, (blocks, n_o), 1)
    spread = (spread_cols // FACE == spread_rows).astype(jnp.float32)
    numbers = lax.broadcasted_iota(jnp.int32, (SLOT, n_o), 0)

    def cells_of(line, chosen):
        own = jnp.broadcast_to(line.astype(jnp.float32), (8, blocks))
        return jnp.dot(own, chosen, precision=HIGHEST)[:1]

    def hot(line):
        return hot_of(cells_of(line, spread))

    def hot_of(cells):
        return (jnp.abs(cells - numbers.astype(jnp.float32)) < 0.5).astype(jnp.float32)

    onehots = [hot(ids[band : band + 1]) for band in range(bands)]

    for k in range(1, waves):
        wave_wait(k - 1)
        wave_signal(k)

    def s1_copy(step):
        return pltpu.make_async_remote_copy(
            stage_out.at[0], lat_sums.at[me_lat], s1_send.at[0], s1_recv.at[0],
            device_id={"lat": lax.rem(me_lat + step, n_lat)}, device_id_type=MESH,
        )

    here = me_lat * n_lon + me_lon if direct else me_lon
    group = n_lat * n_lon * n_rad if direct else n_lon * n_rad
    plane = n_lon * n_rad

    def s2_copy(step):
        device = {
            "lon": lax.rem(me_lon + (step % plane) // n_rad, n_lon),
            "rad": lax.rem(me_rad + step % n_rad, n_rad),
        }
        if direct:
            device["lat"] = lax.rem(me_lat + step // plane, n_lat)
        return pltpu.make_async_remote_copy(
            stage_out.at[1], sums.at[here], s2_send.at[0], s2_recv.at[0],
            device_id=device, device_id_type=MESH,
        )

    def cross(k, x, drag):
        return [
            (x[1] * drag[2] - x[2] * drag[1]) * k,
            (x[2] * drag[0] - x[0] * drag[2]) * k,
            (x[0] * drag[1] - x[1] * drag[0]) * k,
        ]

    def torques():
        top = n_r - 1
        guess = [
            [(1.0 - RELAX) * v[2][c, r + 1] + gain[r] * num[1, c, r] for c in range(COMPS)]
            for r in (top, top - 1)
        ]
        drag = [eta[n_r] * (guess[0][c] - guess[1][c]) for c in range(COMPS)]
        twist = cross(cos_lat, (rx, ry, rz), drag) + [cos_lat]
        outer = []
        for s in both:
            k = (me_lat * n_a + (n_a if s else -1)).astype(jnp.float32)
            tilt = math.pi * ((jnp.full((1, n_o), 0.5, jnp.float32) + k) / (n_lat * n_a) - 0.5)
            cos_tilt = jnp.cos(tilt)
            moved = [row_g[s, r] * row_w[s, r] * row_out[1, s, r] for r in (top, top - 1)]
            shift = row_in[0, s, top, :1] * (moved[0] - moved[1])
            push = [shift[1 + c : 2 + c] for c in range(COMPS)]
            outer.append(cross(cos_tilt, (cos_tilt * cos_lon, cos_tilt * sin_lon, jnp.sin(tilt)), push))
        moved = col_g[end] * col_w[end] * col_out[1, end]
        shift = repeat_first(joined(col_in[0, end, 0], col_in[0, end, 1])) * (moved - turn(moved, 2 * FIELDS, 1))
        push = [ends_of(shift, lane_at(1 + c, UNROLL - 1)) for c in range(COMPS)]
        around = n_lon * n_o
        column = jnp.where(
            lane_wide[:1] == 0,
            lax.rem(me_lon * n_o + (around - 1), around), lax.rem(me_lon * n_o + n_o, around),
        ).astype(jnp.float32)
        angle = (2.0 * math.pi) * (column + 0.5) / around
        beside = cross(cos_lat, (cos_lat * jnp.cos(angle), cos_lat * jnp.sin(angle), rz), push)
        firsts = [(spread_rows == block).astype(jnp.float32) for block in (blocks - 1, 0)]
        packed = jnp.zeros((1, LANES), jnp.float32)
        for band in range(bands):
            cut = slice(band * FACE, (band + 1) * FACE)

            def stack(parts):
                return jnp.concatenate(
                    parts + [jnp.zeros((8 - len(parts), n_o), jnp.float32)], 0,
                )

            lines = [stack([jnp.sum(x[cut], axis=0, keepdims=True) for x in twist])]
            hots = [onehots[band]]
            lines.append(stack([jnp.sum(x[cut], axis=0, keepdims=True) for x in beside]))
            hots.append(hot_of(jnp.where(
                lane_wide[:1] == 0,
                cells_of(ids_near[2, band : band + 1], firsts[0]),
                cells_of(ids_near[3, band : band + 1], firsts[1]),
            )))
            for s in both:
                if band == (0, bands - 1)[s]:
                    lines.append(stack(outer[s]))
                    other = (bands - 1, 0)[s]
                    hots.append(hot(ids_near[s, other : other + 1]))
            totals = lax.dot_general(
                jnp.concatenate(lines, 1), jnp.concatenate(hots, 1), (((1,), (1,)), ((), ())),
                precision=HIGHEST, preferred_element_type=jnp.float32,
            )
            packed = packed + jnp.concatenate([totals[i : i + 1] for i in range(COMPS + 1)], 1)
        if direct:
            stage_out[1] = packed
            sums[here] = packed
            for step in range(1, group):
                s2_copy(step).start()
        else:
            stage_out[0] = packed
            lat_sums[me_lat] = packed
            for step in range(1, n_lat):
                s1_copy(step).start()

    def surface():
        if waves:
            wave_wait(waves - 1)
        for i, (_, _, take) in enumerate(near_devices):
            guarded(take, ids_copy(i).wait_recv)
        pl.when(is_top)(torques)

    def advance(b):
        phase(functools.partial(prepare, 1, b))
        if b == end:
            surface()
        start(1, b)

    def ready(b, done):
        return all(k in done for k in (b - 1, b, b + 1) if 0 <= k <= end)

    def sweep(h, order, finish, ship):
        stepped, done, shipped = set(), set(), set()
        for b in order:
            first_step(h, b)
            stepped.add(b)
            for k in order:
                if k not in done and ready(k, stepped):
                    phase(functools.partial(finish, k))
                    done.add(k)
                    for m in [end, 0] + order:
                        if ship and m not in shipped and ready(m, done):
                            ship(m)
                            shipped.add(m)

    first_order = list(reversed(range(blocks_r)))
    second_order = list(reversed(range(1, end))) + ([end, 0] if end else [0])

    def ship_off(b):
        if b == end:
            sent(0)
        advance(b)

    sweep(0, first_order, functools.partial(second_step, 1), ship_off)

    if not direct:
        @pl.when(is_top)
        def _():
            await_thin(s1_recv.at[0], n_lat - 1)
            total = lat_sums[0]
            for i in range(1, n_lat):
                total = total + lat_sums[i]
            stage_out[1] = total
            sums[here] = total
            for step in range(1, group):
                s2_copy(step).start()

    sweep(1, second_order, residual, None)

    half = n_o // 2
    thin_r = lax.broadcasted_iota(jnp.int32, (LANES, half), 0)
    thin_c = lax.broadcasted_iota(jnp.int32, (LANES, half), 1)
    count = COMPS * (n_r // 2) * n_a // 2
    merged = jnp.zeros((count, half), jnp.float32)
    for h in range(reps):
        choose = jnp.where((thin_r + h * LANES) // 2 == thin_c, 0.125, 0.0).astype(jnp.bfloat16)
        summed = pairs[h, pl.ds(0, count, stride=2)] + pairs[h, pl.ds(1, count, stride=2)]
        big = summed.astype(jnp.bfloat16)
        small = (summed - big.astype(jnp.float32)).astype(jnp.bfloat16)
        merged = merged + (
            jnp.dot(big, choose, preferred_element_type=jnp.float32)
            + jnp.dot(small, choose, preferred_element_type=jnp.float32)
        )
    mine = count // COMPS
    spot = pl.ds(pl.multiple_of(me_rad * mine, mine), mine)
    for c in range(COMPS):
        coarse[c, spot] = merged[c * mine : (c + 1) * mine]

    def g_copy(step):
        return pltpu.make_async_remote_copy(
            coarse.at[:, spot], coarse.at[:, spot], g_send.at[step - 1], g_recv.at[me_rad],
            device_id={"rad": lax.rem(me_rad + step, n_rad)}, device_id_type=MESH,
        )

    for step in range(1, n_rad):
        g_copy(step).start()

    sources = n_lat * n_lon if direct else n_lon
    pl.when(is_top)(functools.partial(await_thin, s2_recv.at[0], sources - 1))
    pl.when(jnp.logical_not(is_top))(functools.partial(await_thin, s2_recv.at[0], sources))
    terms = [sums[i] for i in range(sources)]
    while len(terms) > 1:
        terms = [terms[i] + terms[i + 1] if i + 1 < len(terms) else terms[i] for i in range(0, len(terms), 2)]
    total = terms[0]
    area = total[:, COMPS * SLOT : (COMPS + 1) * SLOT]
    valid = lax.broadcasted_iota(jnp.int32, (1, SLOT), 1) < PLATES
    root = jnp.sqrt(jnp.where(valid, area, 1.0))
    turns = jnp.concatenate(
        [total[:, i * SLOT : (i + 1) * SLOT] / root for i in range(COMPS)]
        + [jnp.zeros((8 - COMPS, SLOT), jnp.float32)], 0,
    )
    for band in range(bands):
        cut = slice(band * FACE, (band + 1) * FACE)
        cell = jnp.dot(turns, onehots[band], precision=HIGHEST, preferred_element_type=jnp.float32)
        ox, oy, oz = (cell[i : i + 1] for i in range(COMPS))
        plate[0, cut] = oy * rz[cut] - oz * ry[cut]
        plate[1, cut] = oz * rx[cut] - ox * rz[cut]
        plate[2, cut] = ox * ry[cut] - oy * rx[cut]

    sent(1)
    for i, (_, send, _) in enumerate(near_devices):
        guarded(send, ids_copy(i).wait_send)

    @pl.when(is_top)
    def _():
        if not direct:
            await_thin(s1_send.at[0], n_lat - 1, True)
        await_thin(s2_send.at[0], group - 1, True)

    for step in range(1, n_rad):
        source = lax.rem(me_rad + step, n_rad)
        region = coarse.at[:, pl.ds(pl.multiple_of(source * mine, mine), mine)]
        pltpu.make_async_remote_copy(
            region, region, g_send.at[0], g_recv.at[source],
            device_id={"rad": source}, device_id_type=MESH,
        ).wait_recv()
        g_copy(step).wait_send()


def write_out(last, coarse, plate, new_v_out, coarse_out, plate_out, sem):
    n_r = new_v_out.shape[1]
    copies = [
        pltpu.make_async_copy(last.at[:, pl.ds(1, n_r)], new_v_out, sem.at[0]),
        pltpu.make_async_copy(coarse, coarse_out, sem.at[1]),
        pltpu.make_async_copy(plate, plate_out, sem.at[2]),
    ]
    for copy in copies:
        copy.start()
    for copy in copies:
        copy.wait()


def on_device(sizes, velocity, forcing, viscosity, plate_ids):
    n_lat, n_lon, n_rad = sizes
    _, n_r, n_a, n_o = velocity.shape
    chunks = n_r // UNROLL
    f32 = jnp.float32
    dma = pltpu.SemaphoreType.DMA
    direct = n_lat * n_lon * n_rad <= DIRECT
    group = n_lat * n_lon * n_rad if direct else n_lon * n_rad
    sources = n_lat * n_lon if direct else n_lon
    in_any = pl.BlockSpec(memory_space=pl.ANY)
    in_vmem = pl.BlockSpec(memory_space=pltpu.VMEM)
    coarse_rows = n_rad * (n_r // 2) * (n_a // 2)
    whole = (n_r, n_a, n_o)
    thin = (n_a, LANES)

    def vmem(*shape):
        return pltpu.VMEM(shape, f32)

    held = pl.pallas_call(
        functools.partial(kernel, sizes),
        out_shape=(
            pltpu.VMEM((COMPS, n_r + 2, n_a, n_o), f32),
            pltpu.VMEM((COMPS, coarse_rows, n_o // 2), f32),
            pltpu.VMEM((COMPS, n_a, n_o), f32),
        ),
        in_specs=[pl.BlockSpec(memory_space=pltpu.HBM)] * 4,
        out_specs=(in_vmem,) * 3,
        scratch_shapes=[
            vmem(SWEEPS, COMPS, n_r + 2, n_a, n_o),
            pltpu.VMEM(plate_ids.shape, jnp.int32),
            pltpu.VMEM((4,) + plate_ids.shape, jnp.int32),
            vmem(COMPS, *whole),
            vmem(n_r + 2, n_a, n_o),
            vmem(2, *whole),
            vmem(2, *whole),
            vmem(n_r + 1, n_a, n_o),
            vmem(*whole),
            vmem(*whole),
            vmem(*whole),
            vmem(2, COMPS, *whole),
            vmem(2, 2, *whole),
            vmem(2, 2, *whole),
            vmem(4, 2, *whole),
            vmem(2, n_r, 1, n_o),
            vmem(2, n_r, 1, n_o),
            vmem(2, n_r, 1, n_o),
            vmem(2, 2, 1, n_o),
            vmem(2, chunks, *thin),
            vmem(2, chunks, 2, *thin),
            vmem(4, chunks, *thin),
            vmem(chunks, *thin),
            vmem(chunks, *thin),
            vmem(chunks, 2, *thin),
            vmem(2, *thin),
            vmem(2, 2, COMPS, n_a, n_o),
            vmem(2, n_a, n_o),
            vmem(2, n_a, n_o),
            vmem(2, n_a, n_o),
            vmem(2, n_a, n_o),
            vmem(2, chunks, 2, 1, LANES),
            vmem(2, chunks, 2, 2, 1, LANES),
            vmem(2, chunks, LANES, 8),
            vmem(2, 2, 2, n_a, n_o),
            vmem(2, 2, 2, *thin),
            vmem(n_o // LANES, COMPS * (n_r // 2) * n_a, LANES),
            vmem(sources, 1, LANES),
            vmem(n_lat, 1, LANES),
            vmem(2, 1, LANES),
            vmem(max(7 * UNROLL * n_a, chunks * (UNROLL * FIELDS + 8)), 1, n_o),
            vmem(max(group, sources, n_lat), 1, LANES),
            dma((chunks + 1,)),
            dma((1,)),
            dma((2,)),
            dma((2,)),
            dma((2, 2)),
            dma((2, chunks)),
            dma((2, chunks, 2)),
            dma((2, 2)),
            dma((2, 2, 2)),
            dma((4,)),
            dma((4,)),
            pltpu.SemaphoreType.REGULAR((n_lat - 1 if direct else 1, 2)),
            dma((1,)),
            dma((1,)),
            dma((1,)),
            dma((1,)),
            dma((n_rad,)),
            dma((n_rad,)),
        ],
        compiler_params=pltpu.CompilerParams(
            collective_id=0, has_side_effects=True, vmem_limit_bytes=32 * 2**20
        ),
    )(*(
        pltpu.with_memory_space_constraint(x, pltpu.HBM)
        for x in (velocity, forcing, viscosity, plate_ids)
    ))
    new_v, coarse, plate = pl.pallas_call(
        write_out,
        out_shape=(
            jax.ShapeDtypeStruct(velocity.shape, f32),
            jax.ShapeDtypeStruct((COMPS, coarse_rows, n_o // 2), f32),
            jax.ShapeDtypeStruct((COMPS, n_a, n_o), f32),
        ),
        in_specs=[in_vmem] * 3,
        out_specs=(in_any,) * 3,
        scratch_shapes=[dma((3,))],
        compiler_params=pltpu.CompilerParams(vmem_limit_bytes=4 * 2**20),
    )(*(pltpu.with_memory_space_constraint(x, pltpu.VMEM) for x in held))
    coarse = coarse.reshape(COMPS, n_rad * (n_r // 2), n_a // 2, n_o // 2)
    return new_v, coarse, plate


def solution(mesh):
    sizes = tuple(mesh.shape[a] for a in ("lat", "lon", "rad"))
    field = P(None, "rad", "lat", "lon")
    return jax.shard_map(
        functools.partial(on_device, sizes),
        mesh=mesh,
        in_specs=(field, field, P("rad", "lat", "lon"), P("lat", "lon")),
        out_specs=(field, P(None, None, "lat", "lon"), P(None, "lat", "lon")),
        check_vma=False,
    )
```

```python
import functools
import math

import jax
import jax.numpy as jnp
from jax import lax
from jax.experimental import pallas as pl
from jax.experimental.pallas import tpu as pltpu
from jax.sharding import PartitionSpec as P

SWEEPS = 3
PLATES = 12
FACE = 8
RELAX = 0.8
COMPS = 3
LANES = 128
SLOT = 32
MESH = pl.DeviceIdType.MESH
HIGHEST = lax.Precision.HIGHEST
UNROLL = 8
DIRECT = 64
FIELDS = 2 * (COMPS + 1)


def harmonic(own, other):
    return 2.0 * own * other / (own + other)


def harmonic0(own, other):
    return 2.0 * own * other / jnp.maximum(own + other, 1e-30)


class Link:
    def __init__(self, make):
        self.make = make

    def start(self):
        self.make().start()

    def wait_send(self):
        self.make().wait_send()

    def wait_recv(self):
        self.make().wait_recv()


def kernel(
    sizes, vel, forc, visc, ids_in,
    last, coarse, plate,
    early, ids, ids_near, f, eta, w_lat, w_lon, w_rad, gain, diag, part, num,
    row_out, row_in, row_sum, row_w, row_g, row_q, row_p,
    col_first, col_out, col_in, col_far, col_sum, col_w, col_g, col_d, col_p,
    plane_num, plane_d, plane_g, plane_l, plane_q,
    corner_out, corner_in, corner_t, edge_out, edge_in, side_in,
    pairs, sums, lat_sums, stage_out, tally, tally_thin,
    load_sem, lon_send, lat_send, rad_send, num_send, edge_send, lon_recv, lat_recv, rad_recv, num_recv, edge_recv, far_send, far_recv,
    ids_send, ids_recv, wave, s1_send, s1_recv, s2_send, s2_recv, g_send, g_recv,
):
    n_lat, n_lon, n_rad = sizes
    n_r, n_a, n_o = visc.shape
    me_lat, me_lon, me_rad = (lax.axis_index(a) for a in ("lat", "lon", "rad"))
    lat_has = (me_lat > 0, me_lat < n_lat - 1)
    rad_has = (me_rad > 0, me_rad < n_rad - 1)
    lat_to = (me_lat - 1, me_lat + 1)
    rad_to = (me_rad - 1, me_rad + 1)
    lon_to = (lax.rem(me_lon + n_lon - 1, n_lon), lax.rem(me_lon + 1, n_lon))
    is_top = me_rad == n_rad - 1
    direct = n_lat * n_lon * n_rad <= DIRECT
    v = [early.at[t] for t in range(SWEEPS)] + [last]
    blocks_r = n_r // UNROLL
    end = blocks_r - 1
    both = (0, 1)

    def guarded(cond, call):
        if cond is None:
            call()
        else:
            pl.when(cond)(call)

    def all_of(*conds):
        conds = [c for c in conds if c is not None]
        return functools.reduce(jnp.logical_and, conds)

    barrier = pltpu.get_barrier_semaphore()

    def greet(device):
        pl.semaphore_signal(barrier, inc=1, device_id=device, device_id_type=MESH)

    expected = n_lon * n_rad - 1
    for step in range(1, n_lon * n_rad):
        greet({
            "lon": lax.rem(me_lon + step // n_rad, n_lon),
            "rad": lax.rem(me_rad + step % n_rad, n_rad),
        })
    for s in both:
        if direct:
            pl.when(lat_has[s])(functools.partial(greet, {"lat": lat_to[s]}))
            expected = expected + jnp.where(lat_has[s], 1, 0)
        for q in both:
            pl.when(lat_has[s])(functools.partial(greet, {"lat": lat_to[s], "lon": lon_to[q]}))
            expected = expected + jnp.where(lat_has[s], 1, 0)
        for p in both:
            has = all_of(lat_has[s], rad_has[p])
            pl.when(has)(functools.partial(greet, {"lat": lat_to[s], "rad": rad_to[p]}))
            expected = expected + jnp.where(has, 1, 0)
    if not direct:
        for step in range(1, n_lat):
            greet({"lat": lax.rem(me_lat + step, n_lat)})
        expected = expected + (n_lat - 1)

    def load_chunk(b):
        here_r = pl.ds(b * UNROLL, UNROLL)
        inner = pl.ds(1 + b * UNROLL, UNROLL)
        return [
            pltpu.make_async_copy(visc.at[here_r], eta.at[inner], load_sem.at[b]),
            pltpu.make_async_copy(vel.at[:, here_r], v[0].at[:, inner], load_sem.at[b]),
            pltpu.make_async_copy(forc.at[:, here_r], f.at[:, here_r], load_sem.at[b]),
        ]

    for b in reversed(range(blocks_r)):
        for load in load_chunk(b):
            load.start()
    load_ids = pltpu.make_async_copy(ids_in, ids, load_sem.at[blocks_r])
    load_ids.start()

    def rows_of(ref):
        return ref.size // n_o

    def await_rows(sem, rows, sending=False):
        some = tally.at[pl.ds(0, rows)]
        copy = pltpu.make_async_remote_copy(
            some, some, sem, sem, device_id={"lon": lon_to[1]}, device_id_type=MESH,
        )
        copy.wait_send() if sending else copy.wait_recv()

    def await_thin(sem, rows, sending=False):
        some = tally_thin.at[pl.ds(0, rows)]
        copy = pltpu.make_async_remote_copy(
            some, some, sem, sem, device_id={"lon": lon_to[1]}, device_id_type=MESH,
        )
        copy.wait_send() if sending else copy.wait_recv()

    def loaded(b):
        some = tally.at[pl.ds(0, (2 * COMPS + 1) * UNROLL * n_a)]
        pltpu.make_async_copy(some, some, load_sem.at[b]).wait()

    lane_wide = lax.broadcasted_iota(jnp.int32, (n_a, n_o), 1)
    lane = lax.broadcasted_iota(jnp.int32, (n_a, LANES), 1)
    row = lax.broadcasted_iota(jnp.int32, (n_a, n_o), 0)
    row_thin = lax.broadcasted_iota(jnp.int32, (n_a, LANES), 0)
    even = lane % 2 == 0
    field_of = (lane + 1) % LANES // 2 % FIELDS
    layer_of = (lane + 1) % LANES // (2 * FIELDS)
    reps = n_o // LANES
    row_edge = (0, n_a - 1)
    lane_edge = (0, n_o - 1)
    thin_edge = (0, LANES - 1)

    plane_rows = n_a
    tile_rows = n_a * LANES // n_o

    def phase(call):
        pl.when(me_lat >= 0)(call)

    for p, slot, face in ((0, 0, 0), (1, n_r + 1, n_r)):
        @pl.when(jnp.logical_not(rad_has[p]))
        def _():
            zero_plane = jnp.zeros((n_a, n_o), jnp.float32)
            w_rad[face] = zero_plane
            for t in range(SWEEPS + 1):
                for c in range(COMPS):
                    v[t][c, slot] = zero_plane
            for h in both:
                for s in both:
                    edge_in[h, s, p] = zero_plane
                    side_in[h, p, s] = jnp.zeros((n_a, LANES), jnp.float32)
    for s in both:
        @pl.when(jnp.logical_not(lat_has[s]))
        def _():
            blank_rows = jnp.where(row == FIELDS - 1, 1.0, 0.0)
            for h in both:
                for r in range(n_r):
                    row_in[h, s, r] = blank_rows
                for b in range(blocks_r):
                    for q in both:
                        corner_in[h, b, s, q] = jnp.zeros((1, LANES), jnp.float32)
                for p in both:
                    edge_in[h, s, p] = jnp.zeros((n_a, n_o), jnp.float32)
            ids_near[s] = jnp.zeros(ids.shape, jnp.int32)

    def messages(h, b, early_part):
        t = 2 * h
        table = []

        def add(src, dst, sends, takes, device, cond):
            table.append((Link(functools.partial(
                pltpu.make_async_remote_copy, src, dst, sends, takes,
                device_id=device, device_id_type=MESH,
            )), cond))

        for p, layer, slot in ((0, 1, n_r + 1), (1, n_r, 0)):
            if p not in near_planes(b):
                continue
            device = {"rad": rad_to[p]}
            if early_part:
                sems = (rad_send.at[p], rad_recv.at[h, 1 - p])
                add(v[t].at[:, layer], v[t].at[:, slot], *sems, device, rad_has[p])
                if h == 0:
                    add(eta.at[layer], eta.at[slot], *sems, device, rad_has[p])
            sems = (num_send.at[p], num_recv.at[h, 1 - p])
            if early_part:
                for q in both:
                    add(
                        col_first.at[h, b], side_in.at[h, 1 - p, 1 - q], *sems,
                        {"lon": lon_to[q], "rad": rad_to[p]}, rad_has[p],
                    )
                for s in both:
                    add(
                        edge_out.at[h, s, p], edge_in.at[h, 1 - s, 1 - p],
                        edge_send.at[s, p], edge_recv.at[h, 1 - s, 1 - p],
                        {"lat": lat_to[s], "rad": rad_to[p]}, all_of(rad_has[p], lat_has[s]),
                    )
            else:
                add(num.at[h, :, layer - 1], plane_num.at[h, 1 - p], *sems, device, rad_has[p])
                if h == 0:
                    add(part.at[layer - 1], plane_d.at[1 - p], *sems, device, rad_has[p])
        if early_part:
            for s in both:
                for q in both:
                    add(
                        corner_out.at[h, b, s], corner_in.at[h, b, 1 - s, 1 - q],
                        far_send.at[s], far_recv.at[h, 1 - s],
                        {"lat": lat_to[s], "lon": lon_to[q]}, lat_has[s],
                    )
            return table
        for q in both:
            add(
                col_out.at[h, b], col_in.at[h, b, 1 - q], lon_send.at[0], lon_recv.at[h, b],
                {"lon": lon_to[q]}, None,
            )
        layers = pl.ds(b * UNROLL, UNROLL)
        for s in both:
            add(
                row_out.at[h, s, layers], row_in.at[h, 1 - s, layers],
                lat_send.at[s], lat_recv.at[h, b, 1 - s], {"lat": lat_to[s]}, lat_has[s],
            )
        return table

    corner_rows = 2 * LANES // n_o
    lat_rows = UNROLL * FIELDS

    def rad_rows(h):
        return (COMPS + (1 if h == 0 else 0)) * n_a

    def num_rows(h):
        return rad_rows(h) + 2 * tile_rows

    def start(h, b, early_part=False):
        for copy, cond in messages(h, b, early_part):
            guarded(cond, copy.start)

    def near_planes(b):
        return [p for p, at in ((0, 0), (1, end)) if b == at]

    def arrive(h, b):
        await_rows(lon_recv.at[h, b], 2 * tile_rows)
        for s in both:
            guarded(lat_has[s], functools.partial(await_rows, lat_recv.at[h, b, s], lat_rows))

    def arrive_far(h):
        for p in both:
            guarded(rad_has[p], functools.partial(await_rows, rad_recv.at[h, p], rad_rows(h)))
            guarded(rad_has[p], functools.partial(await_rows, num_recv.at[h, p], num_rows(h)))
        for s in both:
            for p in both:
                guarded(
                    all_of(rad_has[p], lat_has[s]),
                    functools.partial(await_rows, edge_recv.at[h, s, p], FIELDS),
                )
            guarded(
                lat_has[s],
                functools.partial(await_rows, far_recv.at[h, s], blocks_r * corner_rows),
            )

    def sent(h):
        for p in both:
            guarded(rad_has[p], functools.partial(await_rows, rad_send.at[p], rad_rows(h), True))
            guarded(rad_has[p], functools.partial(await_rows, num_send.at[p], num_rows(h), True))
            for s in both:
                guarded(
                    all_of(rad_has[p], lat_has[s]),
                    functools.partial(await_rows, edge_send.at[s, p], FIELDS, True),
                )
        await_rows(lon_send.at[0], blocks_r * 2 * tile_rows, True)
        for s in both:
            guarded(lat_has[s], functools.partial(await_rows, lat_send.at[s], blocks_r * lat_rows, True))
            guarded(lat_has[s], functools.partial(await_rows, far_send.at[s], blocks_r * corner_rows, True))

    def turn(x, shift, axis):
        shift = shift % x.shape[axis]
        return pltpu.roll(x, shift, axis) if shift else x

    def interior(t, r, c):
        tile = v[t][c, r + 1]
        return tile, (
            (w_lat[0, r] * turn(tile, 1, 0) + w_lat[1, r] * turn(tile, -1, 0))
            + (w_lon[0, r] * turn(tile, 1, 1) + w_lon[1, r] * turn(tile, -1, 1))
        )

    def radial(t, r, c, seams):
        total = None
        for face, slot in ((r, r), (r + 1, r + 2)):
            if (slot in (0, n_r + 1)) == seams or (seams is None):
                term = w_rad[face] * v[t][c, slot]
                total = term if total is None else total + term
        return total

    def lane_at(g, j):
        return 2 * (j * FIELDS + g)

    def ends_of(x, k):
        x = turn(x, -k, 1)
        west = jnp.where(lane == 0, x, 0.0)
        east = jnp.where(lane == LANES - 1, x, 0.0)
        if reps == 1:
            return west + east
        gap = [jnp.zeros((n_a, LANES), jnp.float32)] * (reps - 2)
        return jnp.concatenate([west] + gap + [east], 1)

    def edge_rows(low, high):
        return jnp.where(row == 0, low, jnp.where(row == n_a - 1, high, 0.0))

    def seams(t, b, j, c):
        r = b * UNROLL + j
        low, high = (row_sum[t, s, r, 1 + c : 2 + c] for s in both)
        return edge_rows(low, high) + ends_of(col_sum[t, b], lane_at(1 + c, j))

    def pack(h, r, k, tile, packed):
        for i in range(reps):
            piece = slice(i * LANES, (i + 1) * LANES)
            row_out[h, 0, r, k : k + 1, piece] = tile[:1, piece]
            row_out[h, 1, r, k : k + 1, piece] = tile[n_a - 1 :, piece]
        at = lane_at(k, r % UNROLL)
        two = jnp.where(lane < LANES // 2, tile[:, :LANES], tile[:, n_o - LANES :])
        hit = jnp.logical_and(field_of == k, layer_of == r % UNROLL)
        return jnp.where(hit, turn(two, at, 1), packed)

    def pack_first(h, b):
        t = 2 * h
        packed = jnp.zeros((n_a, LANES), jnp.float32)
        for j in range(UNROLL):
            r = b * UNROLL + j
            tiles = [(1 + c, v[t][c, r + 1]) for c in range(COMPS)]
            if h == 0:
                tiles.append((0, eta[r + 1]))
            for k, tile in tiles:
                packed = pack(h, r, k, tile, packed)
                for p, layer in ((0, 0), (1, n_r - 1)):
                    if r == layer:
                        for s in both:
                            for i in range(reps):
                                piece = slice(i * LANES, (i + 1) * LANES)
                                edge_out[h, s, p, k : k + 1, piece] = tile[row_edge[s] : row_edge[s] + 1, piece]
        col_first[h, b] = packed
        for s in both:
            corner_out[h, b, s] = packed[row_edge[s] : row_edge[s] + 1]

    def prepare(h, b):
        t = 2 * h
        packed = col_first[h, b]
        for j in range(UNROLL):
            r = b * UNROLL + j
            if h == 0:
                own = eta[r + 1]
                below = jnp.where(row == 0, 0.0, harmonic(own, turn(own, 1, 0)))
                above = jnp.where(row == n_a - 1, 0.0, turn(below, -1, 0))
                west = jnp.where(lane_wide == 0, 0.0, harmonic(own, turn(own, 1, 1)))
                east = jnp.where(lane_wide == n_o - 1, 0.0, turn(west, -1, 1))
                w_lat[0, r] = below
                w_lat[1, r] = above
                w_lon[0, r] = west
                w_lon[1, r] = east
                d = 0.5 * own + (below + above) + (west + east)
                if r > 0:
                    down = harmonic(own, eta[r])
                    w_rad[r] = down
                    d = d + down
                if r < n_r - 1:
                    d = d + harmonic(own, eta[r + 2])
                part[r] = d
                packed = pack(h, r, FIELDS - 1, d, packed)
        for j in range(UNROLL):
            r = b * UNROLL + j
            for c in range(COMPS):
                tile, near = interior(t, r, c)
                if h == 0:
                    total = f[c, r] + near
                    if r > 0:
                        total = total + w_rad[r] * v[t][c, r]
                    if r < n_r - 1:
                        up = w_rad[r + 1] if j < UNROLL - 1 else harmonic(eta[r + 1], eta[r + 2])
                        total = total + up * v[t][c, r + 2]
                else:
                    total = f[c, r] + (near + radial(t, r, c, False))
                num[h, c, r] = total
                packed = pack(h, r, 1 + COMPS + c, total, packed)
        col_out[h, b] = packed

    def repeat_from(x, field, shifts):
        fields = field_of if x.shape[0] == n_a else field_of[:1]
        only = jnp.where(fields == field, x, 0.0)
        return functools.reduce(jnp.add, [turn(only, 2 * k, 1) for k in shifts])

    def repeat_first(x):
        return repeat_from(x, 0, range(COMPS + 1))

    def repeat_last(x):
        return repeat_from(x, FIELDS - 1, [1 + c - (FIELDS - 1) for c in range(COMPS)])

    def joined(from_west, from_east):
        at = even if from_west.shape[0] == n_a else even[:1]
        return jnp.where(at, turn(from_west, 1, 1), turn(from_east, -1, 1))

    def near_side(h, b):
        t = 2 * h
        far = joined(col_in[h, b, 0], col_in[h, b, 1])
        col_far[h, b] = far
        if h == 0:
            w = harmonic0(repeat_first(far), repeat_first(col_out[h, b]))
            col_w[b] = w
        else:
            w = col_w[b]
        col_sum[t, b] = w * far
        for s in both:
            for r in range(b * UNROLL, (b + 1) * UNROLL):
                if h == 0:
                    w = harmonic(
                        jnp.broadcast_to(row_in[h, s, r, :1], (n_a, n_o)),
                        jnp.broadcast_to(row_out[h, s, r, :1], (n_a, n_o)),
                    )
                    row_w[s, r] = w
                else:
                    w = row_w[s, r]
                row_sum[t, s, r] = w * row_in[h, s, r]

    def far_rows(h, b):
        t = 2 * h
        for s in both:
            for j in range(UNROLL):
                r = b * UNROLL + j
                far = row_in[h, s, r]
                column = corner_t[h, b, pl.ds(lane_at(0, j), FIELDS, stride=2), :]
                corner = ends_of(column, 2 * s + 1)
                near = [p for p, layer in ((0, 0), (1, n_r - 1)) if r == layer]
                w = row_w[s, r]
                if h == 0:
                    far_eta = jnp.broadcast_to(row_in[h, s, r, :1], (n_a, n_o))
                    wq = harmonic0(far_eta, corner[:1])
                    d = row_in[h, s, r, FIELDS - 1 :] + (w + wq)
                    for p in near:
                        wp = harmonic0(far_eta, edge_in[h, s, p, :1])
                        row_p[s, p] = wp
                        d = d + wp
                    row_q[s, r] = wq
                    gain_far = RELAX / d
                    row_g[s, r] = gain_far
                else:
                    wq, gain_far = row_q[s, r], row_g[s, r]
                total = turn(far, -COMPS, 0) + w * row_out[h, s, r] + wq * corner
                for p in near:
                    total = total + row_p[s, p] * edge_in[h, s, p]
                row_sum[t + 1, s, r] = w * ((1.0 - RELAX) * far + gain_far * total)

    def side_of(h, p):
        return joined(side_in[h, p, 0], side_in[h, p, 1])

    def far_cols(h, b):
        t = 2 * h
        far = col_far[h, b]
        own = col_out[h, b]
        stacked = jnp.zeros((8, LANES), jnp.float32)
        spot = lax.broadcasted_iota(jnp.int32, (8, LANES), 0)
        for s in both:
            stacked = jnp.where(spot == 2 * s + 1, turn(corner_in[h, b, s, 0], 1, 1), stacked)
            stacked = jnp.where(spot == 2 * s, corner_in[h, b, s, 1], stacked)
        corner_t[h, b, :, :8] = stacked.T
        corners = [joined(corner_in[h, b, s, 0], corner_in[h, b, s, 1]) for s in both]
        move = 2 * FIELDS * (UNROLL - 1)
        sides = {p: turn(side_of(h, p), -move if p == 0 else move, 1) for p in near_planes(b)}
        w = col_w[b]
        if h == 0:
            far_eta = repeat_first(far)
            d = repeat_last(far) + w
            for s in both:
                wd = jnp.where(
                    row_thin == row_edge[s], harmonic0(far_eta, repeat_first(corners[s])), 0.0,
                )
                col_d[b, s] = wd
                d = d + wd
            for p in near_planes(b):
                wp = jnp.where(
                    layer_of == (0, UNROLL - 1)[p], harmonic0(far_eta, repeat_first(sides[p])), 0.0,
                )
                col_p[p] = wp
                d = d + wp
            col_g[b] = RELAX / jnp.where(d > 0.0, d, 1.0)
        total = turn(far, -2 * COMPS, 1) + w * own
        for s in both:
            total = total + col_d[b, s] * corners[s]
        for p in near_planes(b):
            total = total + col_p[p] * sides[p]
        col_sum[t + 1, b] = w * ((1.0 - RELAX) * far + col_g[b] * total)

    def link_plane(p):
        slot, layer, face = ((0, 1, 0), (n_r + 1, n_r, n_r))[p]
        w_rad[face] = harmonic(eta[slot], eta[layer])

    def update_plane(h, p):
        t = 2 * h
        slot, layer, face, j = ((0, 1, 0, UNROLL - 1), (n_r + 1, n_r, n_r, 0))[p]
        side = side_of(h, p)
        if h == 0:
            own = eta[slot]
            w = w_rad[face]
            wq = harmonic0(own, ends_of(side, lane_at(0, j)))
            plane_q[p] = wq
            d = plane_d[p] + (w + wq)
            wl = edge_rows(*(harmonic0(own, edge_in[h, s, p, :1]) for s in both))
            plane_l[p] = wl
            plane_g[p] = RELAX / (d + wl)
        for c in range(COMPS):
            total = plane_num[h, p, c] + w_rad[face] * v[t][c, layer]
            total = total + plane_l[p] * edge_rows(*(edge_in[h, s, p, 1 + c : 2 + c] for s in both))
            total = total + plane_q[p] * ends_of(side, lane_at(1 + c, j))
            v[t + 1][c, slot] = (1.0 - RELAX) * v[t][c, slot] + plane_g[p] * total

    def settle(b):
        for j in range(UNROLL):
            r = b * UNROLL + j
            low, high = (row_w[s, r, :1] for s in both)
            d = part[r] + (edge_rows(low, high) + ends_of(col_w[b], lane_at(0, j)))
            if r == 0:
                d = d + w_rad[0]
            if r == n_r - 1:
                d = d + w_rad[n_r]
            diag[r] = d
            gain[r] = RELAX / d

    def advance_face(h, b):
        t = 2 * h
        if h == 0:
            settle(b)
        for c in range(COMPS):
            for j in range(UNROLL):
                r = b * UNROLL + j
                total = num[h, c, r] + seams(t, b, j, c)
                if r in (0, n_r - 1):
                    total = total + radial(t, r, c, True)
                v[t + 1][c, r + 1] = (1.0 - RELAX) * v[t][c, r + 1] + gain[r] * total

    def whole_flux(t, b, c, j):
        r = b * UNROLL + j
        tile, near = interior(t, r, c)
        total = (f[c, r] + near) + (radial(t, r, c, None) + seams(t, b, j, c))
        return r, tile, total

    def second_step(t, b):
        for c in range(COMPS):
            for j in range(UNROLL):
                r, tile, total = whole_flux(t, b, c, j)
                v[t + 1][c, r + 1] = (1.0 - RELAX) * tile + gain[r] * total

    def residual(b):
        t = SWEEPS
        for c in range(COMPS):
            for i in range(UNROLL // 2):
                two = jnp.zeros((n_a, n_o), jnp.float32)
                for j in (2 * i, 2 * i + 1):
                    r, tile, total = whole_flux(t, b, c, j)
                    two = two + (total - diag[r] * tile)
                at = pl.ds((c * (n_r // 2) + b * (UNROLL // 2) + i) * n_a, n_a)
                for k in range(reps):
                    pairs[k, at] = two[:, k * LANES : (k + 1) * LANES]

    for b in reversed(range(blocks_r)):
        loaded(b)
        phase(functools.partial(pack_first, 0, b))
    pl.semaphore_wait(barrier, expected)
    for b in reversed(range(blocks_r)):
        start(0, b, True)
    for b in reversed(range(blocks_r)):
        phase(functools.partial(prepare, 0, b))
        start(0, b)
    load_ids.wait()

    near_devices = [({"lat": lat_to[s]}, lat_has[s], lat_has[1 - s]) for s in both] + [
        ({"lon": lon_to[q]}, None, None) for q in both
    ]

    def ids_copy(i):
        return Link(functools.partial(
            pltpu.make_async_remote_copy, ids, ids_near.at[i ^ 1], ids_send.at[i], ids_recv.at[i],
            device_id=near_devices[i][0], device_id_type=MESH,
        ))

    for i, (_, send, _) in enumerate(near_devices):
        guarded(send, ids_copy(i).start)

    def wave_signal(k):
        for s in both:
            def tell():
                pl.semaphore_signal(wave.at[k, s], inc=1, device_id={"lat": lat_to[s]}, device_id_type=MESH)
            pl.when(lat_has[s])(tell)

    def wave_wait(k):
        for s in both:
            def hear():
                pl.semaphore_wait(wave.at[k, s], 1)
            pl.when(lat_has[1 - s])(hear)

    waves = n_lat - 1 if direct else 0
    if waves:
        wave_signal(0)

    lat_cell = (me_lat * n_a + row).astype(jnp.float32)
    lon_cell = (me_lon * n_o + lane_wide).astype(jnp.float32)
    phi = math.pi * ((lat_cell + 0.5) / (n_lat * n_a) - 0.5)
    lam = (2.0 * math.pi) * (lon_cell[:1] + 0.5) / (n_lon * n_o)
    cos_lat = jnp.cos(phi)
    cos_lon, sin_lon = jnp.cos(lam), jnp.sin(lam)
    rx = cos_lat * cos_lon
    ry = cos_lat * sin_lon
    rz = jnp.sin(phi)
    blocks = ids.shape[1]
    bands = n_a // FACE
    spread_rows = lax.broadcasted_iota(jnp.int32, (blocks, n_o), 0)
    spread_cols = lax.broadcasted_iota(jnp.int32, (blocks, n_o), 1)
    spread = (spread_cols // FACE == spread_rows).astype(jnp.float32)
    numbers = lax.broadcasted_iota(jnp.int32, (SLOT, n_o), 0)

    def cells_of(line, chosen):
        own = jnp.broadcast_to(line.astype(jnp.float32), (8, blocks))
        return jnp.dot(own, chosen, precision=HIGHEST)[:1]

    def hot(line):
        return hot_of(cells_of(line, spread))

    def hot_of(cells):
        return (jnp.abs(cells - numbers.astype(jnp.float32)) < 0.5).astype(jnp.float32)

    onehots = [hot(ids[band : band + 1]) for band in range(bands)]

    for k in range(1, waves):
        wave_wait(k - 1)
        wave_signal(k)

    def s1_copy(step):
        return pltpu.make_async_remote_copy(
            stage_out.at[0], lat_sums.at[me_lat], s1_send.at[0], s1_recv.at[0],
            device_id={"lat": lax.rem(me_lat + step, n_lat)}, device_id_type=MESH,
        )

    here = me_lat * n_lon + me_lon if direct else me_lon
    group = n_lat * n_lon * n_rad if direct else n_lon * n_rad
    plane = n_lon * n_rad

    def s2_copy(step):
        device = {
            "lon": lax.rem(me_lon + (step % plane) // n_rad, n_lon),
            "rad": lax.rem(me_rad + step % n_rad, n_rad),
        }
        if direct:
            device["lat"] = lax.rem(me_lat + step // plane, n_lat)
        return pltpu.make_async_remote_copy(
            stage_out.at[1], sums.at[here], s2_send.at[0], s2_recv.at[0],
            device_id=device, device_id_type=MESH,
        )

    def cross(k, x, drag):
        return [
            (x[1] * drag[2] - x[2] * drag[1]) * k,
            (x[2] * drag[0] - x[0] * drag[2]) * k,
            (x[0] * drag[1] - x[1] * drag[0]) * k,
        ]

    def torques():
        top = n_r - 1
        guess = [
            [(1.0 - RELAX) * v[2][c, r + 1] + gain[r] * num[1, c, r] for c in range(COMPS)]
            for r in (top, top - 1)
        ]
        drag = [eta[n_r] * (guess[0][c] - guess[1][c]) for c in range(COMPS)]
        twist = cross(cos_lat, (rx, ry, rz), drag) + [cos_lat]
        outer = []
        for s in both:
            k = (me_lat * n_a + (n_a if s else -1)).astype(jnp.float32)
            tilt = math.pi * ((jnp.full((1, n_o), 0.5, jnp.float32) + k) / (n_lat * n_a) - 0.5)
            cos_tilt = jnp.cos(tilt)
            moved = [(row_g[s, r] * row_w[s, r]) * row_out[1, s, r] for r in (top, top - 1)]
            shift = row_in[0, s, top, :1] * (moved[0] - moved[1])
            push = [shift[1 + c : 2 + c] for c in range(COMPS)]
            outer.append(cross(cos_tilt, (cos_tilt * cos_lon, cos_tilt * sin_lon, jnp.sin(tilt)), push))
        moved = col_g[end] * col_w[end] * col_out[1, end]
        shift = repeat_first(col_far[0, end]) * (moved - turn(moved, 2 * FIELDS, 1))
        push = [ends_of(shift, lane_at(1 + c, UNROLL - 1)) for c in range(COMPS)]
        around = n_lon * n_o
        column = jnp.where(
            lane_wide[:1] == 0,
            lax.rem(me_lon * n_o + (around - 1), around), lax.rem(me_lon * n_o + n_o, around),
        ).astype(jnp.float32)
        angle = (2.0 * math.pi) * (column + 0.5) / around
        beside = cross(cos_lat, (cos_lat * jnp.cos(angle), cos_lat * jnp.sin(angle), rz), push)
        firsts = [(spread_rows == block).astype(jnp.float32) for block in (blocks - 1, 0)]
        packed = jnp.zeros((1, LANES), jnp.float32)
        for band in range(bands):
            cut = slice(band * FACE, (band + 1) * FACE)

            def stack(parts):
                return jnp.concatenate(
                    parts + [jnp.zeros((8 - len(parts), n_o), jnp.float32)], 0,
                )

            lines = [stack([jnp.sum(x[cut], axis=0, keepdims=True) for x in twist])]
            hots = [onehots[band]]
            lines.append(stack([jnp.sum(x[cut], axis=0, keepdims=True) for x in beside]))
            hots.append(hot_of(jnp.where(
                lane_wide[:1] == 0,
                cells_of(ids_near[2, band : band + 1], firsts[0]),
                cells_of(ids_near[3, band : band + 1], firsts[1]),
            )))
            for s in both:
                if band == (0, bands - 1)[s]:
                    lines.append(stack(outer[s]))
                    other = (bands - 1, 0)[s]
                    hots.append(hot(ids_near[s, other : other + 1]))
            totals = lax.dot_general(
                jnp.concatenate(lines, 1), jnp.concatenate(hots, 1), (((1,), (1,)), ((), ())),
                precision=HIGHEST, preferred_element_type=jnp.float32,
            )
            packed = packed + jnp.concatenate([totals[i : i + 1] for i in range(COMPS + 1)], 1)
        if direct:
            stage_out[1] = packed
            sums[here] = packed
            for step in range(1, group):
                s2_copy(step).start()
        else:
            stage_out[0] = packed
            lat_sums[me_lat] = packed
            for step in range(1, n_lat):
                s1_copy(step).start()

    def surface():
        if waves:
            wave_wait(waves - 1)
        for i, (_, _, take) in enumerate(near_devices):
            guarded(take, ids_copy(i).wait_recv)
        pl.when(is_top)(torques)

    def advance(b):
        phase(functools.partial(prepare, 1, b))
        if b == end:
            surface()
        start(1, b)

    def ready(b, done):
        return all(k in done for k in (b - 1, b, b + 1) if 0 <= k <= end)

    def sweep(h, order, finish, ship):
        stepped, done, shipped = set(), set(), set()

        def near_part(b):
            near_side(h, b)
            far_cols(h, b)

        def main_part(b):
            advance_face(h, b)
            far_rows(h, b)

        for at, b in enumerate(order):
            arrive(h, b)
            if at == 0:
                arrive_far(h)
                for p in both:
                    if h == 0:
                        pl.when(rad_has[p])(functools.partial(link_plane, p))
                    pl.when(rad_has[p])(functools.partial(update_plane, h, p))
            phase(functools.partial(near_part, b))
            phase(functools.partial(main_part, b))
            stepped.add(b)
            for k in order:
                if k not in done and ready(k, stepped):
                    phase(functools.partial(finish, k))
                    done.add(k)
                    if ship:
                        if k == end:
                            sent(0)
                        phase(functools.partial(pack_first, 1, k))
                        start(1, k, True)
                    for m in [end, 0] + order:
                        if ship and m not in shipped and ready(m, done):
                            ship(m)
                            shipped.add(m)

    first_order = list(reversed(range(blocks_r)))
    second_order = [end] + list(reversed(range(2, end))) + [k for k in (0, 1) if k < end]

    def ship_off(b):
        advance(b)

    sweep(0, first_order, functools.partial(second_step, 1), ship_off)

    if not direct:
        @pl.when(is_top)
        def _():
            await_thin(s1_recv.at[0], n_lat - 1)
            total = lat_sums[0]
            for i in range(1, n_lat):
                total = total + lat_sums[i]
            stage_out[1] = total
            sums[here] = total
            for step in range(1, group):
                s2_copy(step).start()

    sweep(1, second_order, residual, None)

    half = n_o // 2
    thin_r = lax.broadcasted_iota(jnp.int32, (LANES, half), 0)
    thin_c = lax.broadcasted_iota(jnp.int32, (LANES, half), 1)
    count = COMPS * (n_r // 2) * n_a // 2
    merged = jnp.zeros((count, half), jnp.float32)
    for h in range(reps):
        choose = jnp.where((thin_r + h * LANES) // 2 == thin_c, 0.125, 0.0).astype(jnp.bfloat16)
        summed = pairs[h, pl.ds(0, count, stride=2)] + pairs[h, pl.ds(1, count, stride=2)]
        big = summed.astype(jnp.bfloat16)
        small = (summed - big.astype(jnp.float32)).astype(jnp.bfloat16)
        merged = merged + (
            jnp.dot(big, choose, preferred_element_type=jnp.float32)
            + jnp.dot(small, choose, preferred_element_type=jnp.float32)
        )
    mine = count // COMPS
    spot = pl.ds(pl.multiple_of(me_rad * mine, mine), mine)
    for c in range(COMPS):
        coarse[c, spot] = merged[c * mine : (c + 1) * mine]

    def g_copy(step):
        return pltpu.make_async_remote_copy(
            coarse.at[:, spot], coarse.at[:, spot], g_send.at[step - 1], g_recv.at[me_rad],
            device_id={"rad": lax.rem(me_rad + step, n_rad)}, device_id_type=MESH,
        )

    for step in range(1, n_rad):
        g_copy(step).start()

    sources = n_lat * n_lon if direct else n_lon
    pl.when(is_top)(functools.partial(await_thin, s2_recv.at[0], sources - 1))
    pl.when(jnp.logical_not(is_top))(functools.partial(await_thin, s2_recv.at[0], sources))
    terms = [sums[i] for i in range(sources)]
    while len(terms) > 1:
        terms = [terms[i] + terms[i + 1] if i + 1 < len(terms) else terms[i] for i in range(0, len(terms), 2)]
    total = terms[0]
    area = total[:, COMPS * SLOT : (COMPS + 1) * SLOT]
    valid = lax.broadcasted_iota(jnp.int32, (1, SLOT), 1) < PLATES
    root = jnp.sqrt(jnp.where(valid, area, 1.0))
    turns = jnp.concatenate(
        [total[:, i * SLOT : (i + 1) * SLOT] / root for i in range(COMPS)]
        + [jnp.zeros((8 - COMPS, SLOT), jnp.float32)], 0,
    )
    for band in range(bands):
        cut = slice(band * FACE, (band + 1) * FACE)
        cell = jnp.dot(turns, onehots[band], precision=HIGHEST, preferred_element_type=jnp.float32)
        ox, oy, oz = (cell[i : i + 1] for i in range(COMPS))
        plate[0, cut] = oy * rz[cut] - oz * ry[cut]
        plate[1, cut] = oz * rx[cut] - ox * rz[cut]
        plate[2, cut] = ox * ry[cut] - oy * rx[cut]

    sent(1)
    for i, (_, send, _) in enumerate(near_devices):
        guarded(send, ids_copy(i).wait_send)

    @pl.when(is_top)
    def _():
        if not direct:
            await_thin(s1_send.at[0], n_lat - 1, True)
        await_thin(s2_send.at[0], group - 1, True)

    for step in range(1, n_rad):
        source = lax.rem(me_rad + step, n_rad)
        region = coarse.at[:, pl.ds(pl.multiple_of(source * mine, mine), mine)]
        pltpu.make_async_remote_copy(
            region, region, g_send.at[0], g_recv.at[source],
            device_id={"rad": source}, device_id_type=MESH,
        ).wait_recv()
        g_copy(step).wait_send()


def write_out(last, coarse, plate, new_v_out, coarse_out, plate_out, sem):
    n_r = new_v_out.shape[1]
    copies = [
        pltpu.make_async_copy(last.at[:, pl.ds(1, n_r)], new_v_out, sem.at[0]),
        pltpu.make_async_copy(coarse, coarse_out, sem.at[1]),
        pltpu.make_async_copy(plate, plate_out, sem.at[2]),
    ]
    for copy in copies:
        copy.start()
    for copy in copies:
        copy.wait()


def on_device(sizes, velocity, forcing, viscosity, plate_ids):
    n_lat, n_lon, n_rad = sizes
    _, n_r, n_a, n_o = velocity.shape
    chunks = n_r // UNROLL
    f32 = jnp.float32
    dma = pltpu.SemaphoreType.DMA
    direct = n_lat * n_lon * n_rad <= DIRECT
    group = n_lat * n_lon * n_rad if direct else n_lon * n_rad
    sources = n_lat * n_lon if direct else n_lon
    in_any = pl.BlockSpec(memory_space=pl.ANY)
    in_vmem = pl.BlockSpec(memory_space=pltpu.VMEM)
    coarse_rows = n_rad * (n_r // 2) * (n_a // 2)
    whole = (n_r, n_a, n_o)
    thin = (n_a, LANES)

    def vmem(*shape):
        return pltpu.VMEM(shape, f32)

    held = pl.pallas_call(
        functools.partial(kernel, sizes),
        out_shape=(
            pltpu.VMEM((COMPS, n_r + 2, n_a, n_o), f32),
            pltpu.VMEM((COMPS, coarse_rows, n_o // 2), f32),
            pltpu.VMEM((COMPS, n_a, n_o), f32),
        ),
        in_specs=[pl.BlockSpec(memory_space=pltpu.HBM)] * 4,
        out_specs=(in_vmem,) * 3,
        scratch_shapes=[
            vmem(SWEEPS, COMPS, n_r + 2, n_a, n_o),
            pltpu.VMEM(plate_ids.shape, jnp.int32),
            pltpu.VMEM((4,) + plate_ids.shape, jnp.int32),
            vmem(COMPS, *whole),
            vmem(n_r + 2, n_a, n_o),
            vmem(2, *whole),
            vmem(2, *whole),
            vmem(n_r + 1, n_a, n_o),
            vmem(*whole),
            vmem(*whole),
            vmem(*whole),
            vmem(2, COMPS, *whole),
            vmem(2, 2, *whole),
            vmem(2, 2, *whole),
            vmem(4, 2, *whole),
            vmem(2, *whole),
            vmem(2, *whole),
            vmem(2, *whole),
            vmem(2, 2, n_a, n_o),
            vmem(2, chunks, *thin),
            vmem(2, chunks, *thin),
            vmem(2, chunks, 2, *thin),
            vmem(2, chunks, *thin),
            vmem(4, chunks, *thin),
            vmem(chunks, *thin),
            vmem(chunks, *thin),
            vmem(chunks, 2, *thin),
            vmem(2, *thin),
            vmem(2, 2, COMPS, n_a, n_o),
            vmem(2, n_a, n_o),
            vmem(2, n_a, n_o),
            vmem(2, n_a, n_o),
            vmem(2, n_a, n_o),
            vmem(2, chunks, 2, 1, LANES),
            vmem(2, chunks, 2, 2, 1, LANES),
            vmem(2, chunks, LANES, LANES),
            vmem(2, 2, 2, n_a, n_o),
            vmem(2, 2, 2, n_a, n_o),
            vmem(2, 2, 2, *thin),
            vmem(n_o // LANES, COMPS * (n_r // 2) * n_a, LANES),
            vmem(sources, 1, LANES),
            vmem(n_lat, 1, LANES),
            vmem(2, 1, LANES),
            vmem(max(7 * UNROLL * n_a, chunks * (UNROLL * FIELDS + 8)), 1, n_o),
            vmem(max(group, sources, n_lat), 1, LANES),
            dma((chunks + 1,)),
            dma((1,)),
            dma((2,)),
            dma((2,)),
            dma((2,)),
            dma((2, 2)),
            dma((2, chunks)),
            dma((2, chunks, 2)),
            dma((2, 2)),
            dma((2, 2)),
            dma((2, 2, 2)),
            dma((2,)),
            dma((2, 2)),
            dma((4,)),
            dma((4,)),
            pltpu.SemaphoreType.REGULAR((n_lat - 1 if direct else 1, 2)),
            dma((1,)),
            dma((1,)),
            dma((1,)),
            dma((1,)),
            dma((n_rad,)),
            dma((n_rad,)),
        ],
        compiler_params=pltpu.CompilerParams(
            collective_id=0, has_side_effects=True, vmem_limit_bytes=32 * 2**20
        ),
    )(*(
        pltpu.with_memory_space_constraint(x, pltpu.HBM)
        for x in (velocity, forcing, viscosity, plate_ids)
    ))
    new_v, coarse, plate = pl.pallas_call(
        write_out,
        out_shape=(
            jax.ShapeDtypeStruct(velocity.shape, f32),
            jax.ShapeDtypeStruct((COMPS, coarse_rows, n_o // 2), f32),
            jax.ShapeDtypeStruct((COMPS, n_a, n_o), f32),
        ),
        in_specs=[in_vmem] * 3,
        out_specs=(in_any,) * 3,
        scratch_shapes=[dma((3,))],
        compiler_params=pltpu.CompilerParams(vmem_limit_bytes=4 * 2**20),
    )(*(pltpu.with_memory_space_constraint(x, pltpu.VMEM) for x in held))
    coarse = coarse.reshape(COMPS, n_rad * (n_r // 2), n_a // 2, n_o // 2)
    return new_v, coarse, plate


def solution(mesh):
    sizes = tuple(mesh.shape[a] for a in ("lat", "lon", "rad"))
    field = P(None, "rad", "lat", "lon")
    return jax.shard_map(
        functools.partial(on_device, sizes),
        mesh=mesh,
        in_specs=(field, field, P("rad", "lat", "lon"), P("lat", "lon")),
        out_specs=(field, P(None, None, "lat", "lon"), P(None, "lat", "lon")),
        check_vma=False,
    )
```

```python
import functools
import math

import jax
import jax.numpy as jnp
from jax import lax
from jax.experimental import pallas as pl
from jax.experimental.pallas import tpu as pltpu
from jax.sharding import PartitionSpec as P

SWEEPS = 3
PLATES = 12
FACE = 8
RELAX = 0.8
COMPS = 3
LANES = 128
SLOT = 32
MESH = pl.DeviceIdType.MESH
HIGHEST = lax.Precision.HIGHEST
UNROLL = 8
DIRECT = 64
FIELDS = 2 * (COMPS + 1)
PACK = COMPS + 1


def harmonic(own, other):
    return 2.0 * own * other / (own + other)


def harmonic0(own, other):
    return 2.0 * own * other / jnp.maximum(own + other, 1e-30)


class Link:
    def __init__(self, make):
        self.make = make

    def start(self):
        self.make().start()

    def wait_send(self):
        self.make().wait_send()

    def wait_recv(self):
        self.make().wait_recv()


def kernel(
    sizes, vel, forc, visc, ids_in,
    last, coarse, plate,
    early, ids, ids_near, f, eta, w_lat, w_lon, w_rad, gain, diag, part, num,
    row_out, row_in, more_out, more_in, row_sum, row_w, row_g, row_q, row_p,
    col_first, col_out, col_in, col_far, col_sum, col_w, col_g, col_d, col_p,
    plane_num, plane_d, plane_g, plane_l, plane_q,
    corner_out, corner_in, corner_t, edge_out, edge_in, side_in,
    pairs, sums, lat_sums, stage_out, tally, tally_thin,
    load_sem, lon_send, lat_send, rad_send, num_send, edge_send, lon_recv, lat_recv, late_lon_send, late_lat_send, late_lon_recv, late_lat_recv, rad_recv, num_recv, edge_recv, far_send, far_recv,
    ids_send, ids_recv, wave, s1_send, s1_recv, s2_send, s2_recv, g_send, g_recv,
):
    n_lat, n_lon, n_rad = sizes
    n_r, n_a, n_o = visc.shape
    me_lat, me_lon, me_rad = (lax.axis_index(a) for a in ("lat", "lon", "rad"))
    lat_has = (me_lat > 0, me_lat < n_lat - 1)
    rad_has = (me_rad > 0, me_rad < n_rad - 1)
    lat_to = (me_lat - 1, me_lat + 1)
    rad_to = (me_rad - 1, me_rad + 1)
    lon_to = (lax.rem(me_lon + n_lon - 1, n_lon), lax.rem(me_lon + 1, n_lon))
    is_top = me_rad == n_rad - 1
    direct = n_lat * n_lon * n_rad <= DIRECT
    v = [early.at[t] for t in range(SWEEPS)] + [last]
    blocks_r = n_r // UNROLL
    end = blocks_r - 1
    both = (0, 1)

    def guarded(cond, call):
        if cond is None:
            call()
        else:
            pl.when(cond)(call)

    def all_of(*conds):
        conds = [c for c in conds if c is not None]
        return functools.reduce(jnp.logical_and, conds)

    barrier = pltpu.get_barrier_semaphore()

    def greet(device):
        pl.semaphore_signal(barrier, inc=1, device_id=device, device_id_type=MESH)

    expected = n_lon * n_rad - 1
    for step in range(1, n_lon * n_rad):
        greet({
            "lon": lax.rem(me_lon + step // n_rad, n_lon),
            "rad": lax.rem(me_rad + step % n_rad, n_rad),
        })
    for s in both:
        if direct:
            pl.when(lat_has[s])(functools.partial(greet, {"lat": lat_to[s]}))
            expected = expected + jnp.where(lat_has[s], 1, 0)
        for q in both:
            pl.when(lat_has[s])(functools.partial(greet, {"lat": lat_to[s], "lon": lon_to[q]}))
            expected = expected + jnp.where(lat_has[s], 1, 0)
        for p in both:
            has = all_of(lat_has[s], rad_has[p])
            pl.when(has)(functools.partial(greet, {"lat": lat_to[s], "rad": rad_to[p]}))
            expected = expected + jnp.where(has, 1, 0)
    if not direct:
        for step in range(1, n_lat):
            greet({"lat": lax.rem(me_lat + step, n_lat)})
        expected = expected + (n_lat - 1)

    def load_chunk(b, rest):
        here_r = pl.ds(b * UNROLL, UNROLL)
        inner = pl.ds(1 + b * UNROLL, UNROLL)
        if rest:
            return [pltpu.make_async_copy(forc.at[:, here_r], f.at[:, here_r], load_sem.at[blocks_r + b])]
        return [
            pltpu.make_async_copy(visc.at[here_r], eta.at[inner], load_sem.at[b]),
            pltpu.make_async_copy(vel.at[:, here_r], v[0].at[:, inner], load_sem.at[b]),
        ]

    for rest in (False, True):
        for b in reversed(range(blocks_r)):
            for load in load_chunk(b, rest):
                load.start()
    load_ids = pltpu.make_async_copy(ids_in, ids, load_sem.at[2 * blocks_r])
    load_ids.start()

    def rows_of(ref):
        return ref.size // n_o

    def await_rows(sem, rows, sending=False):
        some = tally.at[pl.ds(0, rows)]
        copy = pltpu.make_async_remote_copy(
            some, some, sem, sem, device_id={"lon": lon_to[1]}, device_id_type=MESH,
        )
        copy.wait_send() if sending else copy.wait_recv()

    def await_thin(sem, rows, sending=False):
        some = tally_thin.at[pl.ds(0, rows)]
        copy = pltpu.make_async_remote_copy(
            some, some, sem, sem, device_id={"lon": lon_to[1]}, device_id_type=MESH,
        )
        copy.wait_send() if sending else copy.wait_recv()

    def loaded(b, rest=False):
        fields = COMPS if rest else COMPS + 1
        some = tally.at[pl.ds(0, fields * UNROLL * n_a)]
        pltpu.make_async_copy(some, some, load_sem.at[blocks_r + b if rest else b]).wait()

    lane_wide = lax.broadcasted_iota(jnp.int32, (n_a, n_o), 1)
    lane = lax.broadcasted_iota(jnp.int32, (n_a, LANES), 1)
    row = lax.broadcasted_iota(jnp.int32, (n_a, n_o), 0)
    row_thin = lax.broadcasted_iota(jnp.int32, (n_a, LANES), 0)
    even = lane % 2 == 0
    field_of = (lane + 1) % LANES // 2 % FIELDS
    layer_of = (lane + 1) % LANES // (2 * FIELDS)
    reps = n_o // LANES
    row_edge = (0, n_a - 1)
    lane_edge = (0, n_o - 1)
    thin_edge = (0, LANES - 1)

    plane_rows = n_a
    tile_rows = n_a * LANES // n_o

    def phase(call):
        pl.when(me_lat >= 0)(call)

    for p, slot, face in ((0, 0, 0), (1, n_r + 1, n_r)):
        @pl.when(jnp.logical_not(rad_has[p]))
        def _():
            zero_plane = jnp.zeros((n_a, n_o), jnp.float32)
            w_rad[face] = zero_plane
            for t in range(SWEEPS + 1):
                for c in range(COMPS):
                    v[t][c, slot] = zero_plane
            for h in both:
                for s in both:
                    edge_in[h, s, p] = jnp.zeros((PACK, n_o), jnp.float32)
                    side_in[h, p, s] = jnp.zeros((n_a, LANES), jnp.float32)
    for s in both:
        @pl.when(jnp.logical_not(lat_has[s]))
        def _():
            blank_rows = jnp.zeros((PACK, n_o), jnp.float32)
            for h in both:
                for r in range(n_r):
                    row_in[h, s, r] = blank_rows
                    more_in[h, s, r] = blank_rows + 1.0
                for b in range(blocks_r):
                    for q in both:
                        corner_in[h, b, s, q] = jnp.zeros((1, LANES), jnp.float32)
                for p in both:
                    edge_in[h, s, p] = blank_rows
            ids_near[s] = jnp.zeros(ids.shape, jnp.int32)

    def messages(h, b, early_part):
        t = 2 * h
        table = []

        def add(src, dst, sends, takes, device, cond):
            table.append((Link(functools.partial(
                pltpu.make_async_remote_copy, src, dst, sends, takes,
                device_id=device, device_id_type=MESH,
            )), cond))

        for p, layer, slot in ((0, 1, n_r + 1), (1, n_r, 0)):
            if p not in near_planes(b):
                continue
            device = {"rad": rad_to[p]}
            if early_part:
                sems = (rad_send.at[p], rad_recv.at[h, 1 - p])
                add(v[t].at[:, layer], v[t].at[:, slot], *sems, device, rad_has[p])
                if h == 0:
                    add(eta.at[layer], eta.at[slot], *sems, device, rad_has[p])
            sems = (num_send.at[p], num_recv.at[h, 1 - p])
            if early_part:
                for q in both:
                    add(
                        col_first.at[h, b], side_in.at[h, 1 - p, 1 - q], *sems,
                        {"lon": lon_to[q], "rad": rad_to[p]}, rad_has[p],
                    )
                for s in both:
                    add(
                        edge_out.at[h, s, p], edge_in.at[h, 1 - s, 1 - p],
                        edge_send.at[s, p], edge_recv.at[h, 1 - s, 1 - p],
                        {"lat": lat_to[s], "rad": rad_to[p]}, all_of(rad_has[p], lat_has[s]),
                    )
            else:
                add(num.at[h, :, layer - 1], plane_num.at[h, 1 - p], *sems, device, rad_has[p])
                if h == 0:
                    add(part.at[layer - 1], plane_d.at[1 - p], *sems, device, rad_has[p])
        layers = pl.ds(b * UNROLL, UNROLL)
        columns, rows, rows_at = (col_first, row_out, row_in) if early_part else (col_out, more_out, more_in)
        lon_sems = (lon_send, lon_recv) if early_part else (late_lon_send, late_lon_recv)
        lat_sems = (lat_send, lat_recv) if early_part else (late_lat_send, late_lat_recv)
        if early_part:
            for s in both:
                for q in both:
                    add(
                        corner_out.at[h, b, s], corner_in.at[h, b, 1 - s, 1 - q],
                        far_send.at[s], far_recv.at[h, 1 - s],
                        {"lat": lat_to[s], "lon": lon_to[q]}, lat_has[s],
                    )
        for q in both:
            add(
                columns.at[h, b], col_in.at[h, b, 0 if early_part else 1, 1 - q],
                lon_sems[0].at[0], lon_sems[1].at[h, b], {"lon": lon_to[q]}, None,
            )
        for s in both:
            add(
                rows.at[h, s, layers], rows_at.at[h, 1 - s, layers],
                lat_sems[0].at[s], lat_sems[1].at[h, b, 1 - s], {"lat": lat_to[s]}, lat_has[s],
            )
        return table

    corner_rows = 2 * LANES // n_o
    lat_rows = UNROLL * PACK

    def rad_rows(h):
        return (COMPS + (1 if h == 0 else 0)) * n_a

    def num_rows(h):
        return rad_rows(h) + 2 * tile_rows

    def start(h, b, early_part=False):
        for copy, cond in messages(h, b, early_part):
            guarded(cond, copy.start)

    def near_planes(b):
        return [p for p, at in ((0, 0), (1, end)) if b == at]

    def arrive(h, b):
        await_rows(lon_recv.at[h, b], 2 * tile_rows)
        for s in both:
            guarded(lat_has[s], functools.partial(await_rows, lat_recv.at[h, b, s], lat_rows))

    def arrive_late(h, b):
        await_rows(late_lon_recv.at[h, b], 2 * tile_rows)
        for s in both:
            guarded(lat_has[s], functools.partial(await_rows, late_lat_recv.at[h, b, s], lat_rows))

    def arrive_planes(h):
        for p in both:
            guarded(rad_has[p], functools.partial(await_rows, rad_recv.at[h, p], rad_rows(h)))

    def arrive_far(h):
        for p in both:
            guarded(rad_has[p], functools.partial(await_rows, num_recv.at[h, p], num_rows(h)))
        for s in both:
            for p in both:
                guarded(
                    all_of(rad_has[p], lat_has[s]),
                    functools.partial(await_rows, edge_recv.at[h, s, p], PACK),
                )
            guarded(
                lat_has[s],
                functools.partial(await_rows, far_recv.at[h, s], blocks_r * corner_rows),
            )

    def sent(h):
        for p in both:
            guarded(rad_has[p], functools.partial(await_rows, rad_send.at[p], rad_rows(h), True))
            guarded(rad_has[p], functools.partial(await_rows, num_send.at[p], num_rows(h), True))
            for s in both:
                guarded(
                    all_of(rad_has[p], lat_has[s]),
                    functools.partial(await_rows, edge_send.at[s, p], PACK, True),
                )
        await_rows(lon_send.at[0], blocks_r * 2 * tile_rows, True)
        await_rows(late_lon_send.at[0], blocks_r * 2 * tile_rows, True)
        for s in both:
            for sem in (lat_send, late_lat_send):
                guarded(lat_has[s], functools.partial(await_rows, sem.at[s], blocks_r * lat_rows, True))
            guarded(lat_has[s], functools.partial(await_rows, far_send.at[s], blocks_r * corner_rows, True))

    def turn(x, shift, axis):
        shift = shift % x.shape[axis]
        return pltpu.roll(x, shift, axis) if shift else x

    def interior(t, r, c):
        tile = v[t][c, r + 1]
        return tile, (
            (w_lat[0, r] * turn(tile, 1, 0) + w_lat[1, r] * turn(tile, -1, 0))
            + (w_lon[0, r] * turn(tile, 1, 1) + w_lon[1, r] * turn(tile, -1, 1))
        )

    def radial(t, r, c, seams):
        total = None
        for face, slot in ((r, r), (r + 1, r + 2)):
            if (slot in (0, n_r + 1)) == seams or (seams is None):
                term = w_rad[face] * v[t][c, slot]
                total = term if total is None else total + term
        return total

    def lane_at(g, j):
        return 2 * (j * FIELDS + g)

    def ends_of(x, k):
        x = turn(x, -k, 1)
        west = jnp.where(lane == 0, x, 0.0)
        east = jnp.where(lane == LANES - 1, x, 0.0)
        if reps == 1:
            return west + east
        gap = [jnp.zeros((n_a, LANES), jnp.float32)] * (reps - 2)
        return jnp.concatenate([west] + gap + [east], 1)

    def edge_rows(low, high):
        return jnp.where(row == 0, low, jnp.where(row == n_a - 1, high, 0.0))

    def seams(t, b, j, c):
        r = b * UNROLL + j
        low, high = (row_sum[t, s, r, 1 + c : 2 + c] for s in both)
        return edge_rows(low, high) + ends_of(col_sum[t, b], lane_at(1 + c, j))

    def pack(h, r, k, tile, packed, rows):
        for i in range(reps):
            piece = slice(i * LANES, (i + 1) * LANES)
            rows[h, 0, r, k : k + 1, piece] = tile[:1, piece]
            rows[h, 1, r, k : k + 1, piece] = tile[n_a - 1 :, piece]
        at = lane_at(k, r % UNROLL)
        two = jnp.where(lane < LANES // 2, tile[:, :LANES], tile[:, n_o - LANES :])
        hit = jnp.logical_and(field_of == k, layer_of == r % UNROLL)
        return jnp.where(hit, turn(two, at, 1), packed)

    def pack_first(h, b):
        t = 2 * h
        packed = jnp.zeros((n_a, LANES), jnp.float32)
        for j in range(UNROLL):
            r = b * UNROLL + j
            tiles = [(1 + c, v[t][c, r + 1]) for c in range(COMPS)]
            if h == 0:
                tiles.append((0, eta[r + 1]))
            for k, tile in tiles:
                packed = pack(h, r, k, tile, packed, row_out)
                for p, layer in ((0, 0), (1, n_r - 1)):
                    if r == layer:
                        for s in both:
                            for i in range(reps):
                                piece = slice(i * LANES, (i + 1) * LANES)
                                edge_out[h, s, p, k : k + 1, piece] = tile[row_edge[s] : row_edge[s] + 1, piece]
        col_first[h, b] = packed
        for s in both:
            corner_out[h, b, s] = packed[row_edge[s] : row_edge[s] + 1]

    def prepare(h, b):
        t = 2 * h
        packed = jnp.zeros((n_a, LANES), jnp.float32)
        for j in range(UNROLL):
            r = b * UNROLL + j
            if h == 0:
                own = eta[r + 1]
                below = jnp.where(row == 0, 0.0, harmonic(own, turn(own, 1, 0)))
                above = jnp.where(row == n_a - 1, 0.0, turn(below, -1, 0))
                west = jnp.where(lane_wide == 0, 0.0, harmonic(own, turn(own, 1, 1)))
                east = jnp.where(lane_wide == n_o - 1, 0.0, turn(west, -1, 1))
                w_lat[0, r] = below
                w_lat[1, r] = above
                w_lon[0, r] = west
                w_lon[1, r] = east
                d = 0.5 * own + (below + above) + (west + east)
                if r > 0:
                    down = harmonic(own, eta[r])
                    w_rad[r] = down
                    d = d + down
                if r < n_r - 1:
                    d = d + harmonic(own, eta[r + 2])
                part[r] = d
                packed = pack(h, r, 0, d, packed, more_out)
        for j in range(UNROLL):
            r = b * UNROLL + j
            for c in range(COMPS):
                tile, near = interior(t, r, c)
                if h == 0:
                    total = f[c, r] + near
                    if r > 0:
                        total = total + w_rad[r] * v[t][c, r]
                    if r < n_r - 1:
                        up = w_rad[r + 1] if j < UNROLL - 1 else harmonic(eta[r + 1], eta[r + 2])
                        total = total + up * v[t][c, r + 2]
                else:
                    total = f[c, r] + (near + radial(t, r, c, False))
                num[h, c, r] = total
                packed = pack(h, r, 1 + c, total, packed, more_out)
        col_out[h, b] = packed

    def repeat_from(x, field, shifts):
        fields = field_of if x.shape[0] == n_a else field_of[:1]
        only = jnp.where(fields == field, x, 0.0)
        return functools.reduce(jnp.add, [turn(only, 2 * k, 1) for k in shifts])

    def repeat_first(x):
        return repeat_from(x, 0, range(COMPS + 1))

    def joined(from_west, from_east):
        at = even if from_west.shape[0] == n_a else even[:1]
        return jnp.where(at, turn(from_west, 1, 1), turn(from_east, -1, 1))

    def near_side(h, b):
        t = 2 * h
        far = joined(col_in[h, b, 0, 0], col_in[h, b, 0, 1])
        col_far[h, b] = far
        if h == 0:
            w = harmonic0(repeat_first(far), repeat_first(col_first[h, b]))
            col_w[b] = w
        else:
            w = col_w[b]
        col_sum[t, b] = w * far
        for s in both:
            for r in range(b * UNROLL, (b + 1) * UNROLL):
                if h == 0:
                    w = harmonic(
                        jnp.broadcast_to(row_in[h, s, r, :1], (PACK, n_o)),
                        jnp.broadcast_to(row_out[h, s, r, :1], (PACK, n_o)),
                    )
                    row_w[s, r] = w
                else:
                    w = row_w[s, r]
                row_sum[t, s, r] = w * row_in[h, s, r]

    def far_rows(h, b):
        t = 2 * h
        for s in both:
            for j in range(UNROLL):
                r = b * UNROLL + j
                far = row_in[h, s, r]
                column = corner_t[h, b, pl.ds(lane_at(0, j), FIELDS, stride=2), :]
                corner = ends_of(column, 2 * s + 1)[:PACK]
                near = [p for p, layer in ((0, 0), (1, n_r - 1)) if r == layer]
                w = row_w[s, r]
                if h == 0:
                    far_eta = jnp.broadcast_to(row_in[h, s, r, :1], (PACK, n_o))
                    wq = harmonic0(far_eta, corner[:1])
                    d = more_in[h, s, r, :1] + (w + wq)
                    for p in near:
                        wp = harmonic0(far_eta, edge_in[h, s, p, :1])
                        row_p[s, p] = wp
                        d = d + wp
                    row_q[s, r] = wq
                    gain_far = RELAX / d
                    row_g[s, r] = gain_far
                else:
                    wq, gain_far = row_q[s, r], row_g[s, r]
                total = more_in[h, s, r] + w * row_out[h, s, r] + wq * corner
                for p in near:
                    total = total + row_p[s, p] * edge_in[h, s, p]
                row_sum[t + 1, s, r] = w * ((1.0 - RELAX) * far + gain_far * total)

    def side_of(h, p):
        return joined(side_in[h, p, 0], side_in[h, p, 1])

    def far_cols(h, b):
        t = 2 * h
        far = col_far[h, b]
        own = col_first[h, b]
        more = joined(col_in[h, b, 1, 0], col_in[h, b, 1, 1])
        stacked = jnp.zeros((8, LANES), jnp.float32)
        spot = lax.broadcasted_iota(jnp.int32, (8, LANES), 0)
        for s in both:
            stacked = jnp.where(spot == 2 * s + 1, turn(corner_in[h, b, s, 0], 1, 1), stacked)
            stacked = jnp.where(spot == 2 * s, corner_in[h, b, s, 1], stacked)
        corner_t[h, b, :, :8] = stacked.T
        corners = [joined(corner_in[h, b, s, 0], corner_in[h, b, s, 1]) for s in both]
        move = 2 * FIELDS * (UNROLL - 1)
        sides = {p: turn(side_of(h, p), -move if p == 0 else move, 1) for p in near_planes(b)}
        w = col_w[b]
        if h == 0:
            far_eta = repeat_first(far)
            d = repeat_first(more) + w
            for s in both:
                wd = jnp.where(
                    row_thin == row_edge[s], harmonic0(far_eta, repeat_first(corners[s])), 0.0,
                )
                col_d[b, s] = wd
                d = d + wd
            for p in near_planes(b):
                wp = jnp.where(
                    layer_of == (0, UNROLL - 1)[p], harmonic0(far_eta, repeat_first(sides[p])), 0.0,
                )
                col_p[p] = wp
                d = d + wp
            col_g[b] = RELAX / jnp.where(d > 0.0, d, 1.0)
        total = more + w * own
        for s in both:
            total = total + col_d[b, s] * corners[s]
        for p in near_planes(b):
            total = total + col_p[p] * sides[p]
        col_sum[t + 1, b] = w * ((1.0 - RELAX) * far + col_g[b] * total)

    def link_plane(p):
        slot, layer, face = ((0, 1, 0), (n_r + 1, n_r, n_r))[p]
        w_rad[face] = harmonic(eta[slot], eta[layer])

    def update_plane(h, p):
        t = 2 * h
        slot, layer, face, j = ((0, 1, 0, UNROLL - 1), (n_r + 1, n_r, n_r, 0))[p]
        side = side_of(h, p)
        if h == 0:
            own = eta[slot]
            w = w_rad[face]
            wq = harmonic0(own, ends_of(side, lane_at(0, j)))
            plane_q[p] = wq
            d = plane_d[p] + (w + wq)
            wl = edge_rows(*(harmonic0(own, edge_in[h, s, p, :1]) for s in both))
            plane_l[p] = wl
            plane_g[p] = RELAX / (d + wl)
        for c in range(COMPS):
            total = plane_num[h, p, c] + w_rad[face] * v[t][c, layer]
            total = total + plane_l[p] * edge_rows(*(edge_in[h, s, p, 1 + c : 2 + c] for s in both))
            total = total + plane_q[p] * ends_of(side, lane_at(1 + c, j))
            v[t + 1][c, slot] = (1.0 - RELAX) * v[t][c, slot] + plane_g[p] * total

    def settle(b):
        for j in range(UNROLL):
            r = b * UNROLL + j
            low, high = (row_w[s, r, :1] for s in both)
            d = part[r] + (edge_rows(low, high) + ends_of(col_w[b], lane_at(0, j)))
            if r == 0:
                d = d + w_rad[0]
            if r == n_r - 1:
                d = d + w_rad[n_r]
            diag[r] = d
            gain[r] = RELAX / d

    def advance_face(h, b):
        t = 2 * h
        if h == 0:
            settle(b)
        for c in range(COMPS):
            for j in range(UNROLL):
                r = b * UNROLL + j
                total = num[h, c, r] + seams(t, b, j, c)
                if r in (0, n_r - 1):
                    total = total + radial(t, r, c, True)
                v[t + 1][c, r + 1] = (1.0 - RELAX) * v[t][c, r + 1] + gain[r] * total

    def whole_flux(t, b, c, j):
        r = b * UNROLL + j
        tile, near = interior(t, r, c)
        total = (f[c, r] + near) + (radial(t, r, c, None) + seams(t, b, j, c))
        return r, tile, total

    def second_step(t, b):
        for c in range(COMPS):
            for j in range(UNROLL):
                r, tile, total = whole_flux(t, b, c, j)
                v[t + 1][c, r + 1] = (1.0 - RELAX) * tile + gain[r] * total

    def pair_rows(c, b, i):
        return pl.ds((c * (n_r // 2) + b * (UNROLL // 2) + i) * n_a, n_a)

    def begin_residual(b):
        t = SWEEPS
        for c in range(COMPS):
            for i in range(UNROLL // 2):
                two = jnp.zeros((n_a, n_o), jnp.float32)
                for j in (2 * i, 2 * i + 1):
                    r = b * UNROLL + j
                    tile, near = interior(t, r, c)
                    two = two + ((f[c, r] + near) + (radial(t, r, c, False) - diag[r] * tile))
                for k in range(reps):
                    pairs[k, pair_rows(c, b, i)] = two[:, k * LANES : (k + 1) * LANES]

    def residual(b):
        t = SWEEPS
        for c in range(COMPS):
            for i in range(UNROLL // 2):
                rows = [
                    sum(row_sum[t, s, b * UNROLL + j, 1 + c : 2 + c] for j in (2 * i, 2 * i + 1))
                    for s in both
                ]
                more = edge_rows(*rows) + (
                    ends_of(col_sum[t, b], lane_at(1 + c, 2 * i))
                    + ends_of(col_sum[t, b], lane_at(1 + c, 2 * i + 1))
                )
                for r in (b * UNROLL + 2 * i, b * UNROLL + 2 * i + 1):
                    if r in (0, n_r - 1):
                        more = more + radial(t, r, c, True)
                at = pair_rows(c, b, i)
                for k in range(reps):
                    pairs[k, at] = pairs[k, at] + more[:, k * LANES : (k + 1) * LANES]

    for b in reversed(range(blocks_r)):
        loaded(b)
        phase(functools.partial(pack_first, 0, b))
    pl.semaphore_wait(barrier, expected)
    for b in reversed(range(blocks_r)):
        start(0, b, True)
    for b in reversed(range(blocks_r)):
        loaded(b, True)
        phase(functools.partial(prepare, 0, b))
        start(0, b)
    load_ids.wait()

    near_devices = [({"lat": lat_to[s]}, lat_has[s], lat_has[1 - s]) for s in both] + [
        ({"lon": lon_to[q]}, None, None) for q in both
    ]

    def ids_copy(i):
        return Link(functools.partial(
            pltpu.make_async_remote_copy, ids, ids_near.at[i ^ 1], ids_send.at[i], ids_recv.at[i],
            device_id=near_devices[i][0], device_id_type=MESH,
        ))

    for i, (_, send, _) in enumerate(near_devices):
        guarded(send, ids_copy(i).start)

    def wave_signal(k):
        for s in both:
            def tell():
                pl.semaphore_signal(wave.at[k, s], inc=1, device_id={"lat": lat_to[s]}, device_id_type=MESH)
            pl.when(lat_has[s])(tell)

    def wave_wait(k):
        for s in both:
            def hear():
                pl.semaphore_wait(wave.at[k, s], 1)
            pl.when(lat_has[1 - s])(hear)

    waves = n_lat - 1 if direct else 0
    if waves:
        wave_signal(0)

    lat_cell = (me_lat * n_a + row).astype(jnp.float32)
    lon_cell = (me_lon * n_o + lane_wide).astype(jnp.float32)
    phi = math.pi * ((lat_cell + 0.5) / (n_lat * n_a) - 0.5)
    lam = (2.0 * math.pi) * (lon_cell[:1] + 0.5) / (n_lon * n_o)
    cos_lat = jnp.cos(phi)
    cos_lon, sin_lon = jnp.cos(lam), jnp.sin(lam)
    rx = cos_lat * cos_lon
    ry = cos_lat * sin_lon
    rz = jnp.sin(phi)
    blocks = ids.shape[1]
    bands = n_a // FACE
    spread_rows = lax.broadcasted_iota(jnp.int32, (blocks, n_o), 0)
    spread_cols = lax.broadcasted_iota(jnp.int32, (blocks, n_o), 1)
    spread = (spread_cols // FACE == spread_rows).astype(jnp.float32)
    numbers = lax.broadcasted_iota(jnp.int32, (SLOT, n_o), 0)

    def cells_of(line, chosen):
        own = jnp.broadcast_to(line.astype(jnp.float32), (8, blocks))
        return jnp.dot(own, chosen, precision=HIGHEST)[:1]

    def hot(line):
        return hot_of(cells_of(line, spread))

    def hot_of(cells):
        return (jnp.abs(cells - numbers.astype(jnp.float32)) < 0.5).astype(jnp.float32)

    onehots = [hot(ids[band : band + 1]) for band in range(bands)]

    pending = list(range(1, waves))

    def relay():
        if pending:
            k = pending.pop(0)
            wave_wait(k - 1)
            wave_signal(k)

    def s1_copy(step):
        return pltpu.make_async_remote_copy(
            stage_out.at[0], lat_sums.at[me_lat], s1_send.at[0], s1_recv.at[0],
            device_id={"lat": lax.rem(me_lat + step, n_lat)}, device_id_type=MESH,
        )

    here = me_lat * n_lon + me_lon if direct else me_lon
    group = n_lat * n_lon * n_rad if direct else n_lon * n_rad
    plane = n_lon * n_rad

    def s2_copy(step):
        device = {
            "lon": lax.rem(me_lon + (step % plane) // n_rad, n_lon),
            "rad": lax.rem(me_rad + step % n_rad, n_rad),
        }
        if direct:
            device["lat"] = lax.rem(me_lat + step // plane, n_lat)
        return pltpu.make_async_remote_copy(
            stage_out.at[1], sums.at[here], s2_send.at[0], s2_recv.at[0],
            device_id=device, device_id_type=MESH,
        )

    def cross(k, x, drag):
        return [
            (x[1] * drag[2] - x[2] * drag[1]) * k,
            (x[2] * drag[0] - x[0] * drag[2]) * k,
            (x[0] * drag[1] - x[1] * drag[0]) * k,
        ]

    def torques():
        top = n_r - 1
        guess = [
            [(1.0 - RELAX) * v[2][c, r + 1] + gain[r] * num[1, c, r] for c in range(COMPS)]
            for r in (top, top - 1)
        ]
        drag = [eta[n_r] * (guess[0][c] - guess[1][c]) for c in range(COMPS)]
        twist = cross(cos_lat, (rx, ry, rz), drag) + [cos_lat]
        outer = []
        for s in both:
            k = (me_lat * n_a + (n_a if s else -1)).astype(jnp.float32)
            tilt = math.pi * ((jnp.full((1, n_o), 0.5, jnp.float32) + k) / (n_lat * n_a) - 0.5)
            cos_tilt = jnp.cos(tilt)
            moved = [(row_g[s, r] * row_w[s, r]) * row_out[1, s, r] for r in (top, top - 1)]
            shift = row_in[0, s, top, :1] * (moved[0] - moved[1])
            push = [shift[1 + c : 2 + c] for c in range(COMPS)]
            outer.append(cross(cos_tilt, (cos_tilt * cos_lon, cos_tilt * sin_lon, jnp.sin(tilt)), push))
        moved = col_g[end] * col_w[end] * col_first[1, end]
        shift = repeat_first(col_far[0, end]) * (moved - turn(moved, 2 * FIELDS, 1))
        push = [ends_of(shift, lane_at(1 + c, UNROLL - 1)) for c in range(COMPS)]
        around = n_lon * n_o
        column = jnp.where(
            lane_wide[:1] == 0,
            lax.rem(me_lon * n_o + (around - 1), around), lax.rem(me_lon * n_o + n_o, around),
        ).astype(jnp.float32)
        angle = (2.0 * math.pi) * (column + 0.5) / around
        beside = cross(cos_lat, (cos_lat * jnp.cos(angle), cos_lat * jnp.sin(angle), rz), push)
        firsts = [(spread_rows == block).astype(jnp.float32) for block in (blocks - 1, 0)]
        packed = jnp.zeros((1, LANES), jnp.float32)
        for band in range(bands):
            cut = slice(band * FACE, (band + 1) * FACE)

            def stack(parts):
                return jnp.concatenate(
                    parts + [jnp.zeros((8 - len(parts), n_o), jnp.float32)], 0,
                )

            lines = [stack([jnp.sum(x[cut], axis=0, keepdims=True) for x in twist])]
            hots = [onehots[band]]
            lines.append(stack([jnp.sum(x[cut], axis=0, keepdims=True) for x in beside]))
            hots.append(hot_of(jnp.where(
                lane_wide[:1] == 0,
                cells_of(ids_near[2, band : band + 1], firsts[0]),
                cells_of(ids_near[3, band : band + 1], firsts[1]),
            )))
            for s in both:
                if band == (0, bands - 1)[s]:
                    lines.append(stack(outer[s]))
                    other = (bands - 1, 0)[s]
                    hots.append(hot(ids_near[s, other : other + 1]))
            totals = lax.dot_general(
                jnp.concatenate(lines, 1), jnp.concatenate(hots, 1), (((1,), (1,)), ((), ())),
                precision=HIGHEST, preferred_element_type=jnp.float32,
            )
            packed = packed + jnp.concatenate([totals[i : i + 1] for i in range(COMPS + 1)], 1)
        if direct:
            stage_out[1] = packed
            sums[here] = packed
            for step in range(1, group):
                s2_copy(step).start()
        else:
            stage_out[0] = packed
            lat_sums[me_lat] = packed
            for step in range(1, n_lat):
                s1_copy(step).start()

    def surface():
        while pending:
            relay()
        if waves:
            wave_wait(waves - 1)
        for i, (_, _, take) in enumerate(near_devices):
            guarded(take, ids_copy(i).wait_recv)
        pl.when(is_top)(torques)

    def advance(b):
        phase(functools.partial(prepare, 1, b))
        start(1, b)

    def ready(b, done):
        return all(k in done for k in (b - 1, b, b + 1) if 0 <= k <= end)

    def sweep(h, order, finish, ship):
        done, shipped = set(), set()

        def near_part(b):
            near_side(h, b)

        def main_part(b):
            advance_face(h, b)

        def far_part(b):
            far_cols(h, b)
            far_rows(h, b)

        arrive_planes(h)
        if h == 0:
            for p in both:
                pl.when(rad_has[p])(functools.partial(link_plane, p))
        for b in order:
            arrive(h, b)
            if b == order[0]:
                relay()
            phase(functools.partial(near_part, b))
            phase(functools.partial(main_part, b))
        if h == 1:
            for b in order:
                phase(functools.partial(begin_residual, b))
        arrive_far(h)
        for p in both:
            pl.when(rad_has[p])(functools.partial(update_plane, h, p))
        for at, b in enumerate(order):
            arrive_late(h, b)
            phase(functools.partial(far_part, b))
            for k in [b]:
                if k not in done:
                    phase(functools.partial(finish, k))
                    done.add(k)
                    if k == order[0]:
                        relay()
                    if ship:
                        if k == end:
                            sent(0)
                        phase(functools.partial(pack_first, 1, k))
                        start(1, k, True)
                    for m in [end, 0] + order:
                        if ship and m not in shipped and ready(m, done):
                            ship(m)
                            shipped.add(m)

    first_order = list(reversed(range(blocks_r)))
    second_order = [end] + list(reversed(range(2, end))) + [k for k in (0, 1) if k < end]

    def ship_off(b):
        advance(b)

    sweep(0, first_order, functools.partial(second_step, 1), ship_off)
    surface()

    if not direct:
        @pl.when(is_top)
        def _():
            await_thin(s1_recv.at[0], n_lat - 1)
            total = lat_sums[0]
            for i in range(1, n_lat):
                total = total + lat_sums[i]
            stage_out[1] = total
            sums[here] = total
            for step in range(1, group):
                s2_copy(step).start()

    sweep(1, second_order, residual, None)

    half = n_o // 2
    thin_r = lax.broadcasted_iota(jnp.int32, (LANES, half), 0)
    thin_c = lax.broadcasted_iota(jnp.int32, (LANES, half), 1)
    count = COMPS * (n_r // 2) * n_a // 2
    merged = jnp.zeros((count, half), jnp.float32)
    for h in range(reps):
        choose = jnp.where((thin_r + h * LANES) // 2 == thin_c, 0.125, 0.0).astype(jnp.bfloat16)
        summed = pairs[h, pl.ds(0, count, stride=2)] + pairs[h, pl.ds(1, count, stride=2)]
        big = summed.astype(jnp.bfloat16)
        small = (summed - big.astype(jnp.float32)).astype(jnp.bfloat16)
        merged = merged + (
            jnp.dot(big, choose, preferred_element_type=jnp.float32)
            + jnp.dot(small, choose, preferred_element_type=jnp.float32)
        )
    mine = count // COMPS
    spot = pl.ds(pl.multiple_of(me_rad * mine, mine), mine)
    for c in range(COMPS):
        coarse[c, spot] = merged[c * mine : (c + 1) * mine]

    def g_copy(step):
        return pltpu.make_async_remote_copy(
            coarse.at[:, spot], coarse.at[:, spot], g_send.at[step - 1], g_recv.at[me_rad],
            device_id={"rad": lax.rem(me_rad + step, n_rad)}, device_id_type=MESH,
        )

    for step in range(1, n_rad):
        g_copy(step).start()

    sources = n_lat * n_lon if direct else n_lon
    pl.when(is_top)(functools.partial(await_thin, s2_recv.at[0], sources - 1))
    pl.when(jnp.logical_not(is_top))(functools.partial(await_thin, s2_recv.at[0], sources))
    terms = [sums[i] for i in range(sources)]
    while len(terms) > 1:
        terms = [terms[i] + terms[i + 1] if i + 1 < len(terms) else terms[i] for i in range(0, len(terms), 2)]
    total = terms[0]
    area = total[:, COMPS * SLOT : (COMPS + 1) * SLOT]
    valid = lax.broadcasted_iota(jnp.int32, (1, SLOT), 1) < PLATES
    root = jnp.sqrt(jnp.where(valid, area, 1.0))
    turns = jnp.concatenate(
        [total[:, i * SLOT : (i + 1) * SLOT] / root for i in range(COMPS)]
        + [jnp.zeros((8 - COMPS, SLOT), jnp.float32)], 0,
    )
    for band in range(bands):
        cut = slice(band * FACE, (band + 1) * FACE)
        cell = jnp.dot(turns, onehots[band], precision=HIGHEST, preferred_element_type=jnp.float32)
        ox, oy, oz = (cell[i : i + 1] for i in range(COMPS))
        plate[0, cut] = oy * rz[cut] - oz * ry[cut]
        plate[1, cut] = oz * rx[cut] - ox * rz[cut]
        plate[2, cut] = ox * ry[cut] - oy * rx[cut]

    sent(1)
    for i, (_, send, _) in enumerate(near_devices):
        guarded(send, ids_copy(i).wait_send)

    @pl.when(is_top)
    def _():
        if not direct:
            await_thin(s1_send.at[0], n_lat - 1, True)
        await_thin(s2_send.at[0], group - 1, True)

    for step in range(1, n_rad):
        source = lax.rem(me_rad + step, n_rad)
        region = coarse.at[:, pl.ds(pl.multiple_of(source * mine, mine), mine)]
        pltpu.make_async_remote_copy(
            region, region, g_send.at[0], g_recv.at[source],
            device_id={"rad": source}, device_id_type=MESH,
        ).wait_recv()
        g_copy(step).wait_send()


def write_out(last, coarse, plate, new_v_out, coarse_out, plate_out, sem):
    n_r = new_v_out.shape[1]
    copies = [
        pltpu.make_async_copy(last.at[:, pl.ds(1, n_r)], new_v_out, sem.at[0]),
        pltpu.make_async_copy(coarse, coarse_out, sem.at[1]),
        pltpu.make_async_copy(plate, plate_out, sem.at[2]),
    ]
    for copy in copies:
        copy.start()
    for copy in copies:
        copy.wait()


def on_device(sizes, velocity, forcing, viscosity, plate_ids):
    n_lat, n_lon, n_rad = sizes
    _, n_r, n_a, n_o = velocity.shape
    chunks = n_r // UNROLL
    f32 = jnp.float32
    dma = pltpu.SemaphoreType.DMA
    direct = n_lat * n_lon * n_rad <= DIRECT
    group = n_lat * n_lon * n_rad if direct else n_lon * n_rad
    sources = n_lat * n_lon if direct else n_lon
    in_any = pl.BlockSpec(memory_space=pl.ANY)
    in_vmem = pl.BlockSpec(memory_space=pltpu.VMEM)
    coarse_rows = n_rad * (n_r // 2) * (n_a // 2)
    whole = (n_r, n_a, n_o)
    thin = (n_a, LANES)
    flat = (PACK, n_o)

    def vmem(*shape):
        return pltpu.VMEM(shape, f32)

    held = pl.pallas_call(
        functools.partial(kernel, sizes),
        out_shape=(
            pltpu.VMEM((COMPS, n_r + 2, n_a, n_o), f32),
            pltpu.VMEM((COMPS, coarse_rows, n_o // 2), f32),
            pltpu.VMEM((COMPS, n_a, n_o), f32),
        ),
        in_specs=[pl.BlockSpec(memory_space=pltpu.HBM)] * 4,
        out_specs=(in_vmem,) * 3,
        scratch_shapes=[
            vmem(SWEEPS, COMPS, n_r + 2, n_a, n_o),
            pltpu.VMEM(plate_ids.shape, jnp.int32),
            pltpu.VMEM((4,) + plate_ids.shape, jnp.int32),
            vmem(COMPS, *whole),
            vmem(n_r + 2, n_a, n_o),
            vmem(2, *whole),
            vmem(2, *whole),
            vmem(n_r + 1, n_a, n_o),
            vmem(*whole),
            vmem(*whole),
            vmem(*whole),
            vmem(2, COMPS, *whole),
            vmem(2, 2, n_r, *flat),
            vmem(2, 2, n_r, *flat),
            vmem(2, 2, n_r, *flat),
            vmem(2, 2, n_r, *flat),
            vmem(4, 2, n_r, *flat),
            vmem(2, n_r, *flat),
            vmem(2, n_r, *flat),
            vmem(2, n_r, *flat),
            vmem(2, 2, *flat),
            vmem(2, chunks, *thin),
            vmem(2, chunks, *thin),
            vmem(2, chunks, 2, 2, *thin),
            vmem(2, chunks, *thin),
            vmem(4, chunks, *thin),
            vmem(chunks, *thin),
            vmem(chunks, *thin),
            vmem(chunks, 2, *thin),
            vmem(2, *thin),
            vmem(2, 2, COMPS, n_a, n_o),
            vmem(2, n_a, n_o),
            vmem(2, n_a, n_o),
            vmem(2, n_a, n_o),
            vmem(2, n_a, n_o),
            vmem(2, chunks, 2, 1, LANES),
            vmem(2, chunks, 2, 2, 1, LANES),
            vmem(2, chunks, LANES, LANES),
            vmem(2, 2, 2, *flat),
            vmem(2, 2, 2, *flat),
            vmem(2, 2, 2, *thin),
            vmem(n_o // LANES, COMPS * (n_r // 2) * n_a, LANES),
            vmem(sources, 1, LANES),
            vmem(n_lat, 1, LANES),
            vmem(2, 1, LANES),
            vmem(max(7 * UNROLL * n_a, chunks * (UNROLL * FIELDS + 8)), 1, n_o),
            vmem(max(group, sources, n_lat), 1, LANES),
            dma((2 * chunks + 1,)),
            dma((1,)),
            dma((2,)),
            dma((2,)),
            dma((2,)),
            dma((2, 2)),
            dma((2, chunks)),
            dma((2, chunks, 2)),
            dma((1,)),
            dma((2,)),
            dma((2, chunks)),
            dma((2, chunks, 2)),
            dma((2, 2)),
            dma((2, 2)),
            dma((2, 2, 2)),
            dma((2,)),
            dma((2, 2)),
            dma((4,)),
            dma((4,)),
            pltpu.SemaphoreType.REGULAR((n_lat - 1 if direct else 1, 2)),
            dma((1,)),
            dma((1,)),
            dma((1,)),
            dma((1,)),
            dma((n_rad,)),
            dma((n_rad,)),
        ],
        compiler_params=pltpu.CompilerParams(
            collective_id=0, has_side_effects=True, vmem_limit_bytes=32 * 2**20
        ),
    )(*(
        pltpu.with_memory_space_constraint(x, pltpu.HBM)
        for x in (velocity, forcing, viscosity, plate_ids)
    ))
    new_v, coarse, plate = pl.pallas_call(
        write_out,
        out_shape=(
            jax.ShapeDtypeStruct(velocity.shape, f32),
            jax.ShapeDtypeStruct((COMPS, coarse_rows, n_o // 2), f32),
            jax.ShapeDtypeStruct((COMPS, n_a, n_o), f32),
        ),
        in_specs=[in_vmem] * 3,
        out_specs=(in_any,) * 3,
        scratch_shapes=[dma((3,))],
        compiler_params=pltpu.CompilerParams(vmem_limit_bytes=4 * 2**20),
    )(*(pltpu.with_memory_space_constraint(x, pltpu.VMEM) for x in held))
    coarse = coarse.reshape(COMPS, n_rad * (n_r // 2), n_a // 2, n_o // 2)
    return new_v, coarse, plate


def solution(mesh):
    sizes = tuple(mesh.shape[a] for a in ("lat", "lon", "rad"))
    field = P(None, "rad", "lat", "lon")
    return jax.shard_map(
        functools.partial(on_device, sizes),
        mesh=mesh,
        in_specs=(field, field, P("rad", "lat", "lon"), P("lat", "lon")),
        out_specs=(field, P(None, None, "lat", "lon"), P(None, "lat", "lon")),
        check_vma=False,
    )
```

```python
import functools
import math

import jax
import jax.numpy as jnp
from jax import lax
from jax.experimental import pallas as pl
from jax.experimental.pallas import tpu as pltpu
from jax.sharding import PartitionSpec as P

SWEEPS = 3
PLATES = 12
FACE = 8
RELAX = 0.8
COMPS = 3
LANES = 128
SLOT = 32
MESH = pl.DeviceIdType.MESH
HIGHEST = lax.Precision.HIGHEST
UNROLL = 8
DIRECT = 64
FIELDS = 2 * (COMPS + 1)
PACK = COMPS + 1


def harmonic(own, other):
    return 2.0 * own * other / (own + other)


def harmonic0(own, other):
    return 2.0 * own * other / jnp.maximum(own + other, 1e-30)


class Link:
    def __init__(self, make):
        self.make = make

    def start(self):
        self.make().start()

    def wait_send(self):
        self.make().wait_send()

    def wait_recv(self):
        self.make().wait_recv()


def kernel(
    sizes, vel, forc, visc, ids_in,
    last, coarse, plate,
    early, ids, ids_near, f, eta, w_lat, w_lon, w_rad, gain, diag, part, num,
    row_out, row_in, more_out, more_in, row_sum, row_w, row_g, row_q, row_p,
    col_first, col_out, col_in, col_far, col_sum, col_w, col_g, col_d, col_p,
    plane_num, plane_d, plane_g, plane_l, plane_q,
    corner_out, corner_in, corner_t, edge_out, edge_in, side_in,
    pairs, sums, lat_sums, stage_out, tally, tally_thin,
    load_sem, lon_send, lat_send, rad_send, num_send, edge_send, lon_recv, lat_recv, late_lon_send, late_lat_send, late_lon_recv, late_lat_recv, rad_recv, num_recv, edge_recv, far_send, far_recv,
    ids_send, ids_recv, wave, misc,
):
    n_lat, n_lon, n_rad = sizes
    g_send, g_recv, s2_send, s2_recv = misc.at[0:1], misc.at[1:2], misc.at[2], misc.at[3]
    n_r, n_a, n_o = visc.shape
    me_lat, me_lon, me_rad = (lax.axis_index(a) for a in ("lat", "lon", "rad"))
    lat_has = (me_lat > 0, me_lat < n_lat - 1)
    rad_has = (me_rad > 0, me_rad < n_rad - 1)
    lat_to = (me_lat - 1, me_lat + 1)
    rad_to = (me_rad - 1, me_rad + 1)
    lon_to = (lax.rem(me_lon + n_lon - 1, n_lon), lax.rem(me_lon + 1, n_lon))
    is_top = me_rad == n_rad - 1
    direct = n_lat * n_lon * n_rad <= DIRECT
    s1_send, s1_recv = (None, None) if direct else (misc.at[4], misc.at[5])
    v = [early.at[t] for t in range(SWEEPS)] + [last]
    blocks_r = n_r // UNROLL
    end = blocks_r - 1
    both = (0, 1)

    def guarded(cond, call):
        if cond is None:
            call()
        else:
            pl.when(cond)(call)

    def all_of(*conds):
        conds = [c for c in conds if c is not None]
        return functools.reduce(jnp.logical_and, conds)

    barrier = pltpu.get_barrier_semaphore()

    def greet(device):
        pl.semaphore_signal(barrier, inc=1, device_id=device, device_id_type=MESH)

    expected = n_lon * n_rad - 1
    for step in range(1, n_lon * n_rad):
        greet({
            "lon": lax.rem(me_lon + step // n_rad, n_lon),
            "rad": lax.rem(me_rad + step % n_rad, n_rad),
        })
    for s in both:
        if direct:
            pl.when(lat_has[s])(functools.partial(greet, {"lat": lat_to[s]}))
            expected = expected + jnp.where(lat_has[s], 1, 0)
        for q in both:
            pl.when(lat_has[s])(functools.partial(greet, {"lat": lat_to[s], "lon": lon_to[q]}))
            expected = expected + jnp.where(lat_has[s], 1, 0)
        for p in both:
            has = all_of(lat_has[s], rad_has[p])
            pl.when(has)(functools.partial(greet, {"lat": lat_to[s], "rad": rad_to[p]}))
            expected = expected + jnp.where(has, 1, 0)
    if not direct:
        for step in range(1, n_lat):
            greet({"lat": lax.rem(me_lat + step, n_lat)})
        expected = expected + (n_lat - 1)

    def load_chunk(b, rest):
        here_r = pl.ds(b * UNROLL, UNROLL)
        inner = pl.ds(1 + b * UNROLL, UNROLL)
        if rest:
            return [pltpu.make_async_copy(forc.at[:, here_r], f.at[:, here_r], load_sem.at[blocks_r])]
        return [
            pltpu.make_async_copy(visc.at[here_r], eta.at[inner], load_sem.at[b]),
            pltpu.make_async_copy(vel.at[:, here_r], v[0].at[:, inner], load_sem.at[b]),
        ]

    for rest in (False, True):
        for b in reversed(range(blocks_r)):
            for load in load_chunk(b, rest):
                load.start()
    load_ids = pltpu.make_async_copy(ids_in, ids, load_sem.at[blocks_r + 1])
    load_ids.start()

    def rows_of(ref):
        return ref.size // n_o

    def await_rows(sem, rows, sending=False):
        some = tally.at[pl.ds(0, rows)]
        copy = pltpu.make_async_remote_copy(
            some, some, sem, sem, device_id={"lon": lon_to[1]}, device_id_type=MESH,
        )
        copy.wait_send() if sending else copy.wait_recv()

    def await_thin(sem, rows, sending=False):
        some = tally_thin.at[pl.ds(0, rows)]
        copy = pltpu.make_async_remote_copy(
            some, some, sem, sem, device_id={"lon": lon_to[1]}, device_id_type=MESH,
        )
        copy.wait_send() if sending else copy.wait_recv()

    def loaded(b):
        some = tally.at[pl.ds(0, (COMPS + 1) * UNROLL * n_a)]
        pltpu.make_async_copy(some, some, load_sem.at[b]).wait()

    def forcing_loaded():
        pltpu.make_async_copy(f, f, load_sem.at[blocks_r]).wait()

    lane_wide = lax.broadcasted_iota(jnp.int32, (n_a, n_o), 1)
    lane = lax.broadcasted_iota(jnp.int32, (n_a, LANES), 1)
    row = lax.broadcasted_iota(jnp.int32, (n_a, n_o), 0)
    row_thin = lax.broadcasted_iota(jnp.int32, (n_a, LANES), 0)
    even = lane % 2 == 0
    field_of = (lane + 1) % LANES // 2 % FIELDS
    layer_of = (lane + 1) % LANES // (2 * FIELDS)
    reps = n_o // LANES
    row_edge = (0, n_a - 1)
    lane_edge = (0, n_o - 1)
    thin_edge = (0, LANES - 1)

    plane_rows = n_a
    tile_rows = n_a * LANES // n_o

    def phase(call):
        pl.when(me_lat >= 0)(call)

    for p, slot, face in ((0, 0, 0), (1, n_r + 1, n_r)):
        @pl.when(jnp.logical_not(rad_has[p]))
        def _():
            zero_plane = jnp.zeros((n_a, n_o), jnp.float32)
            w_rad[face] = zero_plane
            for t in range(SWEEPS + 1):
                for c in range(COMPS):
                    v[t][c, slot] = zero_plane
            for h in both:
                for s in both:
                    edge_in[h, s, p] = jnp.zeros((PACK, n_o), jnp.float32)
                    side_in[h, p, s] = jnp.zeros((n_a, LANES), jnp.float32)
    for s in both:
        @pl.when(jnp.logical_not(lat_has[s]))
        def _():
            blank_rows = jnp.zeros((PACK, n_o), jnp.float32)
            for h in both:
                for r in range(n_r):
                    row_in[h, s, r] = blank_rows
                    more_in[h, s, r] = blank_rows + 1.0
                for b in range(blocks_r):
                    for q in both:
                        corner_in[h, b, s, q] = jnp.zeros((1, LANES), jnp.float32)
                for p in both:
                    edge_in[h, s, p] = blank_rows
            ids_near[s] = jnp.zeros(ids.shape, jnp.int32)

    def messages(h, b, early_part):
        t = 2 * h
        table = []

        def add(src, dst, sends, takes, device, cond):
            table.append((Link(functools.partial(
                pltpu.make_async_remote_copy, src, dst, sends, takes,
                device_id=device, device_id_type=MESH,
            )), cond))

        for p, layer, slot in ((0, 1, n_r + 1), (1, n_r, 0)):
            if p not in near_planes(b):
                continue
            device = {"rad": rad_to[p]}
            if early_part:
                sems = (rad_send.at[p], rad_recv.at[h, 1 - p])
                add(v[t].at[:, layer], v[t].at[:, slot], *sems, device, rad_has[p])
                if h == 0:
                    add(eta.at[layer], eta.at[slot], *sems, device, rad_has[p])
            sems = (num_send.at[p], num_recv.at[h, 1 - p])
            if early_part:
                for q in both:
                    add(
                        col_first.at[h, b], side_in.at[h, 1 - p, 1 - q], *sems,
                        {"lon": lon_to[q], "rad": rad_to[p]}, rad_has[p],
                    )
                for s in both:
                    add(
                        edge_out.at[h, s, p], edge_in.at[h, 1 - s, 1 - p],
                        edge_send.at[s, p], edge_recv.at[h, 1 - s, 1 - p],
                        {"lat": lat_to[s], "rad": rad_to[p]}, all_of(rad_has[p], lat_has[s]),
                    )
            else:
                add(num.at[h, :, layer - 1], plane_num.at[h, 1 - p], *sems, device, rad_has[p])
                if h == 0:
                    add(part.at[layer - 1], plane_d.at[1 - p], *sems, device, rad_has[p])
        layers = pl.ds(b * UNROLL, UNROLL)
        columns, rows, rows_at = (col_first, row_out, row_in) if early_part else (col_out, more_out, more_in)
        lon_sems = (lon_send, lon_recv) if early_part else (late_lon_send, late_lon_recv)
        which = (h, b) if early_part else (h,)
        lat_sems = (lat_send, lat_recv) if early_part else (late_lat_send, late_lat_recv)
        if early_part:
            for s in both:
                for q in both:
                    add(
                        corner_out.at[h, b, s], corner_in.at[h, b, 1 - s, 1 - q],
                        far_send.at[s], far_recv.at[h, 1 - s],
                        {"lat": lat_to[s], "lon": lon_to[q]}, lat_has[s],
                    )
        for q in both:
            add(
                columns.at[h, b], col_in.at[h, b, 0 if early_part else 1, 1 - q],
                lon_sems[0].at[0], lon_sems[1].at[*which], {"lon": lon_to[q]}, None,
            )
        for s in both:
            add(
                rows.at[h, s, layers], rows_at.at[h, 1 - s, layers],
                lat_sems[0].at[s], lat_sems[1].at[*which, 1 - s], {"lat": lat_to[s]}, lat_has[s],
            )
        return table

    corner_rows = 2 * LANES // n_o
    lat_rows = UNROLL * PACK

    def rad_rows(h):
        return (COMPS + (1 if h == 0 else 0)) * n_a

    def num_rows(h):
        return rad_rows(h) + 2 * tile_rows

    def start(h, b, early_part=False):
        for copy, cond in messages(h, b, early_part):
            guarded(cond, copy.start)

    def near_planes(b):
        return [p for p, at in ((0, 0), (1, end)) if b == at]

    def arrive(h, b):
        await_rows(lon_recv.at[h, b], 2 * tile_rows)
        for s in both:
            guarded(lat_has[s], functools.partial(await_rows, lat_recv.at[h, b, s], lat_rows))

    def arrive_late(h):
        await_rows(late_lon_recv.at[h], blocks_r * 2 * tile_rows)
        for s in both:
            guarded(
                lat_has[s], functools.partial(await_rows, late_lat_recv.at[h, s], blocks_r * lat_rows),
            )

    def arrive_planes(h):
        for p in both:
            guarded(rad_has[p], functools.partial(await_rows, rad_recv.at[h, p], rad_rows(h)))

    def arrive_far(h):
        for p in both:
            guarded(rad_has[p], functools.partial(await_rows, num_recv.at[h, p], num_rows(h)))
        for s in both:
            for p in both:
                guarded(
                    all_of(rad_has[p], lat_has[s]),
                    functools.partial(await_rows, edge_recv.at[h, s, p], PACK),
                )
            guarded(
                lat_has[s],
                functools.partial(await_rows, far_recv.at[h, s], blocks_r * corner_rows),
            )

    def sent(h):
        for p in both:
            guarded(rad_has[p], functools.partial(await_rows, rad_send.at[p], rad_rows(h), True))
            guarded(rad_has[p], functools.partial(await_rows, num_send.at[p], num_rows(h), True))
            for s in both:
                guarded(
                    all_of(rad_has[p], lat_has[s]),
                    functools.partial(await_rows, edge_send.at[s, p], PACK, True),
                )
        await_rows(lon_send.at[0], blocks_r * 2 * tile_rows, True)
        await_rows(late_lon_send.at[0], blocks_r * 2 * tile_rows, True)
        for s in both:
            for sem in (lat_send, late_lat_send):
                guarded(lat_has[s], functools.partial(await_rows, sem.at[s], blocks_r * lat_rows, True))
            guarded(lat_has[s], functools.partial(await_rows, far_send.at[s], blocks_r * corner_rows, True))

    def turn(x, shift, axis):
        shift = shift % x.shape[axis]
        return pltpu.roll(x, shift, axis) if shift else x

    def interior(t, r, c):
        tile = v[t][c, r + 1]
        return tile, (
            (w_lat[0, r] * turn(tile, 1, 0) + w_lat[1, r] * turn(tile, -1, 0))
            + (w_lon[0, r] * turn(tile, 1, 1) + w_lon[1, r] * turn(tile, -1, 1))
        )

    def radial(t, r, c, seams):
        total = None
        for face, slot in ((r, r), (r + 1, r + 2)):
            if (slot in (0, n_r + 1)) == seams or (seams is None):
                term = w_rad[face] * v[t][c, slot]
                total = term if total is None else total + term
        return total

    def lane_at(g, j):
        return 2 * (j * FIELDS + g)

    def ends_of(x, k):
        x = turn(x, -k, 1)
        west = jnp.where(lane == 0, x, 0.0)
        east = jnp.where(lane == LANES - 1, x, 0.0)
        if reps == 1:
            return west + east
        gap = [jnp.zeros((n_a, LANES), jnp.float32)] * (reps - 2)
        return jnp.concatenate([west] + gap + [east], 1)

    def edge_rows(low, high):
        return jnp.where(row == 0, low, jnp.where(row == n_a - 1, high, 0.0))

    def seams(t, b, j, c):
        r = b * UNROLL + j
        low, high = (row_sum[t, s, r, 1 + c : 2 + c] for s in both)
        return edge_rows(low, high) + ends_of(col_sum[t, b], lane_at(1 + c, j))

    def pack(h, r, k, tile, packed, rows):
        for i in range(reps):
            piece = slice(i * LANES, (i + 1) * LANES)
            rows[h, 0, r, k : k + 1, piece] = tile[:1, piece]
            rows[h, 1, r, k : k + 1, piece] = tile[n_a - 1 :, piece]
        at = lane_at(k, r % UNROLL)
        two = jnp.where(lane < LANES // 2, tile[:, :LANES], tile[:, n_o - LANES :])
        hit = jnp.logical_and(field_of == k, layer_of == r % UNROLL)
        return jnp.where(hit, turn(two, at, 1), packed)

    def pack_first(h, b):
        t = 2 * h
        packed = jnp.zeros((n_a, LANES), jnp.float32)
        for j in range(UNROLL):
            r = b * UNROLL + j
            tiles = [(1 + c, v[t][c, r + 1]) for c in range(COMPS)]
            if h == 0:
                tiles.append((0, eta[r + 1]))
            for k, tile in tiles:
                packed = pack(h, r, k, tile, packed, row_out)
                for p, layer in ((0, 0), (1, n_r - 1)):
                    if r == layer:
                        for s in both:
                            for i in range(reps):
                                piece = slice(i * LANES, (i + 1) * LANES)
                                edge_out[h, s, p, k : k + 1, piece] = tile[row_edge[s] : row_edge[s] + 1, piece]
        col_first[h, b] = packed
        for s in both:
            corner_out[h, b, s] = packed[row_edge[s] : row_edge[s] + 1]

    def prepare(h, b):
        t = 2 * h
        packed = jnp.zeros((n_a, LANES), jnp.float32)
        for j in range(UNROLL):
            r = b * UNROLL + j
            if h == 0:
                own = eta[r + 1]
                below = jnp.where(row == 0, 0.0, harmonic(own, turn(own, 1, 0)))
                above = jnp.where(row == n_a - 1, 0.0, turn(below, -1, 0))
                west = jnp.where(lane_wide == 0, 0.0, harmonic(own, turn(own, 1, 1)))
                east = jnp.where(lane_wide == n_o - 1, 0.0, turn(west, -1, 1))
                w_lat[0, r] = below
                w_lat[1, r] = above
                w_lon[0, r] = west
                w_lon[1, r] = east
                d = 0.5 * own + (below + above) + (west + east)
                if r > 0:
                    down = harmonic(own, eta[r])
                    w_rad[r] = down
                    d = d + down
                if r < n_r - 1:
                    d = d + harmonic(own, eta[r + 2])
                part[r] = d
                packed = pack(h, r, 0, d, packed, more_out)
        for j in range(UNROLL):
            r = b * UNROLL + j
            for c in range(COMPS):
                tile, near = interior(t, r, c)
                if h == 0:
                    total = f[c, r] + near
                    if r > 0:
                        total = total + w_rad[r] * v[t][c, r]
                    if r < n_r - 1:
                        up = w_rad[r + 1] if j < UNROLL - 1 else harmonic(eta[r + 1], eta[r + 2])
                        total = total + up * v[t][c, r + 2]
                else:
                    total = f[c, r] + (near + radial(t, r, c, False))
                num[h, c, r] = total
                packed = pack(h, r, 1 + c, total, packed, more_out)
        col_out[h, b] = packed

    def repeat_from(x, field, shifts):
        fields = field_of if x.shape[0] == n_a else field_of[:1]
        only = jnp.where(fields == field, x, 0.0)
        return functools.reduce(jnp.add, [turn(only, 2 * k, 1) for k in shifts])

    def repeat_first(x):
        return repeat_from(x, 0, range(COMPS + 1))

    def joined(from_west, from_east):
        at = even if from_west.shape[0] == n_a else even[:1]
        return jnp.where(at, turn(from_west, 1, 1), turn(from_east, -1, 1))

    def near_side(h, b):
        t = 2 * h
        far = joined(col_in[h, b, 0, 0], col_in[h, b, 0, 1])
        col_far[h, b] = far
        if h == 0:
            w = harmonic0(repeat_first(far), repeat_first(col_first[h, b]))
            col_w[b] = w
        else:
            w = col_w[b]
        col_sum[t, b] = w * far
        for s in both:
            for r in range(b * UNROLL, (b + 1) * UNROLL):
                if h == 0:
                    w = harmonic(
                        jnp.broadcast_to(row_in[h, s, r, :1], (PACK, n_o)),
                        jnp.broadcast_to(row_out[h, s, r, :1], (PACK, n_o)),
                    )
                    row_w[s, r] = w
                else:
                    w = row_w[s, r]
                row_sum[t, s, r] = w * row_in[h, s, r]

    def far_rows(h, b):
        t = 2 * h
        for s in both:
            for j in range(UNROLL):
                r = b * UNROLL + j
                far = row_in[h, s, r]
                column = corner_t[h, b, pl.ds(lane_at(0, j), FIELDS, stride=2), :]
                corner = ends_of(column, 2 * s + 1)[:PACK]
                near = [p for p, layer in ((0, 0), (1, n_r - 1)) if r == layer]
                w = row_w[s, r]
                if h == 0:
                    far_eta = jnp.broadcast_to(row_in[h, s, r, :1], (PACK, n_o))
                    wq = harmonic0(far_eta, corner[:1])
                    d = more_in[h, s, r, :1] + (w + wq)
                    for p in near:
                        wp = harmonic0(far_eta, edge_in[h, s, p, :1])
                        row_p[s, p] = wp
                        d = d + wp
                    row_q[s, r] = wq
                    gain_far = RELAX / d
                    row_g[s, r] = gain_far
                else:
                    wq, gain_far = row_q[s, r], row_g[s, r]
                total = more_in[h, s, r] + w * row_out[h, s, r] + wq * corner
                for p in near:
                    total = total + row_p[s, p] * edge_in[h, s, p]
                row_sum[t + 1, s, r] = w * ((1.0 - RELAX) * far + gain_far * total)

    def side_of(h, p):
        return joined(side_in[h, p, 0], side_in[h, p, 1])

    def far_cols(h, b):
        t = 2 * h
        far = col_far[h, b]
        own = col_first[h, b]
        more = joined(col_in[h, b, 1, 0], col_in[h, b, 1, 1])
        stacked = jnp.zeros((8, LANES), jnp.float32)
        spot = lax.broadcasted_iota(jnp.int32, (8, LANES), 0)
        for s in both:
            stacked = jnp.where(spot == 2 * s + 1, turn(corner_in[h, b, s, 0], 1, 1), stacked)
            stacked = jnp.where(spot == 2 * s, corner_in[h, b, s, 1], stacked)
        corner_t[h, b, :, :8] = stacked.T
        corners = [joined(corner_in[h, b, s, 0], corner_in[h, b, s, 1]) for s in both]
        move = 2 * FIELDS * (UNROLL - 1)
        sides = {p: turn(side_of(h, p), -move if p == 0 else move, 1) for p in near_planes(b)}
        w = col_w[b]
        if h == 0:
            far_eta = repeat_first(far)
            d = repeat_first(more) + w
            for s in both:
                wd = jnp.where(
                    row_thin == row_edge[s], harmonic0(far_eta, repeat_first(corners[s])), 0.0,
                )
                col_d[b, s] = wd
                d = d + wd
            for p in near_planes(b):
                wp = jnp.where(
                    layer_of == (0, UNROLL - 1)[p], harmonic0(far_eta, repeat_first(sides[p])), 0.0,
                )
                col_p[p] = wp
                d = d + wp
            col_g[b] = RELAX / jnp.where(d > 0.0, d, 1.0)
        total = more + w * own
        for s in both:
            total = total + col_d[b, s] * corners[s]
        for p in near_planes(b):
            total = total + col_p[p] * sides[p]
        col_sum[t + 1, b] = w * ((1.0 - RELAX) * far + col_g[b] * total)

    def link_plane(p):
        slot, layer, face = ((0, 1, 0), (n_r + 1, n_r, n_r))[p]
        w_rad[face] = harmonic(eta[slot], eta[layer])

    def update_plane(h, p):
        t = 2 * h
        slot, layer, face, j = ((0, 1, 0, UNROLL - 1), (n_r + 1, n_r, n_r, 0))[p]
        side = side_of(h, p)
        if h == 0:
            own = eta[slot]
            w = w_rad[face]
            wq = harmonic0(own, ends_of(side, lane_at(0, j)))
            plane_q[p] = wq
            d = plane_d[p] + (w + wq)
            wl = edge_rows(*(harmonic0(own, edge_in[h, s, p, :1]) for s in both))
            plane_l[p] = wl
            plane_g[p] = RELAX / (d + wl)
        for c in range(COMPS):
            total = plane_num[h, p, c] + w_rad[face] * v[t][c, layer]
            total = total + plane_l[p] * edge_rows(*(edge_in[h, s, p, 1 + c : 2 + c] for s in both))
            total = total + plane_q[p] * ends_of(side, lane_at(1 + c, j))
            v[t + 1][c, slot] = (1.0 - RELAX) * v[t][c, slot] + plane_g[p] * total

    def settle(b):
        for j in range(UNROLL):
            r = b * UNROLL + j
            low, high = (row_w[s, r, :1] for s in both)
            d = part[r] + (edge_rows(low, high) + ends_of(col_w[b], lane_at(0, j)))
            if r == 0:
                d = d + w_rad[0]
            if r == n_r - 1:
                d = d + w_rad[n_r]
            diag[r] = d
            gain[r] = RELAX / d

    def advance_face(h, b):
        t = 2 * h
        if h == 0:
            settle(b)
        for c in range(COMPS):
            for j in range(UNROLL):
                r = b * UNROLL + j
                total = num[h, c, r] + seams(t, b, j, c)
                if r in (0, n_r - 1):
                    total = total + radial(t, r, c, True)
                v[t + 1][c, r + 1] = (1.0 - RELAX) * v[t][c, r + 1] + gain[r] * total

    def begin_second(b):
        for c in range(COMPS):
            for j in range(UNROLL):
                r = b * UNROLL + j
                _, near = interior(1, r, c)
                num[1, c, r] = f[c, r] + (near + radial(1, r, c, False))

    def second_step(b):
        for c in range(COMPS):
            for j in range(UNROLL):
                r = b * UNROLL + j
                total = num[1, c, r] + seams(1, b, j, c)
                if r in (0, n_r - 1):
                    total = total + radial(1, r, c, True)
                v[2][c, r + 1] = (1.0 - RELAX) * v[1][c, r + 1] + gain[r] * total

    def pair_rows(c, b, i):
        return pl.ds((c * (n_r // 2) + b * (UNROLL // 2) + i) * n_a, n_a)

    def begin_residual(b):
        t = SWEEPS
        for c in range(COMPS):
            for i in range(UNROLL // 2):
                two = jnp.zeros((n_a, n_o), jnp.float32)
                for j in (2 * i, 2 * i + 1):
                    r = b * UNROLL + j
                    tile, near = interior(t, r, c)
                    two = two + ((f[c, r] + near) + (radial(t, r, c, False) - diag[r] * tile))
                for k in range(reps):
                    pairs[k, pair_rows(c, b, i)] = two[:, k * LANES : (k + 1) * LANES]

    def residual(b):
        t = SWEEPS
        for c in range(COMPS):
            for i in range(UNROLL // 2):
                rows = [
                    sum(row_sum[t, s, b * UNROLL + j, 1 + c : 2 + c] for j in (2 * i, 2 * i + 1))
                    for s in both
                ]
                more = edge_rows(*rows) + (
                    ends_of(col_sum[t, b], lane_at(1 + c, 2 * i))
                    + ends_of(col_sum[t, b], lane_at(1 + c, 2 * i + 1))
                )
                for r in (b * UNROLL + 2 * i, b * UNROLL + 2 * i + 1):
                    if r in (0, n_r - 1):
                        more = more + radial(t, r, c, True)
                at = pair_rows(c, b, i)
                for k in range(reps):
                    pairs[k, at] = pairs[k, at] + more[:, k * LANES : (k + 1) * LANES]

    for b in reversed(range(blocks_r)):
        loaded(b)
        phase(functools.partial(pack_first, 0, b))
    pl.semaphore_wait(barrier, expected)
    for b in reversed(range(blocks_r)):
        start(0, b, True)
    forcing_loaded()
    for b in reversed(range(blocks_r)):
        phase(functools.partial(prepare, 0, b))
        start(0, b)
    load_ids.wait()

    near_devices = [({"lat": lat_to[s]}, lat_has[s], lat_has[1 - s]) for s in both] + [
        ({"lon": lon_to[q]}, None, None) for q in both
    ]

    def ids_copy(i):
        return Link(functools.partial(
            pltpu.make_async_remote_copy, ids, ids_near.at[i ^ 1], ids_send.at[i], ids_recv.at[i],
            device_id=near_devices[i][0], device_id_type=MESH,
        ))

    for i, (_, send, _) in enumerate(near_devices):
        guarded(send, ids_copy(i).start)

    def wave_signal(k):
        for s in both:
            def tell():
                pl.semaphore_signal(wave.at[k, s], inc=1, device_id={"lat": lat_to[s]}, device_id_type=MESH)
            pl.when(lat_has[s])(tell)

    def wave_wait(k):
        for s in both:
            def hear():
                pl.semaphore_wait(wave.at[k, s], 1)
            pl.when(lat_has[1 - s])(hear)

    waves = n_lat - 1 if direct else 0
    if waves:
        wave_signal(0)

    lat_cell = (me_lat * n_a + row).astype(jnp.float32)
    lon_cell = (me_lon * n_o + lane_wide).astype(jnp.float32)
    phi = math.pi * ((lat_cell + 0.5) / (n_lat * n_a) - 0.5)
    lam = (2.0 * math.pi) * (lon_cell[:1] + 0.5) / (n_lon * n_o)
    cos_lat = jnp.cos(phi)
    cos_lon, sin_lon = jnp.cos(lam), jnp.sin(lam)
    rx = cos_lat * cos_lon
    ry = cos_lat * sin_lon
    rz = jnp.sin(phi)
    blocks = ids.shape[1]
    bands = n_a // FACE
    spread_rows = lax.broadcasted_iota(jnp.int32, (blocks, n_o), 0)
    spread_cols = lax.broadcasted_iota(jnp.int32, (blocks, n_o), 1)
    spread = (spread_cols // FACE == spread_rows).astype(jnp.float32)
    numbers = lax.broadcasted_iota(jnp.int32, (SLOT, n_o), 0)

    def cells_of(line, chosen):
        own = jnp.broadcast_to(line.astype(jnp.float32), (8, blocks))
        return jnp.dot(own, chosen, precision=HIGHEST)[:1]

    def hot(line):
        return hot_of(cells_of(line, spread))

    def hot_of(cells):
        return (jnp.abs(cells - numbers.astype(jnp.float32)) < 0.5).astype(jnp.float32)

    onehots = [hot(ids[band : band + 1]) for band in range(bands)]

    pending = list(range(1, waves))

    def relay():
        if pending:
            k = pending.pop(0)
            wave_wait(k - 1)
            wave_signal(k)

    def s1_copy(step):
        return pltpu.make_async_remote_copy(
            stage_out.at[0], lat_sums.at[me_lat], s1_send, s1_recv,
            device_id={"lat": lax.rem(me_lat + step, n_lat)}, device_id_type=MESH,
        )

    here = me_lat * n_lon + me_lon if direct else me_lon
    group = n_lat * n_lon * n_rad if direct else n_lon * n_rad
    plane = n_lon * n_rad

    def s2_copy(step):
        device = {
            "lon": lax.rem(me_lon + (step % plane) // n_rad, n_lon),
            "rad": lax.rem(me_rad + step % n_rad, n_rad),
        }
        if direct:
            device["lat"] = lax.rem(me_lat + step // plane, n_lat)
        return pltpu.make_async_remote_copy(
            stage_out.at[1], sums.at[here], s2_send, s2_recv,
            device_id=device, device_id_type=MESH,
        )

    def cross(k, x, drag):
        return [
            (x[1] * drag[2] - x[2] * drag[1]) * k,
            (x[2] * drag[0] - x[0] * drag[2]) * k,
            (x[0] * drag[1] - x[1] * drag[0]) * k,
        ]

    def torques():
        top = n_r - 1
        guess = [
            [(1.0 - RELAX) * v[2][c, r + 1] + gain[r] * num[1, c, r] for c in range(COMPS)]
            for r in (top, top - 1)
        ]
        drag = [eta[n_r] * (guess[0][c] - guess[1][c]) for c in range(COMPS)]
        twist = cross(cos_lat, (rx, ry, rz), drag) + [cos_lat]
        outer = []
        for s in both:
            k = (me_lat * n_a + (n_a if s else -1)).astype(jnp.float32)
            tilt = math.pi * ((jnp.full((1, n_o), 0.5, jnp.float32) + k) / (n_lat * n_a) - 0.5)
            cos_tilt = jnp.cos(tilt)
            moved = [(row_g[s, r] * row_w[s, r]) * row_out[1, s, r] for r in (top, top - 1)]
            shift = row_in[0, s, top, :1] * (moved[0] - moved[1])
            push = [shift[1 + c : 2 + c] for c in range(COMPS)]
            outer.append(cross(cos_tilt, (cos_tilt * cos_lon, cos_tilt * sin_lon, jnp.sin(tilt)), push))
        moved = col_g[end] * col_w[end] * col_first[1, end]
        shift = repeat_first(col_far[0, end]) * (moved - turn(moved, 2 * FIELDS, 1))
        push = [ends_of(shift, lane_at(1 + c, UNROLL - 1)) for c in range(COMPS)]
        around = n_lon * n_o
        column = jnp.where(
            lane_wide[:1] == 0,
            lax.rem(me_lon * n_o + (around - 1), around), lax.rem(me_lon * n_o + n_o, around),
        ).astype(jnp.float32)
        angle = (2.0 * math.pi) * (column + 0.5) / around
        beside = cross(cos_lat, (cos_lat * jnp.cos(angle), cos_lat * jnp.sin(angle), rz), push)
        firsts = [(spread_rows == block).astype(jnp.float32) for block in (blocks - 1, 0)]
        packed = jnp.zeros((1, LANES), jnp.float32)
        for band in range(bands):
            cut = slice(band * FACE, (band + 1) * FACE)

            def stack(parts):
                return jnp.concatenate(
                    parts + [jnp.zeros((8 - len(parts), n_o), jnp.float32)], 0,
                )

            lines = [stack([jnp.sum(x[cut], axis=0, keepdims=True) for x in twist])]
            hots = [onehots[band]]
            lines.append(stack([jnp.sum(x[cut], axis=0, keepdims=True) for x in beside]))
            hots.append(hot_of(jnp.where(
                lane_wide[:1] == 0,
                cells_of(ids_near[2, band : band + 1], firsts[0]),
                cells_of(ids_near[3, band : band + 1], firsts[1]),
            )))
            for s in both:
                if band == (0, bands - 1)[s]:
                    lines.append(stack(outer[s]))
                    other = (bands - 1, 0)[s]
                    hots.append(hot(ids_near[s, other : other + 1]))
            totals = lax.dot_general(
                jnp.concatenate(lines, 1), jnp.concatenate(hots, 1), (((1,), (1,)), ((), ())),
                precision=HIGHEST, preferred_element_type=jnp.float32,
            )
            packed = packed + jnp.concatenate([totals[i : i + 1] for i in range(COMPS + 1)], 1)
        if direct:
            stage_out[1] = packed
            sums[here] = packed
            for step in range(1, group):
                s2_copy(step).start()
        else:
            stage_out[0] = packed
            lat_sums[me_lat] = packed
            for step in range(1, n_lat):
                s1_copy(step).start()

    def surface():
        while pending:
            relay()
        if waves:
            wave_wait(waves - 1)
        for i, (_, _, take) in enumerate(near_devices):
            guarded(take, ids_copy(i).wait_recv)
        pl.when(is_top)(torques)

    def advance(b):
        phase(functools.partial(prepare, 1, b))
        start(1, b)

    def ready(b, done):
        return all(k in done for k in (b - 1, b, b + 1) if 0 <= k <= end)

    def sweep(h, order, finish, ship):
        done, shipped = set(), set()

        def near_part(b):
            near_side(h, b)

        def main_part(b):
            advance_face(h, b)

        def far_part(b):
            far_cols(h, b)
            far_rows(h, b)

        arrive_planes(h)
        if h == 0:
            for p in both:
                pl.when(rad_has[p])(functools.partial(link_plane, p))
        for b in order:
            arrive(h, b)
            if b == order[0]:
                relay()
            phase(functools.partial(near_part, b))
            phase(functools.partial(main_part, b))
        for b in order:
            phase(functools.partial((begin_second, begin_residual)[h], b))
        arrive_far(h)
        for p in both:
            pl.when(rad_has[p])(functools.partial(update_plane, h, p))
        arrive_late(h)
        for at, b in enumerate(order):
            phase(functools.partial(far_part, b))
            for k in [b]:
                if k not in done:
                    phase(functools.partial(finish, k))
                    done.add(k)
                    if k == order[0]:
                        relay()
                    if ship:
                        if k == end:
                            sent(0)
                        phase(functools.partial(pack_first, 1, k))
                        start(1, k, True)
                    for m in [end, 0] + order:
                        if ship and m not in shipped and ready(m, done):
                            ship(m)
                            shipped.add(m)

    first_order = list(reversed(range(blocks_r)))
    second_order = [end] + list(reversed(range(2, end))) + [k for k in (0, 1) if k < end]

    def ship_off(b):
        advance(b)

    sweep(0, first_order, second_step, ship_off)
    surface()

    if not direct:
        @pl.when(is_top)
        def _():
            await_thin(s1_recv, n_lat - 1)
            total = lat_sums[0]
            for i in range(1, n_lat):
                total = total + lat_sums[i]
            stage_out[1] = total
            sums[here] = total
            for step in range(1, group):
                s2_copy(step).start()

    sweep(1, second_order, residual, None)

    half = n_o // 2
    thin_r = lax.broadcasted_iota(jnp.int32, (LANES, half), 0)
    thin_c = lax.broadcasted_iota(jnp.int32, (LANES, half), 1)
    count = COMPS * (n_r // 2) * n_a // 2
    merged = jnp.zeros((count, half), jnp.float32)
    for h in range(reps):
        choose = jnp.where((thin_r + h * LANES) // 2 == thin_c, 0.125, 0.0).astype(jnp.bfloat16)
        summed = pairs[h, pl.ds(0, count, stride=2)] + pairs[h, pl.ds(1, count, stride=2)]
        big = summed.astype(jnp.bfloat16)
        small = (summed - big.astype(jnp.float32)).astype(jnp.bfloat16)
        merged = merged + (
            jnp.dot(big, choose, preferred_element_type=jnp.float32)
            + jnp.dot(small, choose, preferred_element_type=jnp.float32)
        )
    mine = count // COMPS
    spot = pl.ds(pl.multiple_of(me_rad * mine, mine), mine)
    for c in range(COMPS):
        coarse[c, spot] = merged[c * mine : (c + 1) * mine]

    def g_copy(step):
        return pltpu.make_async_remote_copy(
            coarse.at[:, spot], coarse.at[:, spot], g_send.at[0], g_recv.at[0],
            device_id={"rad": lax.rem(me_rad + step, n_rad)}, device_id_type=MESH,
        )

    for step in range(1, n_rad):
        g_copy(step).start()

    sources = n_lat * n_lon if direct else n_lon
    pl.when(is_top)(functools.partial(await_thin, s2_recv, sources - 1))
    pl.when(jnp.logical_not(is_top))(functools.partial(await_thin, s2_recv, sources))
    terms = [sums[i] for i in range(sources)]
    while len(terms) > 1:
        terms = [terms[i] + terms[i + 1] if i + 1 < len(terms) else terms[i] for i in range(0, len(terms), 2)]
    total = terms[0]
    area = total[:, COMPS * SLOT : (COMPS + 1) * SLOT]
    valid = lax.broadcasted_iota(jnp.int32, (1, SLOT), 1) < PLATES
    root = jnp.sqrt(jnp.where(valid, area, 1.0))
    turns = jnp.concatenate(
        [total[:, i * SLOT : (i + 1) * SLOT] / root for i in range(COMPS)]
        + [jnp.zeros((8 - COMPS, SLOT), jnp.float32)], 0,
    )
    for band in range(bands):
        cut = slice(band * FACE, (band + 1) * FACE)
        cell = jnp.dot(turns, onehots[band], precision=HIGHEST, preferred_element_type=jnp.float32)
        ox, oy, oz = (cell[i : i + 1] for i in range(COMPS))
        plate[0, cut] = oy * rz[cut] - oz * ry[cut]
        plate[1, cut] = oz * rx[cut] - ox * rz[cut]
        plate[2, cut] = ox * ry[cut] - oy * rx[cut]

    sent(1)
    for i, (_, send, _) in enumerate(near_devices):
        guarded(send, ids_copy(i).wait_send)

    @pl.when(is_top)
    def _():
        if not direct:
            await_thin(s1_send, n_lat - 1, True)
        await_thin(s2_send, group - 1, True)

    gathered = (n_rad - 1) * COMPS * mine // 2
    await_rows(g_recv.at[0], gathered)
    await_rows(g_send.at[0], gathered, True)


def write_out(last, coarse, plate, new_v_out, coarse_out, plate_out, sem):
    n_r = new_v_out.shape[1]
    copies = [
        pltpu.make_async_copy(last.at[:, pl.ds(1, n_r)], new_v_out, sem.at[0]),
        pltpu.make_async_copy(coarse, coarse_out, sem.at[1]),
        pltpu.make_async_copy(plate, plate_out, sem.at[2]),
    ]
    for copy in copies:
        copy.start()
    for copy in copies:
        copy.wait()


def on_device(sizes, velocity, forcing, viscosity, plate_ids):
    n_lat, n_lon, n_rad = sizes
    _, n_r, n_a, n_o = velocity.shape
    chunks = n_r // UNROLL
    f32 = jnp.float32
    dma = pltpu.SemaphoreType.DMA
    direct = n_lat * n_lon * n_rad <= DIRECT
    group = n_lat * n_lon * n_rad if direct else n_lon * n_rad
    sources = n_lat * n_lon if direct else n_lon
    in_any = pl.BlockSpec(memory_space=pl.ANY)
    in_vmem = pl.BlockSpec(memory_space=pltpu.VMEM)
    coarse_rows = n_rad * (n_r // 2) * (n_a // 2)
    whole = (n_r, n_a, n_o)
    thin = (n_a, LANES)
    flat = (PACK, n_o)

    def vmem(*shape):
        return pltpu.VMEM(shape, f32)

    held = pl.pallas_call(
        functools.partial(kernel, sizes),
        out_shape=(
            pltpu.VMEM((COMPS, n_r + 2, n_a, n_o), f32),
            pltpu.VMEM((COMPS, coarse_rows, n_o // 2), f32),
            pltpu.VMEM((COMPS, n_a, n_o), f32),
        ),
        in_specs=[pl.BlockSpec(memory_space=pltpu.HBM)] * 4,
        out_specs=(in_vmem,) * 3,
        scratch_shapes=[
            vmem(SWEEPS, COMPS, n_r + 2, n_a, n_o),
            pltpu.VMEM(plate_ids.shape, jnp.int32),
            pltpu.VMEM((4,) + plate_ids.shape, jnp.int32),
            vmem(COMPS, *whole),
            vmem(n_r + 2, n_a, n_o),
            vmem(2, *whole),
            vmem(2, *whole),
            vmem(n_r + 1, n_a, n_o),
            vmem(*whole),
            vmem(*whole),
            vmem(*whole),
            vmem(2, COMPS, *whole),
            vmem(2, 2, n_r, *flat),
            vmem(2, 2, n_r, *flat),
            vmem(2, 2, n_r, *flat),
            vmem(2, 2, n_r, *flat),
            vmem(4, 2, n_r, *flat),
            vmem(2, n_r, *flat),
            vmem(2, n_r, *flat),
            vmem(2, n_r, *flat),
            vmem(2, 2, *flat),
            vmem(2, chunks, *thin),
            vmem(2, chunks, *thin),
            vmem(2, chunks, 2, 2, *thin),
            vmem(2, chunks, *thin),
            vmem(4, chunks, *thin),
            vmem(chunks, *thin),
            vmem(chunks, *thin),
            vmem(chunks, 2, *thin),
            vmem(2, *thin),
            vmem(2, 2, COMPS, n_a, n_o),
            vmem(2, n_a, n_o),
            vmem(2, n_a, n_o),
            vmem(2, n_a, n_o),
            vmem(2, n_a, n_o),
            vmem(2, chunks, 2, 1, LANES),
            vmem(2, chunks, 2, 2, 1, LANES),
            vmem(2, chunks, LANES, LANES),
            vmem(2, 2, 2, *flat),
            vmem(2, 2, 2, *flat),
            vmem(2, 2, 2, *thin),
            vmem(n_o // LANES, COMPS * (n_r // 2) * n_a, LANES),
            vmem(sources, 1, LANES),
            vmem(n_lat, 1, LANES),
            vmem(2, 1, LANES),
            vmem(max(7 * UNROLL * n_a, chunks * (UNROLL * FIELDS + 8)), 1, n_o),
            vmem(max(group, sources, n_lat), 1, LANES),
            dma((chunks + 2,)),
            dma((1,)),
            dma((2,)),
            dma((2,)),
            dma((2,)),
            dma((2, 2)),
            dma((2, chunks)),
            dma((2, chunks, 2)),
            dma((1,)),
            dma((2,)),
            dma((2,)),
            dma((2, 2)),
            dma((2, 2)),
            dma((2, 2)),
            dma((2, 2, 2)),
            dma((2,)),
            dma((2, 2)),
            dma((4,)),
            dma((4,)),
            pltpu.SemaphoreType.REGULAR((n_lat - 1 if direct else 1, 2)),
            dma((4 if direct else 6,)),
        ],
        compiler_params=pltpu.CompilerParams(
            collective_id=0, has_side_effects=True, vmem_limit_bytes=32 * 2**20
        ),
    )(*(
        pltpu.with_memory_space_constraint(x, pltpu.HBM)
        for x in (velocity, forcing, viscosity, plate_ids)
    ))
    new_v, coarse, plate = pl.pallas_call(
        write_out,
        out_shape=(
            jax.ShapeDtypeStruct(velocity.shape, f32),
            jax.ShapeDtypeStruct((COMPS, coarse_rows, n_o // 2), f32),
            jax.ShapeDtypeStruct((COMPS, n_a, n_o), f32),
        ),
        in_specs=[in_vmem] * 3,
        out_specs=(in_any,) * 3,
        scratch_shapes=[dma((3,))],
        compiler_params=pltpu.CompilerParams(vmem_limit_bytes=4 * 2**20),
    )(*(pltpu.with_memory_space_constraint(x, pltpu.VMEM) for x in held))
    coarse = coarse.reshape(COMPS, n_rad * (n_r // 2), n_a // 2, n_o // 2)
    return new_v, coarse, plate


def solution(mesh):
    sizes = tuple(mesh.shape[a] for a in ("lat", "lon", "rad"))
    field = P(None, "rad", "lat", "lon")
    return jax.shard_map(
        functools.partial(on_device, sizes),
        mesh=mesh,
        in_specs=(field, field, P("rad", "lat", "lon"), P("lat", "lon")),
        out_specs=(field, P(None, None, "lat", "lon"), P(None, "lat", "lon")),
        check_vma=False,
    )
```

```python
import functools
import math

import jax
import jax.numpy as jnp
from jax import lax
from jax.experimental import pallas as pl
from jax.experimental.pallas import tpu as pltpu
from jax.sharding import PartitionSpec as P

SWEEPS = 3
PLATES = 12
FACE = 8
RELAX = 0.8
COMPS = 3
LANES = 128
SLOT = 32
MESH = pl.DeviceIdType.MESH
HIGHEST = lax.Precision.HIGHEST
UNROLL = 8
DIRECT = 64
FIELDS = 2 * (COMPS + 1)
PACK = COMPS + 1


def harmonic(own, other):
    return 2.0 * own * other / (own + other)


def harmonic0(own, other):
    return 2.0 * own * other / jnp.maximum(own + other, 1e-30)


class Link:
    def __init__(self, make):
        self.make = make

    def start(self):
        self.make().start()

    def wait_send(self):
        self.make().wait_send()

    def wait_recv(self):
        self.make().wait_recv()


def kernel(
    sizes, vel, forc, visc, ids_in,
    last, coarse, plate,
    early, ids, ids_near, f, eta, w_lat, w_lon, w_rad, gain, diag, part, num,
    row_out, row_in, more_out, more_in, row_sum, row_w, row_g, row_q, row_p,
    col_first, col_out, col_in, col_far, col_sum, col_w, col_g, col_d, col_p,
    plane_num, plane_d, plane_g, plane_l, plane_q,
    corner_out, corner_in, corner_t, edge_out, edge_in, side_in,
    pairs, sums, lat_sums, stage_out, tally, tally_thin,
    load_sem, lon_send, lat_send, rad_send, edge_send, lon_recv, lat_recv, late_lon_recv, late_lat_recv, rad_recv, num_recv, edge_recv, far_recv,
    ids_send, ids_recv, wave, misc,
):
    n_lat, n_lon, n_rad = sizes
    g_send, g_recv, s2_send, s2_recv = misc.at[0:1], misc.at[1:2], misc.at[2], misc.at[3]
    n_r, n_a, n_o = visc.shape
    me_lat, me_lon, me_rad = (lax.axis_index(a) for a in ("lat", "lon", "rad"))
    lat_has = (me_lat > 0, me_lat < n_lat - 1)
    rad_has = (me_rad > 0, me_rad < n_rad - 1)
    lat_to = (me_lat - 1, me_lat + 1)
    rad_to = (me_rad - 1, me_rad + 1)
    lon_to = (lax.rem(me_lon + n_lon - 1, n_lon), lax.rem(me_lon + 1, n_lon))
    is_top = me_rad == n_rad - 1
    direct = n_lat * n_lon * n_rad <= DIRECT
    s1_send, s1_recv = (None, None) if direct else (misc.at[4], misc.at[5])
    v = [early.at[t] for t in range(SWEEPS)] + [last]
    blocks_r = n_r // UNROLL
    end = blocks_r - 1
    both = (0, 1)

    def guarded(cond, call):
        if cond is None:
            call()
        else:
            pl.when(cond)(call)

    def all_of(*conds):
        conds = [c for c in conds if c is not None]
        return functools.reduce(jnp.logical_and, conds)

    barrier = pltpu.get_barrier_semaphore()

    def greet(device):
        pl.semaphore_signal(barrier, inc=1, device_id=device, device_id_type=MESH)

    expected = n_lon * n_rad - 1
    for step in range(1, n_lon * n_rad):
        greet({
            "lon": lax.rem(me_lon + step // n_rad, n_lon),
            "rad": lax.rem(me_rad + step % n_rad, n_rad),
        })
    for s in both:
        if direct:
            pl.when(lat_has[s])(functools.partial(greet, {"lat": lat_to[s]}))
            expected = expected + jnp.where(lat_has[s], 1, 0)
        for q in both:
            pl.when(lat_has[s])(functools.partial(greet, {"lat": lat_to[s], "lon": lon_to[q]}))
            expected = expected + jnp.where(lat_has[s], 1, 0)
        for p in both:
            has = all_of(lat_has[s], rad_has[p])
            pl.when(has)(functools.partial(greet, {"lat": lat_to[s], "rad": rad_to[p]}))
            expected = expected + jnp.where(has, 1, 0)
    if not direct:
        for step in range(1, n_lat):
            greet({"lat": lax.rem(me_lat + step, n_lat)})
        expected = expected + (n_lat - 1)

    def load_chunk(b, rest):
        here_r = pl.ds(b * UNROLL, UNROLL)
        inner = pl.ds(1 + b * UNROLL, UNROLL)
        if rest:
            return [pltpu.make_async_copy(forc.at[:, here_r], f.at[:, here_r], load_sem.at[blocks_r])]
        return [
            pltpu.make_async_copy(visc.at[here_r], eta.at[inner], load_sem.at[b]),
            pltpu.make_async_copy(vel.at[:, here_r], v[0].at[:, inner], load_sem.at[b]),
        ]

    for rest in (False, True):
        for b in reversed(range(blocks_r)):
            for load in load_chunk(b, rest):
                load.start()
    load_ids = pltpu.make_async_copy(ids_in, ids, load_sem.at[blocks_r + 1])
    load_ids.start()

    def rows_of(ref):
        return ref.size // n_o

    def await_rows(sem, rows, sending=False):
        some = tally.at[pl.ds(0, rows)]
        copy = pltpu.make_async_remote_copy(
            some, some, sem, sem, device_id={"lon": lon_to[1]}, device_id_type=MESH,
        )
        copy.wait_send() if sending else copy.wait_recv()

    def await_thin(sem, rows, sending=False):
        some = tally_thin.at[pl.ds(0, rows)]
        copy = pltpu.make_async_remote_copy(
            some, some, sem, sem, device_id={"lon": lon_to[1]}, device_id_type=MESH,
        )
        copy.wait_send() if sending else copy.wait_recv()

    def loaded(b):
        some = tally.at[pl.ds(0, (COMPS + 1) * UNROLL * n_a)]
        pltpu.make_async_copy(some, some, load_sem.at[b]).wait()

    def forcing_loaded():
        pltpu.make_async_copy(f, f, load_sem.at[blocks_r]).wait()

    lane_wide = lax.broadcasted_iota(jnp.int32, (n_a, n_o), 1)
    lane = lax.broadcasted_iota(jnp.int32, (n_a, LANES), 1)
    row = lax.broadcasted_iota(jnp.int32, (n_a, n_o), 0)
    row_thin = lax.broadcasted_iota(jnp.int32, (n_a, LANES), 0)
    even = lane % 2 == 0
    field_of = (lane + 1) % LANES // 2 % FIELDS
    layer_of = (lane + 1) % LANES // (2 * FIELDS)
    reps = n_o // LANES
    row_edge = (0, n_a - 1)
    lane_edge = (0, n_o - 1)
    thin_edge = (0, LANES - 1)

    plane_rows = n_a
    tile_rows = n_a * LANES // n_o

    def phase(call):
        pl.when(me_lat >= 0)(call)

    for p, slot, face in ((0, 0, 0), (1, n_r + 1, n_r)):
        @pl.when(jnp.logical_not(rad_has[p]))
        def _():
            zero_plane = jnp.zeros((n_a, n_o), jnp.float32)
            w_rad[face] = zero_plane
            for t in range(SWEEPS + 1):
                for c in range(COMPS):
                    v[t][c, slot] = zero_plane
            for h in both:
                for s in both:
                    edge_in[h, s, p] = jnp.zeros((PACK, n_o), jnp.float32)
                    side_in[h, p, s] = jnp.zeros((n_a, LANES), jnp.float32)
    for s in both:
        @pl.when(jnp.logical_not(lat_has[s]))
        def _():
            blank_rows = jnp.zeros((PACK, n_o), jnp.float32)
            for h in both:
                for r in range(n_r):
                    row_in[h, s, r] = blank_rows
                    more_in[h, s, r] = blank_rows + 1.0
                for b in range(blocks_r):
                    for q in both:
                        corner_in[h, b, s, q] = jnp.zeros((1, LANES), jnp.float32)
                for p in both:
                    edge_in[h, s, p] = blank_rows
            ids_near[s] = jnp.zeros(ids.shape, jnp.int32)

    def messages(h, b, early_part):
        t = 2 * h
        table = []

        def add(src, dst, sends, takes, device, cond):
            table.append((Link(functools.partial(
                pltpu.make_async_remote_copy, src, dst, sends, takes,
                device_id=device, device_id_type=MESH,
            )), cond))

        for p, layer, slot in ((0, 1, n_r + 1), (1, n_r, 0)):
            if p not in near_planes(b):
                continue
            device = {"rad": rad_to[p]}
            if early_part:
                sems = (rad_send.at[p], rad_recv.at[h, 1 - p])
                add(v[t].at[:, layer], v[t].at[:, slot], *sems, device, rad_has[p])
                if h == 0:
                    add(eta.at[layer], eta.at[slot], *sems, device, rad_has[p])
            sems = (rad_send.at[p], num_recv.at[h, 1 - p])
            if early_part:
                for q in both:
                    add(
                        col_first.at[h, b], side_in.at[h, 1 - p, 1 - q], *sems,
                        {"lon": lon_to[q], "rad": rad_to[p]}, rad_has[p],
                    )
                for s in both:
                    add(
                        edge_out.at[h, s, p], edge_in.at[h, 1 - s, 1 - p],
                        edge_send.at[s, p], edge_recv.at[h, 1 - s, 1 - p],
                        {"lat": lat_to[s], "rad": rad_to[p]}, all_of(rad_has[p], lat_has[s]),
                    )
            else:
                add(num.at[h, :, layer - 1], plane_num.at[h, 1 - p], *sems, device, rad_has[p])
                if h == 0:
                    add(part.at[layer - 1], plane_d.at[1 - p], *sems, device, rad_has[p])
        layers = pl.ds(b * UNROLL, UNROLL)
        columns, rows, rows_at = (col_first, row_out, row_in) if early_part else (col_out, more_out, more_in)
        lon_sems = (lon_send, lon_recv) if early_part else (lon_send, late_lon_recv)
        which = (h, b) if early_part else (h,)
        lat_sems = (lat_send, lat_recv) if early_part else (lat_send, late_lat_recv)
        if early_part:
            for s in both:
                for q in both:
                    add(
                        corner_out.at[h, b, s], corner_in.at[h, b, 1 - s, 1 - q],
                        lat_send.at[s], far_recv.at[h, 1 - s],
                        {"lat": lat_to[s], "lon": lon_to[q]}, lat_has[s],
                    )
        for q in both:
            add(
                columns.at[h, b], col_in.at[h, b, 0 if early_part else 1, 1 - q],
                lon_sems[0].at[0], lon_sems[1].at[*which], {"lon": lon_to[q]}, None,
            )
        for s in both:
            add(
                rows.at[h, s, layers], rows_at.at[h, 1 - s, layers],
                lat_sems[0].at[s], lat_sems[1].at[*which, 1 - s], {"lat": lat_to[s]}, lat_has[s],
            )
        return table

    corner_rows = 2 * LANES // n_o
    lat_rows = UNROLL * PACK

    def rad_rows(h):
        return (COMPS + (1 if h == 0 else 0)) * n_a

    def num_rows(h):
        return rad_rows(h) + 2 * tile_rows

    def start(h, b, early_part=False):
        for copy, cond in messages(h, b, early_part):
            guarded(cond, copy.start)

    def near_planes(b):
        return [p for p, at in ((0, 0), (1, end)) if b == at]

    def arrive(h, b):
        await_rows(lon_recv.at[h, b], 2 * tile_rows)
        for s in both:
            guarded(lat_has[s], functools.partial(await_rows, lat_recv.at[h, b, s], lat_rows))

    def arrive_late(h):
        await_rows(late_lon_recv.at[h], blocks_r * 2 * tile_rows)
        for s in both:
            guarded(
                lat_has[s], functools.partial(await_rows, late_lat_recv.at[h, s], blocks_r * lat_rows),
            )

    def arrive_planes(h):
        for p in both:
            guarded(rad_has[p], functools.partial(await_rows, rad_recv.at[h, p], rad_rows(h)))

    def arrive_far(h):
        for p in both:
            guarded(rad_has[p], functools.partial(await_rows, num_recv.at[h, p], num_rows(h)))
        for s in both:
            for p in both:
                guarded(
                    all_of(rad_has[p], lat_has[s]),
                    functools.partial(await_rows, edge_recv.at[h, s, p], PACK),
                )
            guarded(
                lat_has[s],
                functools.partial(await_rows, far_recv.at[h, s], blocks_r * corner_rows),
            )

    def sent(h):
        for p in both:
            guarded(
                rad_has[p],
                functools.partial(await_rows, rad_send.at[p], rad_rows(h) + num_rows(h), True),
            )
            for s in both:
                guarded(
                    all_of(rad_has[p], lat_has[s]),
                    functools.partial(await_rows, edge_send.at[s, p], PACK, True),
                )
        await_rows(lon_send.at[0], 2 * blocks_r * 2 * tile_rows, True)
        for s in both:
            guarded(
                lat_has[s],
                functools.partial(
                    await_rows, lat_send.at[s], blocks_r * (2 * lat_rows + corner_rows), True,
                ),
            )

    def turn(x, shift, axis):
        shift = shift % x.shape[axis]
        return pltpu.roll(x, shift, axis) if shift else x

    def interior(t, r, c):
        tile = v[t][c, r + 1]
        return tile, (
            (w_lat[0, r] * turn(tile, 1, 0) + w_lat[1, r] * turn(tile, -1, 0))
            + (w_lon[0, r] * turn(tile, 1, 1) + w_lon[1, r] * turn(tile, -1, 1))
        )

    def radial(t, r, c, seams):
        total = None
        for face, slot in ((r, r), (r + 1, r + 2)):
            if (slot in (0, n_r + 1)) == seams or (seams is None):
                term = w_rad[face] * v[t][c, slot]
                total = term if total is None else total + term
        return total

    def lane_at(g, j):
        return 2 * (j * FIELDS + g)

    def ends_of(x, k):
        x = turn(x, -k, 1)
        west = jnp.where(lane == 0, x, 0.0)
        east = jnp.where(lane == LANES - 1, x, 0.0)
        if reps == 1:
            return west + east
        gap = [jnp.zeros((n_a, LANES), jnp.float32)] * (reps - 2)
        return jnp.concatenate([west] + gap + [east], 1)

    def edge_rows(low, high):
        return jnp.where(row == 0, low, jnp.where(row == n_a - 1, high, 0.0))

    def seams(t, b, j, c):
        r = b * UNROLL + j
        low, high = (row_sum[t, s, r, 1 + c : 2 + c] for s in both)
        return edge_rows(low, high) + ends_of(col_sum[t, b], lane_at(1 + c, j))

    def pack(h, r, k, tile, packed, rows):
        for i in range(reps):
            piece = slice(i * LANES, (i + 1) * LANES)
            rows[h, 0, r, k : k + 1, piece] = tile[:1, piece]
            rows[h, 1, r, k : k + 1, piece] = tile[n_a - 1 :, piece]
        at = lane_at(k, r % UNROLL)
        two = jnp.where(lane < LANES // 2, tile[:, :LANES], tile[:, n_o - LANES :])
        hit = jnp.logical_and(field_of == k, layer_of == r % UNROLL)
        return jnp.where(hit, turn(two, at, 1), packed)

    def pack_first(h, b):
        t = 2 * h
        packed = jnp.zeros((n_a, LANES), jnp.float32)
        for j in range(UNROLL):
            r = b * UNROLL + j
            tiles = [(1 + c, v[t][c, r + 1]) for c in range(COMPS)]
            if h == 0:
                tiles.append((0, eta[r + 1]))
            for k, tile in tiles:
                packed = pack(h, r, k, tile, packed, row_out)
                for p, layer in ((0, 0), (1, n_r - 1)):
                    if r == layer:
                        for s in both:
                            for i in range(reps):
                                piece = slice(i * LANES, (i + 1) * LANES)
                                edge_out[h, s, p, k : k + 1, piece] = tile[row_edge[s] : row_edge[s] + 1, piece]
        col_first[h, b] = packed
        for s in both:
            corner_out[h, b, s] = packed[row_edge[s] : row_edge[s] + 1]

    def prepare(h, b):
        t = 2 * h
        packed = jnp.zeros((n_a, LANES), jnp.float32)
        for j in range(UNROLL):
            r = b * UNROLL + j
            if h == 0:
                own = eta[r + 1]
                below = jnp.where(row == 0, 0.0, harmonic(own, turn(own, 1, 0)))
                above = jnp.where(row == n_a - 1, 0.0, turn(below, -1, 0))
                west = jnp.where(lane_wide == 0, 0.0, harmonic(own, turn(own, 1, 1)))
                east = jnp.where(lane_wide == n_o - 1, 0.0, turn(west, -1, 1))
                w_lat[0, r] = below
                w_lat[1, r] = above
                w_lon[0, r] = west
                w_lon[1, r] = east
                d = 0.5 * own + (below + above) + (west + east)
                if r > 0:
                    down = harmonic(own, eta[r])
                    w_rad[r] = down
                    d = d + down
                if r < n_r - 1:
                    d = d + harmonic(own, eta[r + 2])
                part[r] = d
                packed = pack(h, r, 0, d, packed, more_out)
        for j in range(UNROLL):
            r = b * UNROLL + j
            for c in range(COMPS):
                tile, near = interior(t, r, c)
                if h == 0:
                    total = f[c, r] + near
                    if r > 0:
                        total = total + w_rad[r] * v[t][c, r]
                    if r < n_r - 1:
                        up = w_rad[r + 1] if j < UNROLL - 1 else harmonic(eta[r + 1], eta[r + 2])
                        total = total + up * v[t][c, r + 2]
                else:
                    total = f[c, r] + (near + radial(t, r, c, False))
                num[h, c, r] = total
                packed = pack(h, r, 1 + c, total, packed, more_out)
        col_out[h, b] = packed

    def repeat_from(x, field, shifts):
        fields = field_of if x.shape[0] == n_a else field_of[:1]
        only = jnp.where(fields == field, x, 0.0)
        return functools.reduce(jnp.add, [turn(only, 2 * k, 1) for k in shifts])

    def repeat_first(x):
        return repeat_from(x, 0, range(COMPS + 1))

    def joined(from_west, from_east):
        at = even if from_west.shape[0] == n_a else even[:1]
        return jnp.where(at, turn(from_west, 1, 1), turn(from_east, -1, 1))

    def near_side(h, b):
        t = 2 * h
        far = joined(col_in[h, b, 0, 0], col_in[h, b, 0, 1])
        col_far[h, b] = far
        if h == 0:
            w = harmonic0(repeat_first(far), repeat_first(col_first[h, b]))
            col_w[b] = w
        else:
            w = col_w[b]
        col_sum[t, b] = w * far
        for s in both:
            for r in range(b * UNROLL, (b + 1) * UNROLL):
                if h == 0:
                    w = harmonic(
                        jnp.broadcast_to(row_in[h, s, r, :1], (PACK, n_o)),
                        jnp.broadcast_to(row_out[h, s, r, :1], (PACK, n_o)),
                    )
                    row_w[s, r] = w
                else:
                    w = row_w[s, r]
                row_sum[t, s, r] = w * row_in[h, s, r]

    def far_rows(h, b):
        t = 2 * h
        for s in both:
            for j in range(UNROLL):
                r = b * UNROLL + j
                far = row_in[h, s, r]
                column = corner_t[h, b, pl.ds(lane_at(0, j), FIELDS, stride=2), :]
                corner = ends_of(column, 2 * s + 1)[:PACK]
                near = [p for p, layer in ((0, 0), (1, n_r - 1)) if r == layer]
                w = row_w[s, r]
                if h == 0:
                    far_eta = jnp.broadcast_to(row_in[h, s, r, :1], (PACK, n_o))
                    wq = harmonic0(far_eta, corner[:1])
                    d = more_in[h, s, r, :1] + (w + wq)
                    for p in near:
                        wp = harmonic0(far_eta, edge_in[h, s, p, :1])
                        row_p[s, p] = wp
                        d = d + wp
                    row_q[s, r] = wq
                    gain_far = RELAX / d
                    row_g[s, r] = gain_far
                else:
                    wq, gain_far = row_q[s, r], row_g[s, r]
                total = more_in[h, s, r] + w * row_out[h, s, r] + wq * corner
                for p in near:
                    total = total + row_p[s, p] * edge_in[h, s, p]
                row_sum[t + 1, s, r] = w * ((1.0 - RELAX) * far + gain_far * total)

    def side_of(h, p):
        return joined(side_in[h, p, 0], side_in[h, p, 1])

    def far_cols(h, b):
        t = 2 * h
        far = col_far[h, b]
        own = col_first[h, b]
        more = joined(col_in[h, b, 1, 0], col_in[h, b, 1, 1])
        stacked = jnp.zeros((8, LANES), jnp.float32)
        spot = lax.broadcasted_iota(jnp.int32, (8, LANES), 0)
        for s in both:
            stacked = jnp.where(spot == 2 * s + 1, turn(corner_in[h, b, s, 0], 1, 1), stacked)
            stacked = jnp.where(spot == 2 * s, corner_in[h, b, s, 1], stacked)
        corner_t[h, b, :, :8] = stacked.T
        corners = [joined(corner_in[h, b, s, 0], corner_in[h, b, s, 1]) for s in both]
        move = 2 * FIELDS * (UNROLL - 1)
        sides = {p: turn(side_of(h, p), -move if p == 0 else move, 1) for p in near_planes(b)}
        w = col_w[b]
        if h == 0:
            far_eta = repeat_first(far)
            d = repeat_first(more) + w
            for s in both:
                wd = jnp.where(
                    row_thin == row_edge[s], harmonic0(far_eta, repeat_first(corners[s])), 0.0,
                )
                col_d[b, s] = wd
                d = d + wd
            for p in near_planes(b):
                wp = jnp.where(
                    layer_of == (0, UNROLL - 1)[p], harmonic0(far_eta, repeat_first(sides[p])), 0.0,
                )
                col_p[p] = wp
                d = d + wp
            col_g[b] = RELAX / jnp.where(d > 0.0, d, 1.0)
        total = more + w * own
        for s in both:
            total = total + col_d[b, s] * corners[s]
        for p in near_planes(b):
            total = total + col_p[p] * sides[p]
        col_sum[t + 1, b] = w * ((1.0 - RELAX) * far + col_g[b] * total)

    def link_plane(p):
        slot, layer, face = ((0, 1, 0), (n_r + 1, n_r, n_r))[p]
        w_rad[face] = harmonic(eta[slot], eta[layer])

    def update_plane(h, p):
        t = 2 * h
        slot, layer, face, j = ((0, 1, 0, UNROLL - 1), (n_r + 1, n_r, n_r, 0))[p]
        side = side_of(h, p)
        if h == 0:
            own = eta[slot]
            w = w_rad[face]
            wq = harmonic0(own, ends_of(side, lane_at(0, j)))
            plane_q[p] = wq
            d = plane_d[p] + (w + wq)
            wl = edge_rows(*(harmonic0(own, edge_in[h, s, p, :1]) for s in both))
            plane_l[p] = wl
            plane_g[p] = RELAX / (d + wl)
        for c in range(COMPS):
            total = plane_num[h, p, c] + w_rad[face] * v[t][c, layer]
            total = total + plane_l[p] * edge_rows(*(edge_in[h, s, p, 1 + c : 2 + c] for s in both))
            total = total + plane_q[p] * ends_of(side, lane_at(1 + c, j))
            v[t + 1][c, slot] = (1.0 - RELAX) * v[t][c, slot] + plane_g[p] * total

    def settle(b):
        for j in range(UNROLL):
            r = b * UNROLL + j
            low, high = (row_w[s, r, :1] for s in both)
            d = part[r] + (edge_rows(low, high) + ends_of(col_w[b], lane_at(0, j)))
            if r == 0:
                d = d + w_rad[0]
            if r == n_r - 1:
                d = d + w_rad[n_r]
            diag[r] = d
            gain[r] = RELAX / d

    def advance_face(h, b):
        t = 2 * h
        if h == 0:
            settle(b)
        for c in range(COMPS):
            for j in range(UNROLL):
                r = b * UNROLL + j
                total = num[h, c, r] + seams(t, b, j, c)
                if r in (0, n_r - 1):
                    total = total + radial(t, r, c, True)
                v[t + 1][c, r + 1] = (1.0 - RELAX) * v[t][c, r + 1] + gain[r] * total

    def begin_second(b):
        for c in range(COMPS):
            for j in range(UNROLL):
                r = b * UNROLL + j
                _, near = interior(1, r, c)
                num[1, c, r] = f[c, r] + (near + radial(1, r, c, False))

    def second_step(b):
        for c in range(COMPS):
            for j in range(UNROLL):
                r = b * UNROLL + j
                total = num[1, c, r] + seams(1, b, j, c)
                if r in (0, n_r - 1):
                    total = total + radial(1, r, c, True)
                v[2][c, r + 1] = (1.0 - RELAX) * v[1][c, r + 1] + gain[r] * total

    def pair_rows(c, b, i):
        return pl.ds((c * (n_r // 2) + b * (UNROLL // 2) + i) * n_a, n_a)

    def begin_residual(b):
        t = SWEEPS
        for c in range(COMPS):
            for i in range(UNROLL // 2):
                two = jnp.zeros((n_a, n_o), jnp.float32)
                for j in (2 * i, 2 * i + 1):
                    r = b * UNROLL + j
                    tile, near = interior(t, r, c)
                    two = two + ((f[c, r] + near) + (radial(t, r, c, False) - diag[r] * tile))
                for k in range(reps):
                    pairs[k, pair_rows(c, b, i)] = two[:, k * LANES : (k + 1) * LANES]

    def residual(b):
        t = SWEEPS
        for c in range(COMPS):
            for i in range(UNROLL // 2):
                rows = [
                    sum(row_sum[t, s, b * UNROLL + j, 1 + c : 2 + c] for j in (2 * i, 2 * i + 1))
                    for s in both
                ]
                more = edge_rows(*rows) + (
                    ends_of(col_sum[t, b], lane_at(1 + c, 2 * i))
                    + ends_of(col_sum[t, b], lane_at(1 + c, 2 * i + 1))
                )
                for r in (b * UNROLL + 2 * i, b * UNROLL + 2 * i + 1):
                    if r in (0, n_r - 1):
                        more = more + radial(t, r, c, True)
                at = pair_rows(c, b, i)
                for k in range(reps):
                    pairs[k, at] = pairs[k, at] + more[:, k * LANES : (k + 1) * LANES]

    for b in reversed(range(blocks_r)):
        loaded(b)
        phase(functools.partial(pack_first, 0, b))
    pl.semaphore_wait(barrier, expected)
    for b in reversed(range(blocks_r)):
        start(0, b, True)
    forcing_loaded()
    for b in reversed(range(blocks_r)):
        phase(functools.partial(prepare, 0, b))
        start(0, b)
    load_ids.wait()

    near_devices = [({"lat": lat_to[s]}, lat_has[s], lat_has[1 - s]) for s in both] + [
        ({"lon": lon_to[q]}, None, None) for q in both
    ]

    def ids_copy(i):
        return Link(functools.partial(
            pltpu.make_async_remote_copy, ids, ids_near.at[i ^ 1], ids_send.at[i], ids_recv.at[i],
            device_id=near_devices[i][0], device_id_type=MESH,
        ))

    for i, (_, send, _) in enumerate(near_devices):
        guarded(send, ids_copy(i).start)

    def wave_signal(k):
        for s in both:
            def tell():
                pl.semaphore_signal(wave.at[k, s], inc=1, device_id={"lat": lat_to[s]}, device_id_type=MESH)
            pl.when(lat_has[s])(tell)

    def wave_wait(k):
        for s in both:
            def hear():
                pl.semaphore_wait(wave.at[k, s], 1)
            pl.when(lat_has[1 - s])(hear)

    waves = n_lat - 1 if direct else 0
    if waves:
        wave_signal(0)

    lat_cell = (me_lat * n_a + row).astype(jnp.float32)
    lon_cell = (me_lon * n_o + lane_wide).astype(jnp.float32)
    phi = math.pi * ((lat_cell + 0.5) / (n_lat * n_a) - 0.5)
    lam = (2.0 * math.pi) * (lon_cell[:1] + 0.5) / (n_lon * n_o)
    cos_lat = jnp.cos(phi)
    cos_lon, sin_lon = jnp.cos(lam), jnp.sin(lam)
    rx = cos_lat * cos_lon
    ry = cos_lat * sin_lon
    rz = jnp.sin(phi)
    blocks = ids.shape[1]
    bands = n_a // FACE
    spread_rows = lax.broadcasted_iota(jnp.int32, (blocks, n_o), 0)
    spread_cols = lax.broadcasted_iota(jnp.int32, (blocks, n_o), 1)
    spread = (spread_cols // FACE == spread_rows).astype(jnp.float32)
    numbers = lax.broadcasted_iota(jnp.int32, (SLOT, n_o), 0)

    def cells_of(line, chosen):
        own = jnp.broadcast_to(line.astype(jnp.float32), (8, blocks))
        return jnp.dot(own, chosen, precision=HIGHEST)[:1]

    def hot(line):
        return hot_of(cells_of(line, spread))

    def hot_of(cells):
        return (jnp.abs(cells - numbers.astype(jnp.float32)) < 0.5).astype(jnp.float32)

    onehots = [hot(ids[band : band + 1]) for band in range(bands)]

    pending = list(range(1, waves))

    def relay():
        if pending:
            k = pending.pop(0)
            wave_wait(k - 1)
            wave_signal(k)

    def s1_copy(step):
        return pltpu.make_async_remote_copy(
            stage_out.at[0], lat_sums.at[me_lat], s1_send, s1_recv,
            device_id={"lat": lax.rem(me_lat + step, n_lat)}, device_id_type=MESH,
        )

    here = me_lat * n_lon + me_lon if direct else me_lon
    group = n_lat * n_lon * n_rad if direct else n_lon * n_rad
    plane = n_lon * n_rad

    def s2_copy(step):
        device = {
            "lon": lax.rem(me_lon + (step % plane) // n_rad, n_lon),
            "rad": lax.rem(me_rad + step % n_rad, n_rad),
        }
        if direct:
            device["lat"] = lax.rem(me_lat + step // plane, n_lat)
        return pltpu.make_async_remote_copy(
            stage_out.at[1], sums.at[here], s2_send, s2_recv,
            device_id=device, device_id_type=MESH,
        )

    def cross(k, x, drag):
        return [
            (x[1] * drag[2] - x[2] * drag[1]) * k,
            (x[2] * drag[0] - x[0] * drag[2]) * k,
            (x[0] * drag[1] - x[1] * drag[0]) * k,
        ]

    def torques():
        top = n_r - 1
        guess = [
            [(1.0 - RELAX) * v[2][c, r + 1] + gain[r] * num[1, c, r] for c in range(COMPS)]
            for r in (top, top - 1)
        ]
        drag = [eta[n_r] * (guess[0][c] - guess[1][c]) for c in range(COMPS)]
        twist = cross(cos_lat, (rx, ry, rz), drag) + [cos_lat]
        outer = []
        for s in both:
            k = (me_lat * n_a + (n_a if s else -1)).astype(jnp.float32)
            tilt = math.pi * ((jnp.full((1, n_o), 0.5, jnp.float32) + k) / (n_lat * n_a) - 0.5)
            cos_tilt = jnp.cos(tilt)
            moved = [(row_g[s, r] * row_w[s, r]) * row_out[1, s, r] for r in (top, top - 1)]
            shift = row_in[0, s, top, :1] * (moved[0] - moved[1])
            push = [shift[1 + c : 2 + c] for c in range(COMPS)]
            outer.append(cross(cos_tilt, (cos_tilt * cos_lon, cos_tilt * sin_lon, jnp.sin(tilt)), push))
        moved = col_g[end] * col_w[end] * col_first[1, end]
        shift = repeat_first(col_far[0, end]) * (moved - turn(moved, 2 * FIELDS, 1))
        push = [ends_of(shift, lane_at(1 + c, UNROLL - 1)) for c in range(COMPS)]
        around = n_lon * n_o
        column = jnp.where(
            lane_wide[:1] == 0,
            lax.rem(me_lon * n_o + (around - 1), around), lax.rem(me_lon * n_o + n_o, around),
        ).astype(jnp.float32)
        angle = (2.0 * math.pi) * (column + 0.5) / around
        beside = cross(cos_lat, (cos_lat * jnp.cos(angle), cos_lat * jnp.sin(angle), rz), push)
        firsts = [(spread_rows == block).astype(jnp.float32) for block in (blocks - 1, 0)]
        packed = jnp.zeros((1, LANES), jnp.float32)
        for band in range(bands):
            cut = slice(band * FACE, (band + 1) * FACE)

            def stack(parts):
                return jnp.concatenate(
                    parts + [jnp.zeros((8 - len(parts), n_o), jnp.float32)], 0,
                )

            lines = [stack([jnp.sum(x[cut], axis=0, keepdims=True) for x in twist])]
            hots = [onehots[band]]
            lines.append(stack([jnp.sum(x[cut], axis=0, keepdims=True) for x in beside]))
            hots.append(hot_of(jnp.where(
                lane_wide[:1] == 0,
                cells_of(ids_near[2, band : band + 1], firsts[0]),
                cells_of(ids_near[3, band : band + 1], firsts[1]),
            )))
            for s in both:
                if band == (0, bands - 1)[s]:
                    lines.append(stack(outer[s]))
                    other = (bands - 1, 0)[s]
                    hots.append(hot(ids_near[s, other : other + 1]))
            totals = lax.dot_general(
                jnp.concatenate(lines, 1), jnp.concatenate(hots, 1), (((1,), (1,)), ((), ())),
                precision=HIGHEST, preferred_element_type=jnp.float32,
            )
            packed = packed + jnp.concatenate([totals[i : i + 1] for i in range(COMPS + 1)], 1)
        if direct:
            stage_out[1] = packed
            sums[here] = packed
            for step in range(1, group):
                s2_copy(step).start()
        else:
            stage_out[0] = packed
            lat_sums[me_lat] = packed
            for step in range(1, n_lat):
                s1_copy(step).start()

    def surface():
        while pending:
            relay()
        if waves:
            wave_wait(waves - 1)
        for i, (_, _, take) in enumerate(near_devices):
            guarded(take, ids_copy(i).wait_recv)
        pl.when(is_top)(torques)

    def advance(b):
        phase(functools.partial(prepare, 1, b))
        start(1, b)

    def ready(b, done):
        return all(k in done for k in (b - 1, b, b + 1) if 0 <= k <= end)

    def sweep(h, order, finish, ship):
        done, shipped = set(), set()

        def near_part(b):
            near_side(h, b)

        def main_part(b):
            advance_face(h, b)

        def far_part(b):
            far_cols(h, b)
            far_rows(h, b)

        arrive_planes(h)
        if h == 0:
            for p in both:
                pl.when(rad_has[p])(functools.partial(link_plane, p))
        for b in order:
            arrive(h, b)
            if b == order[0]:
                relay()
            def both_parts(b=b):
                near_part(b)
                main_part(b)

            phase(both_parts)
        for b in order:
            phase(functools.partial((begin_second, begin_residual)[h], b))
        arrive_far(h)
        for p in both:
            pl.when(rad_has[p])(functools.partial(update_plane, h, p))
        arrive_late(h)
        for at, b in enumerate(order):
            phase(functools.partial(far_part, b))
            for k in [b]:
                if k not in done:
                    phase(functools.partial(finish, k))
                    done.add(k)
                    if k == order[0]:
                        relay()
                    if ship:
                        if k == end:
                            sent(0)
                        phase(functools.partial(pack_first, 1, k))
                        start(1, k, True)
                    for m in [end, 0] + order:
                        if ship and m not in shipped and ready(m, done):
                            ship(m)
                            shipped.add(m)

    first_order = list(reversed(range(blocks_r)))
    second_order = [end] + list(reversed(range(2, end))) + [k for k in (0, 1) if k < end]

    def ship_off(b):
        advance(b)

    sweep(0, first_order, second_step, ship_off)
    surface()

    if not direct:
        @pl.when(is_top)
        def _():
            await_thin(s1_recv, n_lat - 1)
            total = lat_sums[0]
            for i in range(1, n_lat):
                total = total + lat_sums[i]
            stage_out[1] = total
            sums[here] = total
            for step in range(1, group):
                s2_copy(step).start()

    sweep(1, second_order, residual, None)

    half = n_o // 2
    thin_r = lax.broadcasted_iota(jnp.int32, (LANES, half), 0)
    thin_c = lax.broadcasted_iota(jnp.int32, (LANES, half), 1)
    count = COMPS * (n_r // 2) * n_a // 2
    merged = jnp.zeros((count, half), jnp.float32)
    for h in range(reps):
        choose = jnp.where((thin_r + h * LANES) // 2 == thin_c, 0.125, 0.0).astype(jnp.bfloat16)
        summed = pairs[h, pl.ds(0, count, stride=2)] + pairs[h, pl.ds(1, count, stride=2)]
        big = summed.astype(jnp.bfloat16)
        small = (summed - big.astype(jnp.float32)).astype(jnp.bfloat16)
        merged = merged + (
            jnp.dot(big, choose, preferred_element_type=jnp.float32)
            + jnp.dot(small, choose, preferred_element_type=jnp.float32)
        )
    mine = count // COMPS
    spot = pl.ds(pl.multiple_of(me_rad * mine, mine), mine)
    for c in range(COMPS):
        coarse[c, spot] = merged[c * mine : (c + 1) * mine]

    def g_copy(step):
        return pltpu.make_async_remote_copy(
            coarse.at[:, spot], coarse.at[:, spot], g_send.at[0], g_recv.at[0],
            device_id={"rad": lax.rem(me_rad + step, n_rad)}, device_id_type=MESH,
        )

    for step in range(1, n_rad):
        g_copy(step).start()

    sources = n_lat * n_lon if direct else n_lon
    pl.when(is_top)(functools.partial(await_thin, s2_recv, sources - 1))
    pl.when(jnp.logical_not(is_top))(functools.partial(await_thin, s2_recv, sources))
    terms = [sums[i] for i in range(sources)]
    while len(terms) > 1:
        terms = [terms[i] + terms[i + 1] if i + 1 < len(terms) else terms[i] for i in range(0, len(terms), 2)]
    total = terms[0]
    area = total[:, COMPS * SLOT : (COMPS + 1) * SLOT]
    valid = lax.broadcasted_iota(jnp.int32, (1, SLOT), 1) < PLATES
    root = jnp.sqrt(jnp.where(valid, area, 1.0))
    turns = jnp.concatenate(
        [total[:, i * SLOT : (i + 1) * SLOT] / root for i in range(COMPS)]
        + [jnp.zeros((8 - COMPS, SLOT), jnp.float32)], 0,
    )
    for band in range(bands):
        cut = slice(band * FACE, (band + 1) * FACE)
        cell = jnp.dot(turns, onehots[band], precision=HIGHEST, preferred_element_type=jnp.float32)
        ox, oy, oz = (cell[i : i + 1] for i in range(COMPS))
        plate[0, cut] = oy * rz[cut] - oz * ry[cut]
        plate[1, cut] = oz * rx[cut] - ox * rz[cut]
        plate[2, cut] = ox * ry[cut] - oy * rx[cut]

    sent(1)
    for i, (_, send, _) in enumerate(near_devices):
        guarded(send, ids_copy(i).wait_send)

    @pl.when(is_top)
    def _():
        if not direct:
            await_thin(s1_send, n_lat - 1, True)
        await_thin(s2_send, group - 1, True)

    gathered = (n_rad - 1) * COMPS * mine // 2
    await_rows(g_recv.at[0], gathered)
    await_rows(g_send.at[0], gathered, True)


def write_out(last, coarse, plate, new_v_out, coarse_out, plate_out, sem):
    n_r = new_v_out.shape[1]
    copies = [
        pltpu.make_async_copy(last.at[:, pl.ds(1, n_r)], new_v_out, sem.at[0]),
        pltpu.make_async_copy(coarse, coarse_out, sem.at[1]),
        pltpu.make_async_copy(plate, plate_out, sem.at[2]),
    ]
    for copy in copies:
        copy.start()
    for copy in copies:
        copy.wait()


def on_device(sizes, velocity, forcing, viscosity, plate_ids):
    n_lat, n_lon, n_rad = sizes
    _, n_r, n_a, n_o = velocity.shape
    chunks = n_r // UNROLL
    f32 = jnp.float32
    dma = pltpu.SemaphoreType.DMA
    direct = n_lat * n_lon * n_rad <= DIRECT
    group = n_lat * n_lon * n_rad if direct else n_lon * n_rad
    sources = n_lat * n_lon if direct else n_lon
    in_any = pl.BlockSpec(memory_space=pl.ANY)
    in_vmem = pl.BlockSpec(memory_space=pltpu.VMEM)
    coarse_rows = n_rad * (n_r // 2) * (n_a // 2)
    whole = (n_r, n_a, n_o)
    thin = (n_a, LANES)
    flat = (PACK, n_o)

    def vmem(*shape):
        return pltpu.VMEM(shape, f32)

    held = pl.pallas_call(
        functools.partial(kernel, sizes),
        out_shape=(
            pltpu.VMEM((COMPS, n_r + 2, n_a, n_o), f32),
            pltpu.VMEM((COMPS, coarse_rows, n_o // 2), f32),
            pltpu.VMEM((COMPS, n_a, n_o), f32),
        ),
        in_specs=[pl.BlockSpec(memory_space=pltpu.HBM)] * 4,
        out_specs=(in_vmem,) * 3,
        scratch_shapes=[
            vmem(SWEEPS, COMPS, n_r + 2, n_a, n_o),
            pltpu.VMEM(plate_ids.shape, jnp.int32),
            pltpu.VMEM((4,) + plate_ids.shape, jnp.int32),
            vmem(COMPS, *whole),
            vmem(n_r + 2, n_a, n_o),
            vmem(2, *whole),
            vmem(2, *whole),
            vmem(n_r + 1, n_a, n_o),
            vmem(*whole),
            vmem(*whole),
            vmem(*whole),
            vmem(2, COMPS, *whole),
            vmem(2, 2, n_r, *flat),
            vmem(2, 2, n_r, *flat),
            vmem(2, 2, n_r, *flat),
            vmem(2, 2, n_r, *flat),
            vmem(4, 2, n_r, *flat),
            vmem(2, n_r, *flat),
            vmem(2, n_r, *flat),
            vmem(2, n_r, *flat),
            vmem(2, 2, *flat),
            vmem(2, chunks, *thin),
            vmem(2, chunks, *thin),
            vmem(2, chunks, 2, 2, *thin),
            vmem(2, chunks, *thin),
            vmem(4, chunks, *thin),
            vmem(chunks, *thin),
            vmem(chunks, *thin),
            vmem(chunks, 2, *thin),
            vmem(2, *thin),
            vmem(2, 2, COMPS, n_a, n_o),
            vmem(2, n_a, n_o),
            vmem(2, n_a, n_o),
            vmem(2, n_a, n_o),
            vmem(2, n_a, n_o),
            vmem(2, chunks, 2, 1, LANES),
            vmem(2, chunks, 2, 2, 1, LANES),
            vmem(2, chunks, LANES, LANES),
            vmem(2, 2, 2, *flat),
            vmem(2, 2, 2, *flat),
            vmem(2, 2, 2, *thin),
            vmem(n_o // LANES, COMPS * (n_r // 2) * n_a, LANES),
            vmem(sources, 1, LANES),
            vmem(n_lat, 1, LANES),
            vmem(2, 1, LANES),
            vmem(max(7 * UNROLL * n_a, chunks * (UNROLL * FIELDS + 8)), 1, n_o),
            vmem(max(group, sources, n_lat), 1, LANES),
            dma((chunks + 2,)),
            dma((1,)),
            dma((2,)),
            dma((2,)),
            dma((2, 2)),
            dma((2, chunks)),
            dma((2, chunks, 2)),
            dma((2,)),
            dma((2, 2)),
            dma((2, 2)),
            dma((2, 2)),
            dma((2, 2, 2)),
            dma((2, 2)),
            dma((4,)),
            dma((4,)),
            pltpu.SemaphoreType.REGULAR((n_lat - 1 if direct else 1, 2)),
            dma((4 if direct else 6,)),
        ],
        compiler_params=pltpu.CompilerParams(
            collective_id=0, has_side_effects=True, vmem_limit_bytes=32 * 2**20
        ),
    )(*(
        pltpu.with_memory_space_constraint(x, pltpu.HBM)
        for x in (velocity, forcing, viscosity, plate_ids)
    ))
    new_v, coarse, plate = pl.pallas_call(
        write_out,
        out_shape=(
            jax.ShapeDtypeStruct(velocity.shape, f32),
            jax.ShapeDtypeStruct((COMPS, coarse_rows, n_o // 2), f32),
            jax.ShapeDtypeStruct((COMPS, n_a, n_o), f32),
        ),
        in_specs=[in_vmem] * 3,
        out_specs=(in_any,) * 3,
        scratch_shapes=[dma((3,))],
        compiler_params=pltpu.CompilerParams(vmem_limit_bytes=4 * 2**20),
    )(*(pltpu.with_memory_space_constraint(x, pltpu.VMEM) for x in held))
    coarse = coarse.reshape(COMPS, n_rad * (n_r // 2), n_a // 2, n_o // 2)
    return new_v, coarse, plate


def solution(mesh):
    sizes = tuple(mesh.shape[a] for a in ("lat", "lon", "rad"))
    field = P(None, "rad", "lat", "lon")
    return jax.shard_map(
        functools.partial(on_device, sizes),
        mesh=mesh,
        in_specs=(field, field, P("rad", "lat", "lon"), P("lat", "lon")),
        out_specs=(field, P(None, None, "lat", "lon"), P(None, "lat", "lon")),
        check_vma=False,
    )
```
